128 devices in a mesh: req: 16 (over y, z), seq: 2 (over core), exp: 4 (over x).
Axes of the slice: x: 4, y: 4, z: 4, core: 2. Of those that a mesh axis runs over, the one named last changes fastest.
Arguments:
- residual: bfloat16 [256, 7168], P(('req', 'seq', 'exp')), may hold values from -6 to 6
- queries: bfloat16 [16, 16, 128, 576], P('req', None, 'exp'), may hold values from -60 to 60
- latent_cache: bfloat16 [16, 384, 576], P('req', 'seq'), may hold values from -20 to 20
- blocks: int32 [16, 2, 2], P('req', 'seq'), may hold values from 0 to 2, as said below
- lengths: int32 [16], P('req'), may hold values from 208 to 384, as said below
- value_up: bfloat16 [128, 512, 128], P('exp'), may hold values from -0.25 to 0.25
- out_proj: bfloat16 [16384, 7168], P('exp', ('req', 'seq')), may hold values from -0.046875 to 0.046875
- norm_gain: bfloat16 [7168], replicated, may hold values from 0.099609375 to 1.8984375
- router: bfloat16 [7168, 16], replicated, may hold values from -0.0625 to 0.0625
- expert_ids: int32 [256, 8], P(('req', 'seq', 'exp')), may hold values from 0 to 15, all different within a row; in each aligned block of 2 rows (0 to 1, 2 to 3, ...) at most 2 rows name the same one
- w_gate: bfloat16 [16, 7168, 2048], P('req', None, ('seq', 'exp')), may hold values from -0.0625 to 0.0625
- w_up: bfloat16 [16, 7168, 2048], P('req', None, ('seq', 'exp')), may hold values from -0.0625 to 0.0625
- w_down: bfloat16 [16, 2048, 7168], P('req', ('seq', 'exp')), may hold values from -0.125 to 0.125
Outputs:
- layer_out: bfloat16 [256, 7168], P(('req', 'seq', 'exp'))
The draws below stay inside these ranges and needn't reach their ends.
Inputs may be any that keep to these rules, and one draw needn't show every extreme that they name: `blocks`: each request and shard lists 2 different block numbers of that shard. `lengths`: some request has exactly 384, some exactly 208. `expert_ids`: each row names 8 different experts; among the rows of one device (aligned blocks of 2 rows) no expert is named more than 2 times, a bound that some block reaches.
All inputs are finite; a program needn't handle non-finite values.
Results may differ from the reference program's by a relative error of at most 0.019.
Values may be sent and summed in bfloat16 or wider, within the bound.
No kernel may reach another device: no remote copies, remote signals or barrier semaphores. Data moves between devices by JAX's collectives and lax.ppermute only.
A program may use at most 128 MiB of HBM per device.

```python
import math
import jax
import jax.numpy as jnp
import numpy as np
from jax import lax

D = 7168
H = 128
DL = 512
DR = 64
DV = 128
FF = 2048
BLOCK = 64
SHARD_BLOCKS = 3
NSEL = 2
NT = 2
QT = 16
CAP = 2
REQUESTS = 16
TOKENS = 256
EXPERTS = 16
TOPK = 8
CTX_HALF = 192
CTX = 384
N_SEQ = 2
N_EXP = 4


def pick_blocks(key):
    scores = jax.random.randint(jax.random.fold_in(key, 22), (REQUESTS, N_SEQ, SHARD_BLOCKS), 0, 1 << 20)
    scores = scores * SHARD_BLOCKS + jnp.arange(SHARD_BLOCKS, dtype=jnp.int32)
    order = jnp.argsort(scores, axis=-1, stable=True)
    return order[..., :NSEL].astype(jnp.int32)


def cache_values(key):
    normal_part = jnp.clip(jax.random.normal(jax.random.fold_in(key, 11), (REQUESTS, CTX, DL + DR), jnp.float32), -4.0, 4.0)
    return normal_part


def draw_latent_cache(key, part):
    return cache_values(key).astype(jnp.bfloat16)


def draw_blocks(key, part):
    return pick_blocks(key)


def draw_lengths(key, part):
    drawn = jax.random.randint(jax.random.fold_in(key, 33), (REQUESTS,), CTX_HALF + QT, CTX + 1)
    return drawn.at[0].set(CTX).at[1].set(CTX_HALF + QT).astype(jnp.int32)


def draw_queries(key, part):
    normal_part = jnp.clip(jax.random.normal(jax.random.fold_in(key, 44), (REQUESTS, QT, H, DL + DR), jnp.float32), -4.0, 4.0)
    return normal_part.astype(jnp.bfloat16)


def block_levels(rng, dims, shards, least, largest):
    loudness = 1.0
    for dim, shards_of in shards:
        heights = jax.random.uniform(jax.random.fold_in(jax.random.fold_in(rng, 6), dim), (shards_of,), jnp.float32, least / len(shards), largest / len(shards))
        loudness = loudness * jnp.repeat(jnp.exp(heights), dims[dim] // shards_of).reshape((-1,) + (1,) * (len(dims) - 1 - dim))
    return loudness


def shared_out(rng, own, number, rows, amount, top, limit, skew):
    order = jax.random.permutation(rng, amount)
    heavy_load, usual = load_shares(amount, rows * top, limit, skew, True), load_shares(amount, rows * top, limit, skew, False)
    places = jnp.arange(amount)

    def named(tallies, turn):
        used = int((tallies > 0).sum())
        fixed = max(1, used // 4)
        moved = fixed + (places - fixed + turn * (used - fixed)) % max(1, amount - fixed)
        return jnp.zeros((amount,), jnp.int32).at[order[jnp.where(places < fixed, places, moved)]].set(jnp.asarray(tallies, jnp.int32))

    tallies = jnp.where(number % 4 == 0, named(heavy_load, number // 4), named(usual, number - number // 4 - 1))
    mixed = jax.random.permutation(jax.random.fold_in(own, 3), amount)
    source_of, sink = mixed[0:amount // 2 * 2:2], mixed[1:amount // 2 * 2:2]
    margin = jnp.minimum(tallies[source_of] - 1, limit - tallies[sink]) // 2
    margin = jnp.where((source_of == order[0]) | (sink == order[0]) | (tallies[sink] == 0), 0, jnp.maximum(margin, 0))
    moved = jax.random.randint(jax.random.fold_in(own, 4), (amount // 2,), 0, 1 << 20) % (margin + 1)
    tallies = tallies.at[source_of].add(-moved).at[sink].add(moved)
    items = jnp.searchsorted(jnp.cumsum(tallies), jnp.arange(rows * top), side="right").astype(jnp.int32)
    listing = items.reshape(top, rows).T
    listing = listing[jax.random.permutation(jax.random.fold_in(own, 1), rows)]
    turn = jax.random.randint(jax.random.fold_in(own, 2), (rows, 1), 0, top)
    return jnp.take_along_axis(listing, (jnp.arange(top)[None, :] + turn) % top, axis=1)


def load_shares(amount, total, bound, skew, full):
    portions = [(1 << 20) // math.isqrt(rank ** skew) + 1 for rank in range(1, amount + 1)]
    largest = bound if full else min(bound, max(-(-total // amount), total * portions[0] // sum(portions)))
    least = 1 if total - largest >= amount - 1 else 0
    counts, surplus = [largest] + [least] * (amount - 1), total - largest - least * (amount - 1)
    while surplus > 0:
        candidates = [i for i in range(1, amount) if counts[i] < largest] or [i for i in range(1, amount) if counts[i] < bound]
        whole, remaining = sum([portions[i] for i in candidates]), surplus
        for i in candidates:
            more = min(bound - counts[i], max(1, remaining * portions[i] // whole), surplus)
            counts[i] = counts[i] + more
            surplus = surplus - more
    return np.array(counts)


def bell_draw(stream_key, extent, spread, bound, cuts=(), held_as=jnp.bfloat16):
    factor_of = block_levels(stream_key, extent, cuts, -0.22, 0.18) if cuts else 1.0
    values = jax.random.normal(stream_key, extent, jnp.float32) * spread * factor_of
    return jnp.minimum(jnp.maximum(values, -bound), bound).astype(held_as)


def setup_inputs(seed: int = 0) -> dict:
    arg_keys = jax.random.split(jax.random.key(seed), 14)
    residual = bell_draw(arg_keys[0], (TOKENS, D), 1.0, 6.0, ((0, 128),))
    queries = draw_queries(jax.random.fold_in(arg_keys[13], 71), 0)
    latent_cache = draw_latent_cache(jax.random.fold_in(arg_keys[13], 71), 0)
    blocks = draw_blocks(jax.random.fold_in(arg_keys[13], 71), 0)
    lengths = draw_lengths(jax.random.fold_in(arg_keys[13], 71), 0)
    value_up = bell_draw(arg_keys[5], (H, DL, DV), DL ** -0.5, 0.25, ((0, 4),))
    out_proj = bell_draw(arg_keys[6], (H * DV, D), (H * DV) ** -0.5, 0.046875, ((0, 4), (1, 32)))
    norm_gain = jnp.clip(1.0 + 0.18 * jax.random.normal(arg_keys[7], (D,), jnp.float32), 0.099609375, 1.8984375).astype(jnp.bfloat16)
    router = bell_draw(arg_keys[8], (D, EXPERTS), D ** -0.5, 0.0625)
    expert_ids_keys = jax.random.split(jax.random.fold_in(arg_keys[9], 1), TOKENS // NT)
    expert_ids_turns = jax.random.permutation(jax.random.fold_in(arg_keys[9], 3), TOKENS // NT)
    expert_ids = jax.vmap(lambda own, number: shared_out(jax.random.fold_in(arg_keys[9], 2), own, number, NT, EXPERTS, TOPK, CAP, 2))(expert_ids_keys, expert_ids_turns).reshape((TOKENS, TOPK))
    w_gate = bell_draw(arg_keys[10], (EXPERTS, D, FF), D ** -0.5, 0.0625, ((0, 16), (2, 8)))
    w_up = bell_draw(arg_keys[11], (EXPERTS, D, FF), D ** -0.5, 0.0625, ((0, 16), (2, 8)))
    w_down = bell_draw(arg_keys[12], (EXPERTS, FF, D), FF ** -0.5, 0.125, ((0, 16), (1, 8)))
    return dict(residual=residual, queries=queries, latent_cache=latent_cache, blocks=blocks, lengths=lengths, value_up=value_up, out_proj=out_proj, norm_gain=norm_gain, router=router, expert_ids=expert_ids, w_gate=w_gate, w_up=w_up, w_down=w_down)


def pick_rows(block_rows, picks):
    return block_rows[picks]

def shard_partial(queries32, latent_cache, blocks, lengths, shard):
    region = latent_cache[:, shard * CTX_HALF:(shard + 1) * CTX_HALF]
    region = region.reshape(REQUESTS, SHARD_BLOCKS, BLOCK, DL + DR)
    picked = jax.vmap(pick_rows)(region, blocks[:, shard]).reshape(REQUESTS, NSEL * BLOCK, DL + DR)
    positions = shard * CTX_HALF + blocks[:, shard, :, None] * BLOCK + jnp.arange(BLOCK, dtype=jnp.int32)
    positions = positions.reshape(REQUESTS, NSEL * BLOCK)
    limits = lengths[:, None] - (QT - 1) + jnp.arange(QT, dtype=jnp.int32)[None, :]
    usable = positions[:, None, None, :] < limits[:, :, None, None]
    key_rows = picked.astype(jnp.float32)
    scores = jnp.einsum('bqhk,bjk->bqhj', queries32, key_rows) * (DV + DR) ** (-0.5)
    row_max = lax.optimization_barrier(jnp.max(jnp.where(usable, scores, -1e+30), axis=-1))
    weights = jnp.where(usable, jnp.exp(scores - row_max[..., None]), 0.0).astype(jnp.bfloat16).astype(jnp.float32)
    row_sum = lax.optimization_barrier(jnp.sum(weights, -1))
    weighted = jnp.einsum('bqhj,bjd->bqhd', weights, key_rows[..., :DL])
    return (row_max, row_sum, weighted)

def reference(residual, queries, latent_cache, blocks, lengths, value_up, out_proj, norm_gain, router, expert_ids, w_gate, w_up, w_down):
    queries32 = queries.astype(jnp.float32)
    pieces_list = [shard_partial(queries32, latent_cache, blocks, lengths, shard) for shard in range(N_SEQ)]
    overall = pieces_list[0][0]
    for entry in pieces_list[1:]:
        overall = jnp.maximum(overall, entry[0])
    totals = jnp.zeros_like(overall)
    numers = jnp.zeros(pieces_list[0][2].shape, jnp.float32)
    for entry in pieces_list:
        factor = jnp.exp(entry[0] - overall)
        totals = totals + factor * entry[1]
        numers = numers + factor[..., None] * entry[2]
    latent = (numers / totals[..., None]).astype(jnp.bfloat16)
    head_values = jnp.einsum('bqhd,hdv->bqhv', latent.astype(jnp.float32), value_up.astype(jnp.float32)).astype(jnp.bfloat16)
    attended = jnp.dot(head_values.reshape(TOKENS, H * DV), out_proj, preferred_element_type=jnp.float32).astype(jnp.bfloat16)
    hidden_sum = (residual.astype(jnp.float32) + attended.astype(jnp.float32)).astype(jnp.bfloat16)
    hidden32 = hidden_sum.astype(jnp.float32)
    normed = (hidden32 * lax.rsqrt(lax.optimization_barrier(jnp.mean(hidden32 * hidden32, -1, keepdims=True)) + 1e-06) * norm_gain.astype(jnp.float32)).astype(jnp.bfloat16)
    gate_probs = jax.nn.sigmoid(jnp.dot(normed, router, preferred_element_type=jnp.float32))
    chosen = jnp.take_along_axis(gate_probs, expert_ids, axis=1)
    gate_weights = chosen / lax.optimization_barrier(jnp.sum(chosen, -1, keepdims=True)) * 2.5
    groups = N_SEQ * N_EXP
    group_width = FF // groups

    def run_expert(weights_triple):
        gate_mat, up_mat, down_mat = weights_triple
        gate_act = jnp.dot(normed, gate_mat, preferred_element_type=jnp.float32)
        up_act = jnp.dot(normed, up_mat, preferred_element_type=jnp.float32)
        activated = (jax.nn.silu(gate_act) * up_act).astype(jnp.bfloat16)
        parts = jnp.einsum('bsf,sfd->bsd', activated.reshape(TOKENS, groups, group_width).astype(jnp.float32), down_mat.reshape(groups, group_width, D).astype(jnp.float32))
        parts = parts.astype(jnp.bfloat16).astype(jnp.float32)
        return lax.optimization_barrier(jnp.sum(parts, 1)).astype(jnp.bfloat16)
    expert_out = lax.map(run_expert, (w_gate, w_up, w_down))
    token_index = jnp.arange(TOKENS, dtype=jnp.int32)[:, None]
    selected = expert_out[expert_ids, token_index].astype(jnp.float32)
    routed = lax.optimization_barrier(jnp.sum(gate_weights[..., None] * selected, 1))
    return (hidden32 + routed).astype(jnp.bfloat16)
```

```python
import jax
import jax.numpy as jnp
from jax import lax
from jax.experimental import pallas as pl
from jax.experimental.pallas import tpu as pltpu
from jax.sharding import PartitionSpec as P

DL = 512
DR = 64
DV = 128
BLOCK = 64
F32 = jnp.float32
BF16 = jnp.bfloat16
SWAP = [(0, 1), (1, 0)]


def swap(x):
    return lax.ppermute(x, "seq", SWAP)


def shard_softmax(queries, picked, usable):
    scores = jnp.einsum("qhk,jk->qhj", queries, picked, preferred_element_type=F32) * (
        DV + DR
    ) ** (-0.5)
    row_max = jnp.max(jnp.where(usable, scores, -1e30), axis=-1)
    weights = jnp.where(usable, jnp.exp(scores - row_max[..., None]), 0.0).astype(BF16)
    row_sum = jnp.sum(weights.astype(F32), -1)
    weighted = jnp.einsum("qhj,jd->qhd", weights, picked[:, :DL], preferred_element_type=F32)
    return row_max, row_sum, weighted


def gate_up_kernel(idx, own, other, gain_own, gain_other, w_gate, w_up, router, act, acc_g, acc_u, acc_l, ssq):
    step = pl.program_id(0)
    width = gain_own.shape[-1]

    @pl.when(step == 0)
    def _():
        acc_g[...] = jnp.zeros_like(acc_g)
        acc_u[...] = jnp.zeros_like(acc_u)
        acc_l[...] = jnp.zeros_like(acc_l)
        ssq[...] = jnp.zeros_like(ssq)

    for rows, gain, side in ((own, gain_own, idx[0]), (other, gain_other, 1 - idx[0])):
        start = pl.multiple_of(side * width, 16)
        hidden = rows[0, :, :width].astype(F32)
        ssq[...] += jnp.sum(hidden * hidden, -1, keepdims=True)
        scaled = (hidden * gain[0].astype(F32)).astype(BF16)
        acc_g[...] += jnp.dot(scaled, w_gate[pl.ds(start, width), :], preferred_element_type=F32)
        acc_u[...] += jnp.dot(scaled, w_up[pl.ds(start, width), :], preferred_element_type=F32)
        acc_l[...] += jnp.dot(scaled, router[pl.ds(start, width), :], preferred_element_type=F32)

    @pl.when(step == pl.num_programs(0) - 1)
    def _():
        experts = router.shape[-1]
        columns = 2 * width * pl.num_programs(0)
        scale = lax.rsqrt(ssq[...] / columns + 1e-06)
        named = own[0, :, width : width + experts].astype(F32)
        chosen = named * jax.nn.sigmoid(acc_l[...] * scale)
        mine = lax.broadcasted_iota(jnp.int32, chosen.shape, 1) == idx[1]
        weight = jnp.sum(jnp.where(mine, chosen, 0.0), -1, keepdims=True)
        weight = weight / jnp.sum(chosen, -1, keepdims=True) * 2.5
        act[...] = (jax.nn.silu(acc_g[...] * scale) * (acc_u[...] * scale) * weight).astype(BF16)


def gate_up(idx, own, other, gain_own, gain_other, w_gate, w_up, router):
    steps, tokens, padded = own.shape
    width = gain_own.shape[-1]
    hidden = w_gate.shape[-1]
    experts = router.shape[-1]
    row_spec = pl.BlockSpec((1, tokens, padded), lambda i, idx: (i, 0, 0))
    gain_spec = pl.BlockSpec((1, 1, width), lambda i, idx: (i, 0, 0))
    return pl.pallas_call(
        gate_up_kernel,
        out_shape=jax.ShapeDtypeStruct((tokens, hidden), BF16),
        grid_spec=pltpu.PrefetchScalarGridSpec(
            num_scalar_prefetch=1,
            grid=(steps,),
            in_specs=[
                row_spec,
                row_spec,
                gain_spec,
                gain_spec,
                pl.BlockSpec((2 * width, hidden), lambda i, idx: (i, 0)),
                pl.BlockSpec((2 * width, hidden), lambda i, idx: (i, 0)),
                pl.BlockSpec((2 * width, experts), lambda i, idx: (i, 0)),
            ],
            out_specs=pl.BlockSpec((tokens, hidden), lambda i, idx: (0, 0)),
            scratch_shapes=[
                pltpu.VMEM((tokens, hidden), F32),
                pltpu.VMEM((tokens, hidden), F32),
                pltpu.VMEM((tokens, experts), F32),
                pltpu.VMEM((tokens, 1), F32),
            ],
        ),
        name="gate_up",
    )(idx, own, other, gain_own, gain_other, w_gate, w_up, router)


def down_first_kernel(idx, act, w_down, out):
    out[...] = jnp.dot(act[...], w_down[...], preferred_element_type=F32).astype(BF16)


def down_second_kernel(idx, act, w_down, arrived, out):
    total = jnp.dot(act[...], w_down[...], preferred_element_type=F32) + arrived[...].astype(F32)
    out[...] = total.reshape(out.shape).astype(BF16)


def down(idx, act, w_down, arrived):
    tokens, hidden = act.shape
    half = w_down.shape[1] // 2
    steps = 4
    block = half // steps
    side = (lambda idx: 1 - idx[0]) if arrived is None else (lambda idx: idx[0])
    in_specs = [
        pl.BlockSpec((tokens, hidden), lambda i, idx: (0, 0)),
        pl.BlockSpec((hidden, block), lambda i, idx: (0, side(idx) * steps + i)),
    ]
    operands = [idx, act, w_down]
    if arrived is None:
        kernel = down_first_kernel
        out_shape = jax.ShapeDtypeStruct((tokens, half), BF16)
        out_spec = pl.BlockSpec((tokens, block), lambda i, idx: (0, i))
    else:
        kernel = down_second_kernel
        operands.append(arrived)
        in_specs.append(pl.BlockSpec((tokens, block), lambda i, idx: (0, i)))
        out_shape = jax.ShapeDtypeStruct((tokens // 4, 4, half), BF16)
        out_spec = pl.BlockSpec((tokens // 4, 4, block), lambda i, idx: (0, 0, i))
    return pl.pallas_call(
        kernel,
        out_shape=out_shape,
        grid_spec=pltpu.PrefetchScalarGridSpec(
            num_scalar_prefetch=1, grid=(steps,), in_specs=in_specs, out_specs=out_spec
        ),
        name="down",
    )(*operands)


def per_device(
    residual,
    queries,
    latent_cache,
    blocks,
    lengths,
    value_up,
    out_proj,
    norm_gain,
    router,
    expert_ids,
    w_gate,
    w_up,
    w_down,
):
    drafts, heads, qk_width = queries.shape[1:]
    shard_len = latent_cache.shape[1]
    picks_count = blocks.shape[2]
    n_req, n_exp = lax.axis_size("req"), lax.axis_size("exp")
    s = lax.axis_index("seq")
    x = lax.axis_index("exp")
    r = lax.axis_index("req")
    model_width = residual.shape[1]
    experts = router.shape[1]
    width = out_proj.shape[1]
    padded = -(-width // 128) * 128
    own_rows = residual.shape[0]
    tokens = n_req * drafts

    block_view = latent_cache.reshape(shard_len // BLOCK, BLOCK, qk_width)
    picked = block_view[blocks[0, 0]].reshape(picks_count * BLOCK, qk_width)
    positions = s * shard_len + blocks[0, 0, :, None] * BLOCK + jnp.arange(BLOCK, dtype=jnp.int32)
    positions = positions.reshape(picks_count * BLOCK)
    limits = lengths[0] - (drafts - 1) + jnp.arange(drafts, dtype=jnp.int32)
    usable = positions[None, None, :] < limits[:, None, None]
    row_max, row_sum, weighted = shard_softmax(queries[0], picked, usable)
    half_heads = heads // 2

    def heads_of(a, side):
        a = a.reshape((drafts, 2, half_heads) + a.shape[2:])
        return lax.dynamic_index_in_dim(a, side, 1, False)

    sent = heads_of(weighted, 1 - s).astype(BF16)
    stats = jnp.stack([heads_of(row_max, 1 - s), heads_of(row_sum, 1 - s)])
    other_weighted, other_stats = swap(sent), swap(stats)
    max_own, sum_own, out_own = heads_of(row_max, s), heads_of(row_sum, s), heads_of(weighted, s)
    top = jnp.maximum(max_own, other_stats[0])
    scale_own, scale_other = jnp.exp(max_own - top), jnp.exp(other_stats[0] - top)
    total = scale_own * sum_own + scale_other * other_stats[1]
    latent = scale_own[..., None] * out_own + scale_other[..., None] * other_weighted.astype(F32)
    latent = (latent / total[..., None]).astype(BF16)
    value_half = lax.dynamic_slice_in_dim(value_up, s * half_heads, half_heads, 0)
    head_values = jnp.einsum("qhd,hdv->qhv", latent, value_half, preferred_element_type=F32)
    flat_values = head_values.astype(BF16).reshape(drafts, half_heads * DV)

    named = jnp.sum(
        (expert_ids[:, :, None] == jnp.arange(experts, dtype=jnp.int32)).astype(F32), 1
    ).astype(BF16)
    columns = residual.reshape(own_rows, n_req * 2, width)
    named = jnp.broadcast_to(named[:, None], (own_rows, n_req * 2, experts))
    spare = jnp.zeros((own_rows, n_req * 2, padded - width - experts), BF16)
    side_rows = jnp.concatenate([columns, named, spare], -1)
    side_rows = side_rows.reshape(own_rows, n_req, 2 * padded // 128, 128).transpose(1, 0, 2, 3)
    side_rows = side_rows.reshape(n_req, own_rows * 2 * padded // 128, 128)
    side_rows = jnp.pad(side_rows, ((0, 0), (0, drafts - side_rows.shape[1]), (0, 0)))
    fanned = jnp.concatenate(
        [jnp.broadcast_to(flat_values[None], (n_req,) + flat_values.shape), side_rows], -1
    )
    gathered = lax.all_to_all(fanned, "req", split_axis=0, concat_axis=0, tiled=True)
    gathered_other = swap(gathered)

    def values_of(a):
        return a[:, :, : half_heads * DV].reshape(tokens, half_heads * DV)

    def residual_of(a):
        a = a[:, : own_rows * 2 * padded // 128, half_heads * DV :]
        return a.reshape(n_req, own_rows, 2, padded)

    depth = half_heads * DV
    terms = jnp.dot(
        values_of(gathered),
        lax.dynamic_slice_in_dim(out_proj, s * depth, depth, 0),
        preferred_element_type=F32,
    )
    terms += jnp.dot(
        values_of(gathered_other),
        lax.dynamic_slice_in_dim(out_proj, (1 - s) * depth, depth, 0),
        preferred_element_type=F32,
    )
    terms = jnp.pad(terms.astype(BF16), ((0, 0), (0, padded - width)))
    new = jnp.arange(tokens, dtype=jnp.int32)
    group = 2 * own_rows
    new_exp, new_req = new // (n_req * group), new // group % n_req
    new_seq, new_row = new // own_rows % 2, new % own_rows
    old = ((new_req * 2 + new_seq) * n_exp + new_exp) * own_rows + new_row
    order = (old[:, None] == new[None, :]).astype(BF16)
    terms = jnp.dot(order, terms, preferred_element_type=F32).astype(BF16)
    terms = lax.all_to_all(
        terms.reshape(n_exp, tokens // n_exp, padded), "exp", split_axis=0, concat_axis=0, tiled=True
    )
    attended = jnp.sum(terms.astype(F32), 0).astype(BF16)
    mine, theirs = residual_of(gathered), residual_of(gathered_other)
    both = jnp.where(s == 0, jnp.stack([mine, theirs], 1), jnp.stack([theirs, mine], 1))
    both = lax.dynamic_index_in_dim(both, s, 3, False).reshape(tokens // n_exp, padded)
    hidden_sum = (both.astype(F32) + attended.astype(F32)).astype(BF16)

    fanned = jnp.broadcast_to(hidden_sum[None], (n_req * n_exp,) + hidden_sum.shape)
    own = lax.all_to_all(fanned, ("req", "exp"), split_axis=0, concat_axis=0, tiled=True)
    own = own.reshape(n_req, tokens, padded)
    other = swap(own)
    gains = norm_gain.reshape(n_req, 2, 1, width)
    gain_own = lax.dynamic_index_in_dim(gains, s, 1, False)
    gain_other = lax.dynamic_index_in_dim(gains, 1 - s, 1, False)
    idx = jnp.stack([s, r]).astype(jnp.int32)
    act = gate_up(idx, own, other, gain_own, gain_other, w_gate[0], w_up[0], router)
    arrived = swap(down(idx, act, w_down[0], None))
    pieces = down(idx, act, w_down[0], arrived)
    pieces = lax.all_to_all(pieces, ("exp", "req"), split_axis=0, concat_axis=0, tiled=True)
    routed = jnp.sum(pieces.astype(F32), 0)
    routed = routed.reshape(2, own_rows, model_width // 2)
    routed_mine = lax.dynamic_index_in_dim(routed, s, 0, False)
    routed_theirs = swap(lax.dynamic_index_in_dim(routed, 1 - s, 0, False))
    routed = jnp.where(
        s == 0,
        jnp.concatenate([routed_mine, routed_theirs], -1),
        jnp.concatenate([routed_theirs, routed_mine], -1),
    )
    place = ((x * n_req + r) * 2 + s) * own_rows
    hid_own = lax.dynamic_slice_in_dim(own, place, own_rows, 1)[:, :, :width]
    hid_other = lax.dynamic_slice_in_dim(other, place, own_rows, 1)[:, :, :width]
    hid = jnp.where(s == 0, jnp.stack([hid_own, hid_other], 1), jnp.stack([hid_other, hid_own], 1))
    hid = hid.transpose(2, 0, 1, 3).reshape(own_rows, model_width)
    return (hid.astype(F32) + routed).astype(BF16)


def solution(mesh):
    in_specs = (
        P(("req", "seq", "exp"), None),
        P("req", None, "exp", None),
        P("req", "seq", None),
        P("req", "seq", None),
        P("req"),
        P("exp", None, None),
        P("exp", ("req", "seq")),
        P(),
        P(),
        P(("req", "seq", "exp"), None),
        P("req", None, ("seq", "exp")),
        P("req", None, ("seq", "exp")),
        P("req", ("seq", "exp"), None),
    )
    out_specs = P(("req", "seq", "exp"), None)
    return jax.shard_map(
        per_device, mesh=mesh, in_specs=in_specs, out_specs=out_specs, check_vma=False
    )
```

```python
import jax
import jax.numpy as jnp
from jax import lax
from jax.experimental import pallas as pl
from jax.experimental.pallas import tpu as pltpu
from jax.sharding import PartitionSpec as P

DL = 512
DR = 64
DV = 128
BLOCK = 64
F32 = jnp.float32
BF16 = jnp.bfloat16
SWAP = [(0, 1), (1, 0)]


def swap(x):
    return lax.ppermute(x, "seq", SWAP)


def vmem():
    return pl.BlockSpec(memory_space=pltpu.VMEM)


def call(kernel, name, out_shape, idx, *operands, scratch=(), limit=24):
    many = isinstance(out_shape, (tuple, list))
    return pl.pallas_call(
        kernel,
        out_shape=out_shape,
        in_specs=[pl.BlockSpec(memory_space=pltpu.SMEM)] + [vmem() for _ in operands],
        out_specs=[vmem() for _ in out_shape] if many else vmem(),
        scratch_shapes=list(scratch),
        compiler_params=pltpu.CompilerParams(vmem_limit_bytes=limit * 2**20),
        name=name,
    )(idx, *operands)


def one_hot(shape, source):
    rows = lax.broadcasted_iota(jnp.int32, shape, 0)
    columns = lax.broadcasted_iota(jnp.int32, shape, 1)
    return jnp.where(source(rows) == columns, 1.0, 0.0).astype(BF16)


def parts_of(a):
    first = a.astype(BF16)
    rest = a - first.astype(F32)
    second = rest.astype(BF16)
    return first, second, (rest - second.astype(F32)).astype(BF16)


def attend_kernel(idx, queries, cache, sent, kept, kept_stats):
    drafts, heads, width = queries.shape
    side, length, first, second = idx[0], idx[2], idx[3], idx[4]
    shard_len = cache.shape[0]
    keys = jnp.concatenate(
        [
            cache[pl.ds(pl.multiple_of(first * BLOCK, BLOCK), BLOCK), :],
            cache[pl.ds(pl.multiple_of(second * BLOCK, BLOCK), BLOCK), :],
        ],
        0,
    )
    rows = queries[...].reshape(drafts * heads, width)
    scores = lax.dot_general(
        rows, keys, (((1,), (1,)), ((), ())), preferred_element_type=F32
    ) * ((DV + DR) ** (-0.5))
    row = lax.broadcasted_iota(jnp.int32, scores.shape, 0)
    col = lax.broadcasted_iota(jnp.int32, scores.shape, 1)
    block = jnp.where(col < BLOCK, first, second - 1)
    usable = side * shard_len + block * BLOCK + col < length - (drafts - 1) + row // heads
    top = jnp.max(jnp.where(usable, scores, -1e30), -1, keepdims=True)
    probs = jnp.where(usable, jnp.exp(scores - top), 0.0).astype(BF16)
    total = jnp.sum(probs.astype(F32), -1, keepdims=True)
    out = jnp.dot(probs, keys[:, :DL], preferred_element_type=F32)
    half = heads // 2

    def split(a):
        a = a.reshape(drafts, 2, half, a.shape[-1])
        low = a[:, 0].reshape(drafts * half, a.shape[-1])
        high = a[:, 1].reshape(drafts * half, a.shape[-1])
        return jnp.where(side == 0, low, high), jnp.where(side == 0, high, low)

    mine, theirs = split(out)
    stats = jnp.concatenate(
        [jnp.broadcast_to(top, (top.shape[0], 128)), jnp.broadcast_to(total, (top.shape[0], 128))],
        -1,
    )
    my_stats, their_stats = split(stats)
    kept[...] = mine
    kept_stats[...] = my_stats
    sent[:, :DL] = theirs.astype(BF16)
    top_parts, sum_parts = parts_of(their_stats[:, :128]), parts_of(their_stats[:, 128:])
    lane = lax.broadcasted_iota(jnp.int32, (drafts * half, 128), 1)
    packed = jnp.zeros((drafts * half, 128), F32)
    for place, part in enumerate(top_parts + sum_parts):
        packed = jnp.where(lane == place, part.astype(F32), packed)
    sent[:, DL:] = packed.astype(BF16)


def values_kernel(idx, kept, kept_stats, arrived, value_up, side_rows, fanned):
    rows = kept.shape[0]
    dests, slabs, drafts, _ = fanned.shape
    half = slabs - 1
    packed = arrived[:, DL:].astype(F32)
    lane = lax.broadcasted_iota(jnp.int32, packed.shape, 1)
    other_top = jnp.sum(jnp.where(lane < 3, packed, 0.0), -1, keepdims=True)
    other_sum = jnp.sum(jnp.where((lane >= 3) & (lane < 6), packed, 0.0), -1, keepdims=True)
    my_top, my_sum = kept_stats[:, 0:1], kept_stats[:, 128:129]
    top = jnp.maximum(my_top, other_top)
    my_scale, other_scale = jnp.exp(my_top - top), jnp.exp(other_top - top)
    total = my_scale * my_sum + other_scale * other_sum
    latent = (my_scale / total) * kept[...] + (other_scale / total) * arrived[:, :DL].astype(F32)
    latent = latent.astype(BF16)
    order = one_hot((rows, rows), lambda i: i % drafts * half + i // drafts)
    latent = jnp.dot(order, latent, preferred_element_type=F32).astype(BF16)
    for head in range(half):
        out = jnp.dot(
            latent[head * drafts : (head + 1) * drafts],
            value_up[idx[0] * half + head],
            preferred_element_type=F32,
        ).astype(BF16)
        for dest in range(dests):
            fanned[dest, head] = out
    for dest in range(dests):
        fanned[dest, half] = side_rows[dest]


def project_terms(gathered, out_proj_t, side):
    reqs, slabs, drafts, lanes = gathered.shape
    half = slabs - 1
    total = None
    for head in range(0, half, 2):
        pair = jnp.concatenate(
            [gathered[:, head].reshape(reqs * drafts, lanes), gathered[:, head + 1].reshape(reqs * drafts, lanes)],
            -1,
        )
        start = pl.multiple_of((side * half + head) * lanes, 256)
        term = lax.dot_general(
            pair,
            out_proj_t[:, pl.ds(start, 2 * lanes)],
            (((1,), (1,)), ((), ())),
            preferred_element_type=F32,
        )
        total = term if total is None else total + term
    return total


def project_own_kernel(idx, gathered, out_proj_t, out):
    out[...] = project_terms(gathered, out_proj_t, idx[0])


def project_both_kernel(idx, started, gathered, gathered_other, out_proj_t, terms, residual):
    reqs, slabs, drafts, lanes = gathered.shape
    exps, _, padded = terms.shape
    width = started.shape[1]
    side = idx[0]
    total = (started[...] + project_terms(gathered_other, out_proj_t, 1 - side)).astype(BF16)
    tokens = reqs * drafts
    own_rows = drafts // (2 * exps)

    def source(i):
        exp, req = i // (tokens // exps), i // (2 * own_rows) % reqs
        seq, row = i // own_rows % 2, i % own_rows
        return ((req * 2 + seq) * exps + exp) * own_rows + row

    total = jnp.dot(one_hot((tokens, tokens), source), total, preferred_element_type=F32)
    total = jnp.concatenate([total, jnp.zeros((tokens, padded - width), F32)], -1)
    terms[...] = total.astype(BF16).reshape(terms.shape)
    tiles = padded // lanes
    for tile in range(tiles):
        picked = jnp.zeros((tokens // exps, lanes), F32)
        for rows, from_side in ((gathered, side), (gathered_other, 1 - side)):

            def residual_source(i):
                req, seq, row = i // (2 * own_rows), i // own_rows % 2, i % own_rows
                place = req * drafts + (row * 2 + side) * tiles + tile
                return jnp.where(seq == from_side, place, -1)

            picked += jnp.dot(
                one_hot((tokens // exps, tokens), residual_source),
                rows[:, slabs - 1].reshape(tokens, lanes),
                preferred_element_type=F32,
            )
        residual[:, tile * lanes : (tile + 1) * lanes] = picked.astype(BF16)


def expert_terms(rows, gains, w_gate, w_up, router_t, side):
    steps, tokens, _ = rows.shape
    width = gains.shape[-1]

    def step(i, state):
        gate, up, logits, squares = state
        start = pl.multiple_of((i * 2 + side) * width, 32)
        hidden = rows[i][:, :width].astype(F32)
        scaled = (hidden * gains[i * 2 + side].astype(F32)).astype(BF16)
        gate += jnp.dot(scaled, w_gate[pl.ds(start, width), :], preferred_element_type=F32)
        up += jnp.dot(scaled, w_up[pl.ds(start, width), :], preferred_element_type=F32)
        logits += lax.dot_general(
            scaled, router_t[i * 2 + side], (((1,), (1,)), ((), ())), preferred_element_type=F32
        )
        return gate, up, logits, squares + hidden * hidden

    state = None
    for i in range(steps):
        if state is None:
            state = (
                jnp.zeros((tokens, w_gate.shape[1]), F32),
                jnp.zeros((tokens, w_up.shape[1]), F32),
                jnp.zeros((tokens, router_t.shape[1]), F32),
                jnp.zeros((tokens, width), F32),
            )
        state = step(i, state)
    gate, up, logits, squares = state
    return gate, up, logits, jnp.sum(squares, -1, keepdims=True)


def gate_up_own_kernel(idx, own, gains, w_gate, w_up, router_t, gate, up, logits, squares):
    a, b, c, d = expert_terms(own, gains, w_gate, w_up, router_t, idx[0])
    gate[...], up[...], logits[...] = a, b, c
    squares[...] = jnp.broadcast_to(d, squares.shape)


def gate_up_both_kernel(idx, gate, up, logits, squares, own, other, gains, w_gate, w_up, router_t, act):
    width = gains.shape[-1]
    experts = logits.shape[1]
    columns = gains.shape[0] * width
    a, b, c, d = expert_terms(other, gains, w_gate, w_up, router_t, 1 - idx[0])
    scale = lax.rsqrt((squares[:, 0:1] + d) / columns + 1e-06)
    named = own[0, :, width : width + experts].astype(F32)
    chosen = named * jax.nn.sigmoid((logits[...] + c) * scale)
    mine = lax.broadcasted_iota(jnp.int32, chosen.shape, 1) == idx[1]
    weight = jnp.sum(jnp.where(mine, chosen, 0.0), -1, keepdims=True)
    weight = weight / jnp.sum(chosen, -1, keepdims=True) * 2.5
    act[...] = (
        jax.nn.silu((gate[...] + a) * scale) * ((up[...] + b) * scale) * weight
    ).astype(BF16)


DOWN_STEPS = 7


def down_first_kernel(idx, act, w_down, out):
    block = out.shape[1] // DOWN_STEPS
    for i in range(DOWN_STEPS):
        start = pl.multiple_of(((1 - idx[0]) * DOWN_STEPS + i) * block, 128)
        out[:, i * block : (i + 1) * block] = jnp.dot(
            act[...], w_down[:, pl.ds(start, block)], preferred_element_type=F32
        ).astype(BF16)


def down_second_kernel(idx, act, w_down, arrived, out):
    block = arrived.shape[1] // DOWN_STEPS
    for i in range(DOWN_STEPS):
        start = pl.multiple_of((idx[0] * DOWN_STEPS + i) * block, 128)
        total = jnp.dot(act[...], w_down[:, pl.ds(start, block)], preferred_element_type=F32)
        total += arrived[:, i * block : (i + 1) * block].astype(F32)
        out[:, :, i * block : (i + 1) * block] = total.reshape(out.shape[:2] + (block,)).astype(BF16)


def per_device(
    residual,
    queries,
    latent_cache,
    blocks,
    lengths,
    value_up,
    out_proj,
    norm_gain,
    router,
    expert_ids,
    w_gate,
    w_up,
    w_down,
):
    drafts, heads, qk_width = queries.shape[1:]
    n_req, n_exp = lax.axis_size("req"), lax.axis_size("exp")
    s = lax.axis_index("seq")
    x = lax.axis_index("exp")
    r = lax.axis_index("req")
    model_width = residual.shape[1]
    experts = router.shape[1]
    width = out_proj.shape[1]
    padded = -(-width // 128) * 128
    own_rows = residual.shape[0]
    tokens = n_req * drafts
    half_heads = heads // 2
    shape = jax.ShapeDtypeStruct

    idx = jnp.concatenate([jnp.stack([s, r]).astype(jnp.int32), lengths, blocks.reshape(-1)])
    half_rows = drafts * half_heads
    sent, kept, kept_stats = call(
        attend_kernel,
        "attend",
        (
            shape((half_rows, DL + 128), BF16),
            shape((half_rows, DL), F32),
            shape((half_rows, 256), F32),
        ),
        idx,
        queries[0],
        latent_cache[0],
    )
    arrived = swap(sent)

    named = jnp.sum(
        (expert_ids[:, :, None] == jnp.arange(experts, dtype=jnp.int32)).astype(F32), 1
    ).astype(BF16)
    columns = residual.reshape(own_rows, n_req * 2, width)
    named = jnp.broadcast_to(named[:, None], (own_rows, n_req * 2, experts))
    spare = jnp.zeros((own_rows, n_req * 2, padded - width - experts), BF16)
    side_rows = jnp.concatenate([columns, named, spare], -1)
    side_rows = side_rows.reshape(own_rows, n_req, 2 * padded // 128, 128).transpose(1, 0, 2, 3)
    side_rows = side_rows.reshape(n_req, own_rows * 2 * padded // 128, 128)
    side_rows = jnp.pad(side_rows, ((0, 0), (0, drafts - side_rows.shape[1]), (0, 0)))
    fanned = call(
        values_kernel,
        "values",
        shape((n_req, half_heads + 1, drafts, DV), BF16),
        idx,
        kept,
        kept_stats,
        arrived,
        value_up,
        side_rows,
    )
    gathered = lax.all_to_all(fanned, "req", split_axis=0, concat_axis=0, tiled=True)
    gathered_other = swap(gathered)
    out_proj_t = out_proj.T
    started = call(
        project_own_kernel, "project_own", shape((tokens, width), F32), idx, gathered, out_proj_t
    )
    terms, resid = call(
        project_both_kernel,
        "project_both",
        (
            shape((n_exp, tokens // n_exp, padded), BF16),
            shape((tokens // n_exp, padded), BF16),
        ),
        idx,
        started,
        gathered,
        gathered_other,
        out_proj_t,
    )
    gains = norm_gain.reshape(n_req * 2, 1, width)
    router_t = router.T.reshape(experts, n_req * 2, width).transpose(1, 0, 2)
    terms, resid, idx, gains, router_t = lax.optimization_barrier(
        (terms, resid, idx, gains, router_t)
    )
    terms = lax.all_to_all(terms, "exp", split_axis=0, concat_axis=0, tiled=True)
    attended = jnp.sum(terms.astype(F32), 0).astype(BF16)
    hidden_sum = (resid.astype(F32) + attended.astype(F32)).astype(BF16)

    fanned = jnp.broadcast_to(hidden_sum[None], (n_req * n_exp,) + hidden_sum.shape)
    own = lax.all_to_all(fanned, ("req", "exp"), split_axis=0, concat_axis=0, tiled=True)
    own = own.reshape(n_req, tokens, padded)
    other = swap(own)
    w_gate, w_up, w_down = w_gate[0], w_up[0], w_down[0]
    hidden_units = w_gate.shape[1]
    started = call(
        gate_up_own_kernel,
        "gate_up_own",
        (
            shape((tokens, hidden_units), F32),
            shape((tokens, hidden_units), F32),
            shape((tokens, experts), F32),
            shape((tokens, 128), F32),
        ),
        idx,
        own,
        gains,
        w_gate,
        w_up,
        router_t,
    )
    act = call(
        gate_up_both_kernel,
        "gate_up_both",
        shape((tokens, hidden_units), BF16),
        idx,
        *started,
        own,
        other,
        gains,
        w_gate,
        w_up,
        router_t,
    )
    half = model_width // 2
    first = call(down_first_kernel, "down_first", shape((tokens, half), BF16), idx, act, w_down)
    pieces = call(
        down_second_kernel,
        "down_second",
        shape((tokens // 4, 4, half), BF16),
        idx,
        act,
        w_down,
        swap(first),
    )
    place = ((x * n_req + r) * 2 + s) * own_rows
    hid_own = lax.dynamic_slice_in_dim(own, place, own_rows, 1)[:, :, :width]
    hid_other = lax.dynamic_slice_in_dim(other, place, own_rows, 1)[:, :, :width]
    hid = jnp.where(s == 0, jnp.stack([hid_own, hid_other], 1), jnp.stack([hid_other, hid_own], 1))
    hid = hid.transpose(2, 0, 1, 3).reshape(own_rows, model_width)
    pieces = lax.all_to_all(pieces, ("exp", "req"), split_axis=0, concat_axis=0, tiled=True)
    routed = jnp.sum(pieces.astype(F32), 0)
    routed = routed.reshape(2, own_rows, half)
    routed_mine = lax.dynamic_index_in_dim(routed, s, 0, False)
    routed_theirs = swap(lax.dynamic_index_in_dim(routed, 1 - s, 0, False))
    routed = jnp.where(
        s == 0,
        jnp.concatenate([routed_mine, routed_theirs], -1),
        jnp.concatenate([routed_theirs, routed_mine], -1),
    )
    return (hid.astype(F32) + routed).astype(BF16)


def solution(mesh):
    in_specs = (
        P(("req", "seq", "exp"), None),
        P("req", None, "exp", None),
        P("req", "seq", None),
        P("req", "seq", None),
        P("req"),
        P("exp", None, None),
        P("exp", ("req", "seq")),
        P(),
        P(),
        P(("req", "seq", "exp"), None),
        P("req", None, ("seq", "exp")),
        P("req", None, ("seq", "exp")),
        P("req", ("seq", "exp"), None),
    )
    out_specs = P(("req", "seq", "exp"), None)
    return jax.shard_map(
        per_device, mesh=mesh, in_specs=in_specs, out_specs=out_specs, check_vma=False
    )
```

```python
import jax
import jax.numpy as jnp
from jax import lax
from jax.experimental import pallas as pl
from jax.experimental.pallas import tpu as pltpu
from jax.sharding import PartitionSpec as P

DL = 512
DR = 64
DV = 128
BLOCK = 64
F32 = jnp.float32
BF16 = jnp.bfloat16
SWAP = [(0, 1), (1, 0)]


def swap(x):
    return lax.ppermute(x, "seq", SWAP)


def vmem():
    return pl.BlockSpec(memory_space=pltpu.VMEM)


def call(kernel, name, out_shape, idx, *operands, outside=(), scratch=(), limit=24):
    many = isinstance(out_shape, (tuple, list))
    return pl.pallas_call(
        kernel,
        out_shape=out_shape,
        in_specs=[pl.BlockSpec(memory_space=pltpu.SMEM)]
        + [pl.BlockSpec(memory_space=pltpu.HBM) for _ in outside]
        + [vmem() for _ in operands],
        out_specs=[vmem() for _ in out_shape] if many else vmem(),
        scratch_shapes=list(scratch),
        compiler_params=pltpu.CompilerParams(vmem_limit_bytes=limit * 2**20),
        name=name,
    )(idx, *[pltpu.with_memory_space_constraint(a, pltpu.HBM) for a in outside], *operands)


def one_hot(shape, source):
    rows = lax.broadcasted_iota(jnp.int32, shape, 0)
    columns = lax.broadcasted_iota(jnp.int32, shape, 1)
    return jnp.where(source(rows) == columns, 1.0, 0.0).astype(BF16)


def parts_of(a):
    first = a.astype(BF16)
    rest = a - first.astype(F32)
    second = rest.astype(BF16)
    return first, second, (rest - second.astype(F32)).astype(BF16)


def attend_kernel(
    idx, queries, cache, value_up, sent, kept, kept_stats, value_half, query_rows, key_rows, sems
):
    drafts, heads, width = queries.shape
    side, length, first, second = idx[0], idx[2], idx[3], idx[4]
    shard_len = cache.shape[0]
    copies = [
        pltpu.make_async_copy(
            cache.at[pl.ds(pl.multiple_of(first * BLOCK, BLOCK), BLOCK), :],
            key_rows.at[pl.ds(0, BLOCK), :],
            sems.at[0],
        ),
        pltpu.make_async_copy(
            cache.at[pl.ds(pl.multiple_of(second * BLOCK, BLOCK), BLOCK), :],
            key_rows.at[pl.ds(BLOCK, BLOCK), :],
            sems.at[1],
        ),
        pltpu.make_async_copy(queries, query_rows, sems.at[2]),
    ]
    value_copy = pltpu.make_async_copy(
        value_up.at[pl.ds(side * (heads // 2), heads // 2)], value_half, sems.at[3]
    )
    for copy in copies:
        copy.start()
    value_copy.start()
    for copy in copies:
        copy.wait()
    keys = key_rows[...]
    rows = query_rows[...].reshape(drafts * heads, width)
    scores = lax.dot_general(
        rows, keys, (((1,), (1,)), ((), ())), preferred_element_type=F32
    ) * ((DV + DR) ** (-0.5))
    row = lax.broadcasted_iota(jnp.int32, scores.shape, 0)
    col = lax.broadcasted_iota(jnp.int32, scores.shape, 1)
    block = jnp.where(col < BLOCK, first, second - 1)
    usable = side * shard_len + block * BLOCK + col < length - (drafts - 1) + row // heads
    top = jnp.max(jnp.where(usable, scores, -1e30), -1, keepdims=True)
    probs = jnp.where(usable, jnp.exp(scores - top), 0.0).astype(BF16)
    total = jnp.sum(probs.astype(F32), -1, keepdims=True)
    out = jnp.dot(probs, keys[:, :DL], preferred_element_type=F32)
    half = heads // 2

    def split(a):
        a = a.reshape(drafts, 2, half, a.shape[-1])
        low = a[:, 0].reshape(drafts * half, a.shape[-1])
        high = a[:, 1].reshape(drafts * half, a.shape[-1])
        return jnp.where(side == 0, low, high), jnp.where(side == 0, high, low)

    mine, theirs = split(out)
    stats = jnp.concatenate(
        [jnp.broadcast_to(top, (top.shape[0], 128)), jnp.broadcast_to(total, (top.shape[0], 128))],
        -1,
    )
    my_stats, their_stats = split(stats)
    kept[...] = mine
    kept_stats[...] = my_stats
    sent[:, :DL] = theirs.astype(BF16)
    top_parts, sum_parts = parts_of(their_stats[:, :128]), parts_of(their_stats[:, 128:])
    lane = lax.broadcasted_iota(jnp.int32, (drafts * half, 128), 1)
    packed = jnp.zeros((drafts * half, 128), F32)
    for place, part in enumerate(top_parts + sum_parts):
        packed = jnp.where(lane == place, part.astype(F32), packed)
    sent[:, DL:] = packed.astype(BF16)
    value_copy.wait()


def values_kernel(idx, kept, kept_stats, arrived, value_up, side_rows, fanned):
    rows = kept.shape[0]
    dests, slabs, drafts, _ = fanned.shape
    half = slabs - 1
    packed = arrived[:, DL:].astype(F32)
    lane = lax.broadcasted_iota(jnp.int32, packed.shape, 1)
    other_top = jnp.sum(jnp.where(lane < 3, packed, 0.0), -1, keepdims=True)
    other_sum = jnp.sum(jnp.where((lane >= 3) & (lane < 6), packed, 0.0), -1, keepdims=True)
    my_top, my_sum = kept_stats[:, 0:1], kept_stats[:, 128:129]
    top = jnp.maximum(my_top, other_top)
    my_scale, other_scale = jnp.exp(my_top - top), jnp.exp(other_top - top)
    total = my_scale * my_sum + other_scale * other_sum
    latent = (my_scale / total) * kept[...] + (other_scale / total) * arrived[:, :DL].astype(F32)
    latent = latent.astype(BF16)
    order = one_hot((rows, rows), lambda i: i % drafts * half + i // drafts)
    latent = jnp.dot(order, latent, preferred_element_type=F32).astype(BF16)
    for head in range(half):
        out = jnp.dot(
            latent[head * drafts : (head + 1) * drafts],
            value_up[head],
            preferred_element_type=F32,
        ).astype(BF16)
        for dest in range(dests):
            fanned[dest, head] = out
    for dest in range(dests):
        fanned[dest, half] = side_rows[dest]


def project_terms(gathered, out_proj_t, side):
    reqs, slabs, drafts, lanes = gathered.shape
    half = slabs - 1
    total = None
    for head in range(0, half, 2):
        pair = jnp.concatenate(
            [gathered[:, head].reshape(reqs * drafts, lanes), gathered[:, head + 1].reshape(reqs * drafts, lanes)],
            -1,
        )
        start = pl.multiple_of((side * half + head) * lanes, 256)
        term = lax.dot_general(
            pair,
            out_proj_t[:, pl.ds(start, 2 * lanes)],
            (((1,), (1,)), ((), ())),
            preferred_element_type=F32,
        )
        total = term if total is None else total + term
    return total


def project_own_kernel(idx, gathered, out_proj_t, out):
    out[...] = project_terms(gathered, out_proj_t, idx[0])


def project_both_kernel(idx, started, gathered, gathered_other, out_proj_t, terms, residual):
    reqs, slabs, drafts, lanes = gathered.shape
    exps, _, padded = terms.shape
    width = started.shape[1]
    side = idx[0]
    total = (started[...] + project_terms(gathered_other, out_proj_t, 1 - side)).astype(BF16)
    tokens = reqs * drafts
    own_rows = drafts // (2 * exps)

    def source(i):
        exp, req = i // (tokens // exps), i // (2 * own_rows) % reqs
        seq, row = i // own_rows % 2, i % own_rows
        return ((req * 2 + seq) * exps + exp) * own_rows + row

    total = jnp.dot(one_hot((tokens, tokens), source), total, preferred_element_type=F32)
    total = jnp.concatenate([total, jnp.zeros((tokens, padded - width), F32)], -1)
    terms[...] = total.astype(BF16).reshape(terms.shape)
    tiles = padded // lanes
    for tile in range(tiles):
        picked = jnp.zeros((tokens // exps, lanes), F32)
        for rows, from_side in ((gathered, side), (gathered_other, 1 - side)):

            def residual_source(i):
                req, seq, row = i // (2 * own_rows), i // own_rows % 2, i % own_rows
                place = req * drafts + (row * 2 + side) * tiles + tile
                return jnp.where(seq == from_side, place, -1)

            picked += jnp.dot(
                one_hot((tokens // exps, tokens), residual_source),
                rows[:, slabs - 1].reshape(tokens, lanes),
                preferred_element_type=F32,
            )
        residual[:, tile * lanes : (tile + 1) * lanes] = picked.astype(BF16)


def expert_terms(rows, gains, w_gate, w_up, router_t, side, copies=()):
    steps, tokens, _ = rows.shape
    width = gains.shape[-1]

    def step(i, state):
        gate, up, logits, squares = state
        start = pl.multiple_of((i * 2 + side) * width, 32)
        hidden = rows[i][:, :width].astype(F32)
        scaled = (hidden * gains[i * 2 + side].astype(F32)).astype(BF16)
        gate += jnp.dot(scaled, w_gate[pl.ds(start, width), :], preferred_element_type=F32)
        up += jnp.dot(scaled, w_up[pl.ds(start, width), :], preferred_element_type=F32)
        logits += lax.dot_general(
            scaled, router_t[i * 2 + side], (((1,), (1,)), ((), ())), preferred_element_type=F32
        )
        return gate, up, logits, squares + hidden * hidden

    state = None
    for i in range(steps):
        if copies and i % (steps // len(copies)) == 0:
            copies[i * len(copies) // steps].wait()
        if state is None:
            state = (
                jnp.zeros((tokens, w_gate.shape[1]), F32),
                jnp.zeros((tokens, w_up.shape[1]), F32),
                jnp.zeros((tokens, router_t.shape[1]), F32),
                jnp.zeros((tokens, width), F32),
            )
        state = step(i, state)
    gate, up, logits, squares = state
    return gate, up, logits, jnp.sum(squares, -1, keepdims=True)


UP_COPIES = 4


def gate_up_own_kernel(
    idx, w_up_there, own, gains, w_gate, router_t, gate, up, logits, squares, w_up, sems
):
    rows = w_up.shape[0] // UP_COPIES
    copies = []
    for i in range(UP_COPIES):
        part = pl.ds(i * rows, rows)
        copies.append(pltpu.make_async_copy(w_up_there.at[part], w_up.at[part], sems.at[i]))
    for copy in copies:
        copy.start()
    a, b, c, d = expert_terms(own, gains, w_gate, w_up, router_t, idx[0], copies)
    gate[...], up[...], logits[...] = a, b, c
    squares[...] = jnp.broadcast_to(d, squares.shape)


def gate_up_both_kernel(
    idx, w_down_there, w_down_other_there, gate, up, logits, squares, own, other, gains, w_gate,
    w_up, router_t, act, w_down, w_down_other, sems,
):
    half = pl.ds(pl.multiple_of(idx[0] * w_down.shape[1], 128), w_down.shape[1])
    copies = [
        pltpu.make_async_copy(w_down_there.at[:, half], w_down, sems.at[0]),
        pltpu.make_async_copy(w_down_other_there.at[:, half], w_down_other, sems.at[1]),
    ]
    for copy in copies:
        copy.start()
    width = gains.shape[-1]
    experts = logits.shape[1]
    columns = gains.shape[0] * width
    a, b, c, d = expert_terms(other, gains, w_gate, w_up, router_t, 1 - idx[0])
    scale = lax.rsqrt((squares[:, 0:1] + d) / columns + 1e-06)
    named = own[0, :, width : width + experts].astype(F32)
    chosen = named * jax.nn.sigmoid((logits[...] + c) * scale)
    mine = lax.broadcasted_iota(jnp.int32, chosen.shape, 1) == idx[1]
    weight = jnp.sum(jnp.where(mine, chosen, 0.0), -1, keepdims=True)
    weight = weight / jnp.sum(chosen, -1, keepdims=True) * 2.5
    act[...] = (
        jax.nn.silu((gate[...] + a) * scale) * ((up[...] + b) * scale) * weight
    ).astype(BF16)
    for copy in copies:
        copy.wait()


DOWN_STEPS = 7


def down_kernel(idx, act, act_other, w_down, w_down_other, out):
    block = out.shape[2] // DOWN_STEPS
    for i in range(DOWN_STEPS):
        columns = pl.ds(i * block, block)
        total = jnp.dot(act[...], w_down[:, columns], preferred_element_type=F32)
        total += jnp.dot(act_other[...], w_down_other[:, columns], preferred_element_type=F32)
        out[:, :, i * block : (i + 1) * block] = total.reshape(out.shape[:2] + (block,)).astype(BF16)


def per_device(
    residual,
    queries,
    latent_cache,
    blocks,
    lengths,
    value_up,
    out_proj,
    norm_gain,
    router,
    expert_ids,
    w_gate,
    w_up,
    w_down,
):
    drafts, heads, qk_width = queries.shape[1:]
    n_req, n_exp = lax.axis_size("req"), lax.axis_size("exp")
    s = lax.axis_index("seq")
    x = lax.axis_index("exp")
    r = lax.axis_index("req")
    model_width = residual.shape[1]
    experts = router.shape[1]
    width = out_proj.shape[1]
    padded = -(-width // 128) * 128
    own_rows = residual.shape[0]
    tokens = n_req * drafts
    half_heads = heads // 2
    shape = jax.ShapeDtypeStruct

    place = ((x * n_req + r) * 2 + s) * own_rows
    idx = jnp.concatenate(
        [jnp.stack([s, r]).astype(jnp.int32), lengths, blocks.reshape(-1), place[None]]
    )
    half_rows = drafts * half_heads
    sent, kept, kept_stats, value_half = call(
        attend_kernel,
        "attend",
        (
            shape((half_rows, DL + 128), BF16),
            shape((half_rows, DL), F32),
            shape((half_rows, 256), F32),
            shape((half_heads,) + value_up.shape[1:], BF16),
        ),
        idx,
        outside=(queries[0], latent_cache[0], value_up),
        scratch=(
            pltpu.VMEM(queries.shape[1:], BF16),
            pltpu.VMEM((blocks.shape[2] * BLOCK, qk_width), BF16),
            pltpu.SemaphoreType.DMA((4,)),
        ),
    )
    arrived = swap(sent)
    w_down_other = swap(w_down[0])

    named = jnp.sum(
        (expert_ids[:, :, None] == jnp.arange(experts, dtype=jnp.int32)).astype(F32), 1
    ).astype(BF16)
    columns = residual.reshape(own_rows, n_req * 2, width)
    named = jnp.broadcast_to(named[:, None], (own_rows, n_req * 2, experts))
    spare = jnp.zeros((own_rows, n_req * 2, padded - width - experts), BF16)
    side_rows = jnp.concatenate([columns, named, spare], -1)
    side_rows = side_rows.reshape(own_rows, n_req, 2 * padded // 128, 128).transpose(1, 0, 2, 3)
    side_rows = side_rows.reshape(n_req, own_rows * 2 * padded // 128, 128)
    side_rows = jnp.pad(side_rows, ((0, 0), (0, drafts - side_rows.shape[1]), (0, 0)))
    fanned = call(
        values_kernel,
        "values",
        shape((n_req, half_heads + 1, drafts, DV), BF16),
        idx,
        kept,
        kept_stats,
        arrived,
        value_half,
        side_rows,
    )
    gathered = lax.all_to_all(fanned, "req", split_axis=0, concat_axis=0, tiled=True)
    gathered_other = swap(gathered)
    out_proj_t = out_proj.T
    w_gate, w_up, w_down = w_gate[0], w_up[0], w_down[0]
    started = call(
        project_own_kernel, "project_own", shape((tokens, width), F32), idx, gathered, out_proj_t
    )
    terms, resid = call(
        project_both_kernel,
        "project_both",
        (
            shape((n_exp, tokens // n_exp, padded), BF16),
            shape((tokens // n_exp, padded), BF16),
        ),
        idx,
        started,
        gathered,
        gathered_other,
        out_proj_t,
    )
    gains = norm_gain.reshape(n_req * 2, 1, width)
    router_t = router.T.reshape(experts, n_req * 2, width).transpose(1, 0, 2)
    terms, resid, idx, gains, router_t, w_down_other = lax.optimization_barrier(
        (terms, resid, idx, gains, router_t, w_down_other)
    )
    terms = lax.all_to_all(terms, "exp", split_axis=0, concat_axis=0, tiled=True)
    attended = jnp.sum(terms.astype(F32), 0).astype(BF16)
    hidden_sum = (resid.astype(F32) + attended.astype(F32)).astype(BF16)

    fanned = jnp.broadcast_to(hidden_sum[None], (n_req * n_exp,) + hidden_sum.shape)
    own = lax.all_to_all(fanned, ("req", "exp"), split_axis=0, concat_axis=0, tiled=True)
    own = own.reshape(n_req, tokens, padded)
    other = swap(own)
    hidden_units = w_gate.shape[1]
    *started, w_up = call(
        gate_up_own_kernel,
        "gate_up_own",
        (
            shape((tokens, hidden_units), F32),
            shape((tokens, hidden_units), F32),
            shape((tokens, experts), F32),
            shape((tokens, 128), F32),
            shape(w_up.shape, BF16),
        ),
        idx,
        own,
        gains,
        w_gate,
        router_t,
        outside=(w_up,),
        scratch=(pltpu.SemaphoreType.DMA((UP_COPIES,)),),
    )
    half = model_width // 2
    act, w_down, w_down_other = call(
        gate_up_both_kernel,
        "gate_up_both",
        (
            shape((tokens, hidden_units), BF16),
            shape((hidden_units, half), BF16),
            shape((hidden_units, half), BF16),
        ),
        idx,
        *started,
        own,
        other,
        gains,
        w_gate,
        w_up,
        router_t,
        outside=(w_down, w_down_other),
        scratch=(pltpu.SemaphoreType.DMA((2,)),),
    )
    pieces = call(
        down_kernel,
        "down",
        shape((tokens // 4, 4, half), BF16),
        idx,
        act,
        swap(act),
        w_down,
        w_down_other,
    )
    pieces, own, other, idx = lax.optimization_barrier((pieces, own, other, idx))
    s, place = idx[0], idx[-1]
    hid_own = lax.dynamic_slice_in_dim(own, place, own_rows, 1)[:, :, :width]
    hid_other = lax.dynamic_slice_in_dim(other, place, own_rows, 1)[:, :, :width]
    hid = jnp.where(s == 0, jnp.stack([hid_own, hid_other], 1), jnp.stack([hid_other, hid_own], 1))
    hid = hid.transpose(2, 0, 1, 3).reshape(own_rows, model_width)
    pieces = lax.all_to_all(pieces, ("exp", "req"), split_axis=0, concat_axis=0, tiled=True)
    routed = jnp.sum(pieces.astype(F32), 0)
    routed = routed.reshape(2, own_rows, half)
    routed_mine = lax.dynamic_index_in_dim(routed, s, 0, False)
    routed_theirs = swap(lax.dynamic_index_in_dim(routed, 1 - s, 0, False))
    routed = jnp.where(
        s == 0,
        jnp.concatenate([routed_mine, routed_theirs], -1),
        jnp.concatenate([routed_theirs, routed_mine], -1),
    )
    return (hid.astype(F32) + routed).astype(BF16)


def solution(mesh):
    in_specs = (
        P(("req", "seq", "exp"), None),
        P("req", None, "exp", None),
        P("req", "seq", None),
        P("req", "seq", None),
        P("req"),
        P("exp", None, None),
        P("exp", ("req", "seq")),
        P(),
        P(),
        P(("req", "seq", "exp"), None),
        P("req", None, ("seq", "exp")),
        P("req", None, ("seq", "exp")),
        P("req", ("seq", "exp"), None),
    )
    out_specs = P(("req", "seq", "exp"), None)
    return jax.shard_map(
        per_device, mesh=mesh, in_specs=in_specs, out_specs=out_specs, check_vma=False
    )
```

```python
import jax
import jax.numpy as jnp
from jax import lax
from jax.experimental import pallas as pl
from jax.experimental.pallas import tpu as pltpu
from jax.sharding import PartitionSpec as P

DL = 512
DR = 64
DV = 128
BLOCK = 64
F32 = jnp.float32
BF16 = jnp.bfloat16
SWAP = [(0, 1), (1, 0)]


def swap(x):
    return lax.ppermute(x, "seq", SWAP)


def vmem():
    return pl.BlockSpec(memory_space=pltpu.VMEM)


def call(kernel, name, out_shape, idx, *operands, outside=(), scratch=(), limit=24):
    many = isinstance(out_shape, (tuple, list))
    return pl.pallas_call(
        kernel,
        out_shape=out_shape,
        in_specs=[pl.BlockSpec(memory_space=pltpu.SMEM)]
        + [pl.BlockSpec(memory_space=pltpu.HBM) for _ in outside]
        + [vmem() for _ in operands],
        out_specs=[vmem() for _ in out_shape] if many else vmem(),
        scratch_shapes=list(scratch),
        compiler_params=pltpu.CompilerParams(vmem_limit_bytes=limit * 2**20),
        name=name,
    )(idx, *[pltpu.with_memory_space_constraint(a, pltpu.HBM) for a in outside], *operands)


def one_hot(shape, source):
    rows = lax.broadcasted_iota(jnp.int32, shape, 0)
    columns = lax.broadcasted_iota(jnp.int32, shape, 1)
    return jnp.where(source(rows) == columns, 1.0, 0.0).astype(BF16)


def parts_of(a):
    first = a.astype(BF16)
    rest = a - first.astype(F32)
    second = rest.astype(BF16)
    return first, second, (rest - second.astype(F32)).astype(BF16)


def attend_kernel(
    idx, queries, cache, value_up, sent, kept, kept_stats, value_half, query_rows, key_rows, sems
):
    drafts, heads, width = queries.shape
    side, length, first, second = idx[0], idx[2], idx[3], idx[4]
    shard_len = cache.shape[0]
    copies = [
        pltpu.make_async_copy(
            cache.at[pl.ds(pl.multiple_of(first * BLOCK, BLOCK), BLOCK), :],
            key_rows.at[pl.ds(0, BLOCK), :],
            sems.at[0],
        ),
        pltpu.make_async_copy(
            cache.at[pl.ds(pl.multiple_of(second * BLOCK, BLOCK), BLOCK), :],
            key_rows.at[pl.ds(BLOCK, BLOCK), :],
            sems.at[1],
        ),
        pltpu.make_async_copy(queries, query_rows, sems.at[2]),
    ]
    quarter = heads // 8
    value_copies = [
        pltpu.make_async_copy(
            value_up.at[pl.ds(side * (heads // 2) + i * quarter, quarter)],
            value_half.at[pl.ds(i * quarter, quarter)],
            sems.at[3 + i],
        )
        for i in range(4)
    ]
    for place, copy in enumerate(copies):
        copy.start(priority=place // 2)
    for place, copy in enumerate(value_copies):
        copy.start(priority=place % 2)
    for copy in copies:
        copy.wait()
    keys = key_rows[...]
    rows = query_rows[...].reshape(drafts * heads, width)
    scores = lax.dot_general(
        rows, keys, (((1,), (1,)), ((), ())), preferred_element_type=F32
    ) * ((DV + DR) ** (-0.5))
    row = lax.broadcasted_iota(jnp.int32, scores.shape, 0)
    col = lax.broadcasted_iota(jnp.int32, scores.shape, 1)
    block = jnp.where(col < BLOCK, first, second - 1)
    usable = side * shard_len + block * BLOCK + col < length - (drafts - 1) + row // heads
    top = jnp.max(jnp.where(usable, scores, -1e30), -1, keepdims=True)
    probs = jnp.where(usable, jnp.exp(scores - top), 0.0).astype(BF16)
    total = jnp.sum(probs.astype(F32), -1, keepdims=True)
    out = jnp.dot(probs, keys[:, :DL], preferred_element_type=F32)
    half = heads // 2

    def split(a):
        a = a.reshape(drafts, 2, half, a.shape[-1])
        low = a[:, 0].reshape(drafts * half, a.shape[-1])
        high = a[:, 1].reshape(drafts * half, a.shape[-1])
        return jnp.where(side == 0, low, high), jnp.where(side == 0, high, low)

    mine, theirs = split(out)
    stats = jnp.concatenate(
        [jnp.broadcast_to(top, (top.shape[0], 128)), jnp.broadcast_to(total, (top.shape[0], 128))],
        -1,
    )
    my_stats, their_stats = split(stats)
    kept[...] = mine
    kept_stats[...] = my_stats
    sent[:, :DL] = theirs.astype(BF16)
    top_parts, sum_parts = parts_of(their_stats[:, :128]), parts_of(their_stats[:, 128:])
    lane = lax.broadcasted_iota(jnp.int32, (drafts * half, 128), 1)
    packed = jnp.zeros((drafts * half, 128), F32)
    for place, part in enumerate(top_parts + sum_parts):
        packed = jnp.where(lane == place, part.astype(F32), packed)
    sent[:, DL:] = packed.astype(BF16)
    for copy in value_copies:
        copy.wait()


def values_kernel(idx, kept, kept_stats, arrived, value_up, side_rows, gains, router_t, fanned):
    rows = kept.shape[0]
    dests, slabs, drafts, _ = fanned.shape
    half = slabs - 1
    packed = arrived[:, DL:].astype(F32)
    lane = lax.broadcasted_iota(jnp.int32, packed.shape, 1)
    other_top = jnp.sum(jnp.where(lane < 3, packed, 0.0), -1, keepdims=True)
    other_sum = jnp.sum(jnp.where((lane >= 3) & (lane < 6), packed, 0.0), -1, keepdims=True)
    my_top, my_sum = kept_stats[:, 0:1], kept_stats[:, 128:129]
    top = jnp.maximum(my_top, other_top)
    my_scale, other_scale = jnp.exp(my_top - top), jnp.exp(other_top - top)
    total = my_scale * my_sum + other_scale * other_sum
    latent = (my_scale / total) * kept[...] + (other_scale / total) * arrived[:, :DL].astype(F32)
    latent = latent.astype(BF16)
    order = one_hot((rows, rows), lambda i: i % drafts * half + i // drafts)
    latent = jnp.dot(order, latent, preferred_element_type=F32).astype(BF16)
    for head in range(half):
        out = jnp.dot(
            latent[head * drafts : (head + 1) * drafts],
            value_up[head],
            preferred_element_type=F32,
        ).astype(BF16)
        for dest in range(dests):
            fanned[dest, head] = out
    for dest in range(dests):
        fanned[dest, half] = side_rows[dest]


def project_terms(gathered, out_proj_t, side):
    reqs, slabs, drafts, lanes = gathered.shape
    half = slabs - 1
    total = None
    for head in range(0, half, 2):
        pair = jnp.concatenate(
            [gathered[:, head].reshape(reqs * drafts, lanes), gathered[:, head + 1].reshape(reqs * drafts, lanes)],
            -1,
        )
        start = pl.multiple_of((side * half + head) * lanes, 256)
        term = lax.dot_general(
            pair,
            out_proj_t[:, pl.ds(start, 2 * lanes)],
            (((1,), (1,)), ((), ())),
            preferred_element_type=F32,
        )
        total = term if total is None else total + term
    return total


def project_kernel(idx, other_there, gathered, own_t, out, other_t, sem):
    reqs, slabs, drafts, lanes = gathered.shape
    _, exps, _, padded = out.shape
    width = own_t.shape[0]
    side, exp = idx[0], idx[6]
    tokens = reqs * drafts
    own_rows = drafts // (2 * exps)

    def parts(i):
        exp, req = i // (tokens // exps), i // (2 * own_rows) % reqs
        return exp, req, i // own_rows % 2, i % own_rows

    def source(i):
        exp, req, seq, row = parts(i)
        return ((req * 2 + seq) * exps + exp) * own_rows + row

    depth = other_t.shape[1]
    copy = pltpu.make_async_copy(
        other_there.at[:, pl.ds(pl.multiple_of(side * depth, depth), depth)], other_t, sem
    )
    copy.start()
    order = one_hot((tokens, tokens), source)
    beside = gathered[:, slabs - 1].reshape(tokens, lanes)
    tiles = padded // lanes
    for columns_t, column_side in ((own_t, side), (other_t, 1 - side)):
        if columns_t is other_t:
            copy.wait()
        terms = project_terms(gathered, columns_t, side if columns_t is own_t else 0).astype(BF16)
        terms = jnp.dot(order, terms, preferred_element_type=F32)
        terms = jnp.concatenate([terms, jnp.zeros((tokens, padded - width), F32)], -1)
        residual = []
        for tile in range(tiles):

            def residual_source(i):
                token_exp, req, seq, row = parts(i)
                place = req * drafts + (row * 2 + column_side) * tiles + tile
                return jnp.where((token_exp == exp) & (seq == side), place, -1)

            residual.append(
                jnp.dot(
                    one_hot((tokens, tokens), residual_source), beside, preferred_element_type=F32
                )
            )
        terms = (terms + jnp.concatenate(residual, -1)).astype(BF16)
        out[column_side] = terms.reshape(out.shape[1:])


def hidden_kernel(idx, terms, fanned):
    hidden = jnp.sum(terms[...].astype(F32), 0).astype(BF16)
    for dest in range(fanned.shape[0]):
        fanned[dest] = hidden


def expert_terms(rows, gains, w_gate, w_up, router_t, side):
    steps, tokens, _ = rows.shape
    width = gains.shape[-1]

    def step(i, state):
        gate, up, logits, squares = state
        start = pl.multiple_of((i * 2 + side) * width, 32)
        hidden = rows[i][:, :width].astype(F32)
        scaled = (hidden * gains[i * 2 + side].astype(F32)).astype(BF16)
        gate += jnp.dot(scaled, w_gate[pl.ds(start, width), :], preferred_element_type=F32)
        up += jnp.dot(scaled, w_up[pl.ds(start, width), :], preferred_element_type=F32)
        logits += lax.dot_general(
            scaled, router_t[i * 2 + side], (((1,), (1,)), ((), ())), preferred_element_type=F32
        )
        return gate, up, logits, squares + hidden * hidden

    state = None
    for i in range(steps):
        if state is None:
            state = (
                jnp.zeros((tokens, w_gate.shape[1]), F32),
                jnp.zeros((tokens, w_up.shape[1]), F32),
                jnp.zeros((tokens, router_t.shape[1]), F32),
                jnp.zeros((tokens, width), F32),
            )
        state = step(i, state)
    gate, up, logits, squares = state
    return gate, up, logits, jnp.sum(squares, -1, keepdims=True)


def gate_up_own_kernel(idx, own, gains, w_gate, w_up, router_t, gate, up, logits, squares):
    a, b, c, d = expert_terms(own, gains, w_gate, w_up, router_t, idx[0])
    gate[...], up[...], logits[...] = a, b, c
    squares[...] = jnp.broadcast_to(d, squares.shape)


def gate_up_both_kernel(
    idx, w_down_there, gate, up, logits, squares, own, other, gains, w_gate, w_up, router_t,
    act, rows_here, w_down_other, sems,
):
    hidden_units, half = w_down_other.shape
    columns = pl.ds(pl.multiple_of(idx[0] * half, 128), half)
    copies = []
    for i in range(2):
        part = pl.ds(i * (hidden_units // 2), hidden_units // 2)
        copies.append(
            pltpu.make_async_copy(
                w_down_there.at[part, columns], w_down_other.at[part], sems.at[i]
            )
        )
        copies[i].start(priority=i)
    pick = one_hot((rows_here.shape[1], own.shape[1]), lambda i: jnp.where(i < idx[7], idx[5] + i, -1))
    for rows, side in ((own, idx[0]), (other, 1 - idx[0])):
        for i in range(own.shape[0]):
            rows_here[i * 2 + side] = jnp.dot(pick, rows[i], preferred_element_type=F32)
    width = gains.shape[-1]
    experts = logits.shape[1]
    columns = gains.shape[0] * width
    a, b, c, d = expert_terms(other, gains, w_gate, w_up, router_t, 1 - idx[0])
    scale = lax.rsqrt((squares[:, 0:1] + d) / columns + 1e-06)
    named = own[0, :, width : width + experts].astype(F32)
    chosen = named * jax.nn.sigmoid((logits[...] + c) * scale)
    mine = lax.broadcasted_iota(jnp.int32, chosen.shape, 1) == idx[1]
    weight = jnp.sum(jnp.where(mine, chosen, 0.0), -1, keepdims=True)
    weight = weight / jnp.sum(chosen, -1, keepdims=True) * 2.5
    act[...] = (
        jax.nn.silu((gate[...] + a) * scale) * ((up[...] + b) * scale) * weight
    ).astype(BF16)
    for copy in copies:
        copy.wait()


DOWN_STEPS = 7


def down_kernel(idx, act, act_other, w_down, w_down_other, out):
    half = out.shape[2]
    block = half // DOWN_STEPS
    for i in range(DOWN_STEPS):
        columns = pl.ds(pl.multiple_of(idx[0] * half + i * block, 128), block)
        total = jnp.dot(act[...], w_down[:, columns], preferred_element_type=F32)
        total += jnp.dot(
            act_other[...], w_down_other[:, i * block : (i + 1) * block], preferred_element_type=F32
        )
        out[:, :, i * block : (i + 1) * block] = total.reshape(out.shape[:2] + (block,)).astype(BF16)


def routed_kernel(idx, pieces, mine, theirs):
    rows = mine.shape[0]
    total = jnp.sum(pieces[...].astype(F32), 0)
    low, high = total[:rows], total[rows:]
    mine[...] = jnp.where(idx[0] == 0, low, high)
    theirs[...] = jnp.where(idx[0] == 0, high, low)


def finish_kernel(idx, mine, theirs, rows_here, out):
    blocks, rows, half = rows_here.shape[0], mine.shape[0], mine.shape[1]
    width = 2 * half // blocks
    for side, first, second in ((0, mine, theirs), (1, theirs, mine)):

        @pl.when(idx[0] == side)
        def _():
            for block in range(blocks):
                start = block * width
                source, offset = (first, start) if start < half else (second, start - half)
                total = rows_here[block, :rows, :width] + source[:, offset : offset + width]
                out[:, start : start + width] = total.astype(BF16)


def per_device(
    residual,
    queries,
    latent_cache,
    blocks,
    lengths,
    value_up,
    out_proj,
    norm_gain,
    router,
    expert_ids,
    w_gate,
    w_up,
    w_down,
):
    drafts, heads, qk_width = queries.shape[1:]
    n_req, n_exp = lax.axis_size("req"), lax.axis_size("exp")
    s = lax.axis_index("seq")
    x = lax.axis_index("exp")
    r = lax.axis_index("req")
    model_width = residual.shape[1]
    experts = router.shape[1]
    width = out_proj.shape[1]
    padded = -(-width // 128) * 128
    own_rows = residual.shape[0]
    tokens = n_req * drafts
    half_heads = heads // 2
    shape = jax.ShapeDtypeStruct

    place = ((x * n_req + r) * 2 + s) * own_rows
    idx = jnp.concatenate(
        [
            jnp.stack([s, r]).astype(jnp.int32),
            lengths,
            blocks.reshape(-1),
            jnp.stack([place, x, jnp.int32(own_rows)]).astype(jnp.int32),
        ]
    )
    half_rows = drafts * half_heads
    sent, kept, kept_stats, value_half = call(
        attend_kernel,
        "attend",
        (
            shape((half_rows, DL + 128), BF16),
            shape((half_rows, DL), F32),
            shape((half_rows, 256), F32),
            shape((half_heads,) + value_up.shape[1:], BF16),
        ),
        idx,
        outside=(queries[0], latent_cache[0], value_up),
        scratch=(
            pltpu.VMEM(queries.shape[1:], BF16),
            pltpu.VMEM((blocks.shape[2] * BLOCK, qk_width), BF16),
            pltpu.SemaphoreType.DMA((7,)),
        ),
    )
    arrived = swap(sent)
    w_gate, w_up, w_down = w_gate[0], w_up[0], w_down[0]
    out_proj_t = out_proj.T
    other_t = swap(out_proj_t)
    w_down_other = swap(w_down)

    gains = norm_gain.reshape(n_req * 2, 1, width)
    router_t = router.T.reshape(experts, n_req * 2, width).transpose(1, 0, 2)
    named = jnp.sum(
        (expert_ids[:, :, None] == jnp.arange(experts, dtype=jnp.int32)).astype(F32), 1
    ).astype(BF16)
    columns = residual.reshape(own_rows, n_req * 2, width)
    named = jnp.broadcast_to(named[:, None], (own_rows, n_req * 2, experts))
    spare = jnp.zeros((own_rows, n_req * 2, padded - width - experts), BF16)
    side_rows = jnp.concatenate([columns, named, spare], -1)
    side_rows = side_rows.reshape(own_rows, n_req, 2 * padded // 128, 128).transpose(1, 0, 2, 3)
    side_rows = side_rows.reshape(n_req, own_rows * 2 * padded // 128, 128)
    side_rows = jnp.pad(side_rows, ((0, 0), (0, drafts - side_rows.shape[1]), (0, 0)))
    fanned = call(
        values_kernel,
        "values",
        shape((n_req, half_heads + 1, drafts, DV), BF16),
        idx,
        kept,
        kept_stats,
        arrived,
        value_half,
        side_rows,
        gains,
        router_t,
    )
    gathered = lax.all_to_all(fanned, "req", split_axis=0, concat_axis=0, tiled=True)
    terms = call(
        project_kernel,
        "project",
        shape((2, n_exp, tokens // n_exp, padded), BF16),
        idx,
        gathered,
        out_proj_t,
        outside=(other_t,),
        scratch=(
            pltpu.VMEM((width, half_heads * DV), BF16),
            pltpu.SemaphoreType.DMA,
        ),
    )
    terms, idx, gains, router_t, w_down_other = lax.optimization_barrier(
        (terms, idx, gains, router_t, w_down_other)
    )
    terms = terms.reshape(2 * n_exp, tokens // n_exp, padded)
    terms = lax.all_to_all(terms, ("seq", "exp"), split_axis=0, concat_axis=0, tiled=True)
    fanned = call(
        hidden_kernel,
        "hidden",
        shape((n_req * n_exp, tokens // n_exp, padded), BF16),
        idx,
        terms,
    )
    own = lax.all_to_all(fanned, ("req", "exp"), split_axis=0, concat_axis=0, tiled=True)
    own = own.reshape(n_req, tokens, padded)
    other = swap(own)
    hidden_units = w_gate.shape[1]
    started = call(
        gate_up_own_kernel,
        "gate_up_own",
        (
            shape((tokens, hidden_units), F32),
            shape((tokens, hidden_units), F32),
            shape((tokens, experts), F32),
            shape((tokens, 128), F32),
        ),
        idx,
        own,
        gains,
        w_gate,
        w_up,
        router_t,
    )
    half = model_width // 2
    act, rows_here, w_down_other = call(
        gate_up_both_kernel,
        "gate_up_both",
        (
            shape((tokens, hidden_units), BF16),
            shape((n_req * 2, 16, padded), F32),
            shape((hidden_units, half), BF16),
        ),
        idx,
        *started,
        own,
        other,
        gains,
        w_gate,
        w_up,
        router_t,
        outside=(w_down_other,),
        scratch=(pltpu.SemaphoreType.DMA((2,)),),
    )
    pieces = call(
        down_kernel,
        "down",
        shape((tokens // 4, 4, half), BF16),
        idx,
        act,
        swap(act),
        w_down,
        w_down_other,
    )
    pieces = lax.all_to_all(pieces, ("exp", "req"), split_axis=0, concat_axis=0, tiled=True)
    mine, theirs = call(
        routed_kernel,
        "routed",
        (shape((own_rows, half), F32), shape((own_rows, half), F32)),
        idx,
        pieces,
    )
    return call(
        finish_kernel,
        "finish",
        shape((own_rows, model_width), BF16),
        idx,
        mine,
        swap(theirs),
        rows_here,
    )


def solution(mesh):
    in_specs = (
        P(("req", "seq", "exp"), None),
        P("req", None, "exp", None),
        P("req", "seq", None),
        P("req", "seq", None),
        P("req"),
        P("exp", None, None),
        P("exp", ("req", "seq")),
        P(),
        P(),
        P(("req", "seq", "exp"), None),
        P("req", None, ("seq", "exp")),
        P("req", None, ("seq", "exp")),
        P("req", ("seq", "exp"), None),
    )
    out_specs = P(("req", "seq", "exp"), None)
    return jax.shard_map(
        per_device, mesh=mesh, in_specs=in_specs, out_specs=out_specs, check_vma=False
    )
```

```python
import jax
import jax.numpy as jnp
from jax import lax
from jax.experimental import pallas as pl
from jax.experimental.pallas import tpu as pltpu
from jax.sharding import PartitionSpec as P

DL = 512
DR = 64
DV = 128
BLOCK = 64
F32 = jnp.float32
BF16 = jnp.bfloat16
SWAP = [(0, 1), (1, 0)]


def swap(x):
    return lax.ppermute(x, "seq", SWAP)


def vmem():
    return pl.BlockSpec(memory_space=pltpu.VMEM)


def call(kernel, name, out_shape, *operands, scalars=(), outside=(), scratch=(), limit=24):
    many = isinstance(out_shape, (tuple, list))
    return pl.pallas_call(
        kernel,
        out_shape=out_shape,
        in_specs=[pl.BlockSpec(memory_space=pltpu.SMEM) for _ in scalars]
        + [pl.BlockSpec(memory_space=pltpu.HBM) for _ in outside]
        + [vmem() for _ in operands],
        out_specs=[vmem() for _ in out_shape] if many else vmem(),
        scratch_shapes=list(scratch),
        compiler_params=pltpu.CompilerParams(vmem_limit_bytes=limit * 2**20),
        name=name,
    )(*scalars, *[pltpu.with_memory_space_constraint(a, pltpu.HBM) for a in outside], *operands)


def one_hot(shape, source):
    rows = lax.broadcasted_iota(jnp.int32, shape, 0)
    columns = lax.broadcasted_iota(jnp.int32, shape, 1)
    return jnp.where(source(rows) == columns, 1.0, 0.0).astype(BF16)


def parts_of(a):
    first = a.astype(BF16)
    rest = a - first.astype(F32)
    second = rest.astype(BF16)
    return first, second, (rest - second.astype(F32)).astype(BF16)


def attend_kernel(
    lengths, blocks, queries, cache, value_up, sent, kept, kept_stats, value_half, query_rows, key_rows, sems
):
    drafts, heads, width = queries.shape
    side = lax.axis_index("seq")
    length, first, second = lengths[0], blocks[0], blocks[1]
    shard_len = cache.shape[0]
    copies = [
        pltpu.make_async_copy(
            cache.at[pl.ds(pl.multiple_of(first * BLOCK, BLOCK), BLOCK), :],
            key_rows.at[pl.ds(0, BLOCK), :],
            sems.at[0],
        ),
        pltpu.make_async_copy(
            cache.at[pl.ds(pl.multiple_of(second * BLOCK, BLOCK), BLOCK), :],
            key_rows.at[pl.ds(BLOCK, BLOCK), :],
            sems.at[1],
        ),
        pltpu.make_async_copy(queries, query_rows, sems.at[2]),
    ]
    quarter = heads // 8
    value_copies = [
        pltpu.make_async_copy(
            value_up.at[pl.ds(side * (heads // 2) + i * quarter, quarter)],
            value_half.at[pl.ds(i * quarter, quarter)],
            sems.at[3 + i],
        )
        for i in range(4)
    ]
    for place, copy in enumerate(copies):
        copy.start(priority=place // 2)
    for place, copy in enumerate(value_copies):
        copy.start(priority=place % 2)
    for copy in copies:
        copy.wait()
    keys = key_rows[...]
    rows = query_rows[...].reshape(drafts * heads, width)
    scores = lax.dot_general(
        rows, keys, (((1,), (1,)), ((), ())), preferred_element_type=F32
    ) * ((DV + DR) ** (-0.5))
    row = lax.broadcasted_iota(jnp.int32, scores.shape, 0)
    col = lax.broadcasted_iota(jnp.int32, scores.shape, 1)
    block = jnp.where(col < BLOCK, first, second - 1)
    usable = side * shard_len + block * BLOCK + col < length - (drafts - 1) + row // heads
    top = jnp.max(jnp.where(usable, scores, -1e30), -1, keepdims=True)
    probs = jnp.where(usable, jnp.exp(scores - top), 0.0).astype(BF16)
    total = jnp.sum(probs.astype(F32), -1, keepdims=True)
    out = jnp.dot(probs, keys[:, :DL], preferred_element_type=F32)
    half = heads // 2

    def split(a):
        a = a.reshape(drafts, 2, half, a.shape[-1])
        low = a[:, 0].reshape(drafts * half, a.shape[-1])
        high = a[:, 1].reshape(drafts * half, a.shape[-1])
        return jnp.where(side == 0, low, high), jnp.where(side == 0, high, low)

    mine, theirs = split(out)
    stats = jnp.concatenate(
        [jnp.broadcast_to(top, (top.shape[0], 128)), jnp.broadcast_to(total, (top.shape[0], 128))],
        -1,
    )
    my_stats, their_stats = split(stats)
    kept[...] = mine
    kept_stats[...] = my_stats
    sent[:, :DL] = theirs.astype(BF16)
    top_parts, sum_parts = parts_of(their_stats[:, :128]), parts_of(their_stats[:, 128:])
    lane = lax.broadcasted_iota(jnp.int32, (drafts * half, 128), 1)
    packed = jnp.zeros((drafts * half, 128), F32)
    for place, part in enumerate(top_parts + sum_parts):
        packed = jnp.where(lane == place, part.astype(F32), packed)
    sent[:, DL:] = packed.astype(BF16)
    for copy in value_copies:
        copy.wait()


def values_kernel(kept, kept_stats, arrived, value_up, residual, expert_ids, fanned):
    rows = kept.shape[0]
    dests, slabs, drafts, _ = fanned.shape
    half = slabs - 1
    packed = arrived[:, DL:].astype(F32)
    lane = lax.broadcasted_iota(jnp.int32, packed.shape, 1)
    other_top = jnp.sum(jnp.where(lane < 3, packed, 0.0), -1, keepdims=True)
    other_sum = jnp.sum(jnp.where((lane >= 3) & (lane < 6), packed, 0.0), -1, keepdims=True)
    my_top, my_sum = kept_stats[:, 0:1], kept_stats[:, 128:129]
    top = jnp.maximum(my_top, other_top)
    my_scale, other_scale = jnp.exp(my_top - top), jnp.exp(other_top - top)
    total = my_scale * my_sum + other_scale * other_sum
    latent = (my_scale / total) * kept[...] + (other_scale / total) * arrived[:, :DL].astype(F32)
    latent = latent.astype(BF16)
    order = one_hot((rows, rows), lambda i: i % drafts * half + i // drafts)
    latent = jnp.dot(order, latent, preferred_element_type=F32).astype(BF16)
    for head in range(half):
        out = jnp.dot(
            latent[head * drafts : (head + 1) * drafts],
            value_up[head],
            preferred_element_type=F32,
        ).astype(BF16)
        for dest in range(dests):
            fanned[dest, head] = out
    own_rows, model_width = residual.shape
    width = model_width // (2 * dests)
    lane = lax.broadcasted_iota(jnp.int32, (own_rows, 128), 1)
    named = jnp.zeros((own_rows, 128), F32)
    for k in range(expert_ids.shape[1]):
        named += jnp.where(expert_ids[:, k : k + 1] + (width - 128) == lane, 1.0, 0.0)
    values = residual[...].astype(F32)
    values = jnp.concatenate([values, jnp.zeros((own_rows, 128), F32)], -1)
    for dest in range(dests):
        pieces = []
        for row in range(own_rows):
            for core in range(2):
                start = (dest * 2 + core) * width
                pieces.append(values[row : row + 1, start : start + 128])
                tail = values[row : row + 1, start + 128 : start + 256]
                pieces.append(jnp.where(lane[:1] < width - 128, tail, named[row : row + 1]))
        pieces.append(jnp.zeros((drafts - len(pieces), 128), F32))
        fanned[dest, half] = jnp.concatenate(pieces, 0).astype(BF16)


def project_terms(gathered, out_proj_t, side):
    reqs, slabs, drafts, lanes = gathered.shape
    half = slabs - 1
    total = None
    for head in range(0, half, 2):
        pair = jnp.concatenate(
            [gathered[:, head].reshape(reqs * drafts, lanes), gathered[:, head + 1].reshape(reqs * drafts, lanes)],
            -1,
        )
        start = pl.multiple_of((side * half + head) * lanes, 256)
        term = lax.dot_general(
            pair,
            out_proj_t[:, pl.ds(start, 2 * lanes)],
            (((1,), (1,)), ((), ())),
            preferred_element_type=F32,
        )
        total = term if total is None else total + term
    return total


def project_own_kernel(gathered, out_proj_t, swapped, out):
    out[...] = project_terms(gathered, out_proj_t, lax.axis_index("seq"))


def project_both_kernel(started, gathered, gathered_other, out_proj_t, terms, residual):
    reqs, slabs, drafts, lanes = gathered.shape
    exps, _, padded = terms.shape
    width = started.shape[1]
    side = lax.axis_index("seq")
    total = (started[...] + project_terms(gathered_other, out_proj_t, 1 - side)).astype(BF16)
    tokens = reqs * drafts
    own_rows = drafts // (2 * exps)

    def source(i):
        exp, req = i // (tokens // exps), i // (2 * own_rows) % reqs
        seq, row = i // own_rows % 2, i % own_rows
        return ((req * 2 + seq) * exps + exp) * own_rows + row

    total = jnp.dot(one_hot((tokens, tokens), source), total, preferred_element_type=F32)
    total = jnp.concatenate([total, jnp.zeros((tokens, padded - width), F32)], -1)
    terms[...] = total.astype(BF16).reshape(terms.shape)
    tiles = padded // lanes
    for tile in range(tiles):
        picked = jnp.zeros((tokens // exps, lanes), F32)
        for rows, from_side in ((gathered, side), (gathered_other, 1 - side)):

            def residual_source(i):
                req, seq, row = i // (2 * own_rows), i // own_rows % 2, i % own_rows
                place = req * drafts + (row * 2 + side) * tiles + tile
                return jnp.where(seq == from_side, place, -1)

            picked += jnp.dot(
                one_hot((tokens // exps, tokens), residual_source),
                rows[:, slabs - 1].reshape(tokens, lanes),
                preferred_element_type=F32,
            )
        residual[:, tile * lanes : (tile + 1) * lanes] = picked.astype(BF16)


def hidden_kernel(terms, residual, fanned):
    attended = jnp.sum(terms[...].astype(F32), 0).astype(BF16)
    hidden = (residual[...].astype(F32) + attended.astype(F32)).astype(BF16)
    for dest in range(fanned.shape[0]):
        fanned[dest] = hidden


def expert_terms(rows, gains, w_gate, w_up, router_t, side):
    steps, tokens, _ = rows.shape
    width = gains.shape[1] // (2 * steps)
    gate = jnp.zeros((tokens, w_gate.shape[1]), F32)
    up = jnp.zeros((tokens, w_up.shape[1]), F32)
    logits = jnp.zeros((tokens, router_t.shape[0]), F32)
    squares = jnp.zeros((tokens, width), F32)

    def columns_of(a, i):
        low = a[:, i * 2 * width : (i * 2 + 1) * width].astype(F32)
        high = a[:, (i * 2 + 1) * width : (i * 2 + 2) * width].astype(F32)
        return jnp.where(side == 0, low, high)

    for i in range(steps):
        start = pl.multiple_of((i * 2 + side) * width, 32)
        hidden = rows[i][:, :width].astype(F32)
        scaled = (hidden * columns_of(gains, i)).astype(BF16)
        gate += jnp.dot(scaled, w_gate[pl.ds(start, width), :], preferred_element_type=F32)
        up += jnp.dot(scaled, w_up[pl.ds(start, width), :], preferred_element_type=F32)
        logits += lax.dot_general(
            scaled,
            columns_of(router_t, i).astype(BF16),
            (((1,), (1,)), ((), ())),
            preferred_element_type=F32,
        )
        squares += hidden * hidden
    return gate, up, logits, jnp.sum(squares, -1, keepdims=True)


def gate_up_own_kernel(own, gains, w_gate, w_up, router_t, gate, up, logits, squares):
    a, b, c, d = expert_terms(own, gains, w_gate, w_up, router_t, lax.axis_index("seq"))
    gate[...], up[...], logits[...] = a, b, c
    squares[...] = jnp.broadcast_to(d, squares.shape)


def gate_up_both_kernel(
    gate, up, logits, squares, own, other, gains, w_gate, w_up, router_t, act, rows_here
):
    side = lax.axis_index("seq")
    own_rows = rows_here.shape[1]
    place = (lax.axis_index("exp") * own.shape[0] + lax.axis_index("req")) * 2 + side
    place = place * own_rows
    around = pl.ds(pl.multiple_of(place // 16 * 16, 16), 16)
    near = lax.broadcasted_iota(jnp.int32, (16, own.shape[2]), 0)
    for rows, from_side in ((own, side), (other, 1 - side)):
        for i in range(own.shape[0]):
            tile = rows[i, around, :].astype(F32)
            picked = [
                jnp.sum(jnp.where(near == place % 16 + row, tile, 0.0), 0, keepdims=True)
                for row in range(own_rows)
            ]
            rows_here[i * 2 + from_side] = jnp.concatenate(picked, 0)
    width = gains.shape[1] // (2 * own.shape[0])
    experts = logits.shape[1]
    columns = gains.shape[1]
    a, b, c, d = expert_terms(other, gains, w_gate, w_up, router_t, 1 - side)
    scale = lax.rsqrt((squares[:, 0:1] + d) / columns + 1e-06)
    named = own[0, :, width : width + experts].astype(F32)
    chosen = named * jax.nn.sigmoid((logits[...] + c) * scale)
    mine = lax.broadcasted_iota(jnp.int32, chosen.shape, 1) == lax.axis_index("req")
    weight = jnp.sum(jnp.where(mine, chosen, 0.0), -1, keepdims=True)
    weight = weight / jnp.sum(chosen, -1, keepdims=True) * 2.5
    act[...] = (
        jax.nn.silu((gate[...] + a) * scale) * ((up[...] + b) * scale) * weight
    ).astype(BF16)


DOWN_STEPS = 7


def down_kernel(act, act_other, w_down, w_down_other, out):
    half = out.shape[2]
    block = half // DOWN_STEPS
    for i in range(DOWN_STEPS):
        columns = pl.ds(pl.multiple_of(lax.axis_index("seq") * half + i * block, 128), block)
        total = jnp.dot(act[...], w_down[:, columns], preferred_element_type=F32)
        total += jnp.dot(act_other[...], w_down_other[:, columns], preferred_element_type=F32)
        out[:, :, i * block : (i + 1) * block] = total.reshape(out.shape[:2] + (block,)).astype(BF16)


def routed_kernel(pieces, mine, theirs):
    rows = mine.shape[0]
    total = jnp.sum(pieces[...].astype(F32), 0)
    side = lax.axis_index("seq")
    low, high = total[:rows], total[rows:]
    mine[...] = jnp.where(side == 0, low, high)
    theirs[...] = jnp.where(side == 0, high, low)


def finish_kernel(mine, theirs, rows_here, out):
    blocks, rows, half = rows_here.shape[0], mine.shape[0], mine.shape[1]
    width = 2 * half // blocks
    for side, first, second in ((0, mine, theirs), (1, theirs, mine)):

        @pl.when(lax.axis_index("seq") == side)
        def _():
            for block in range(blocks):
                start = block * width
                source, offset = (first, start) if start < half else (second, start - half)
                total = rows_here[block, :rows, :width] + source[:, offset : offset + width]
                out[:, start : start + width] = total.astype(BF16)


def per_device(
    residual,
    queries,
    latent_cache,
    blocks,
    lengths,
    value_up,
    out_proj,
    norm_gain,
    router,
    expert_ids,
    w_gate,
    w_up,
    w_down,
):
    drafts, heads, qk_width = queries.shape[1:]
    n_req, n_exp = lax.axis_size("req"), lax.axis_size("exp")
    model_width = residual.shape[1]
    experts = router.shape[1]
    width = out_proj.shape[1]
    padded = -(-width // 128) * 128
    own_rows = residual.shape[0]
    tokens = n_req * drafts
    half_heads = heads // 2
    half_rows = drafts * half_heads
    half = model_width // 2
    shape = jax.ShapeDtypeStruct
    w_gate, w_up, w_down = w_gate[0], w_up[0], w_down[0]
    hidden_units = w_gate.shape[1]
    gains, router_t, out_proj_t = norm_gain.reshape(1, model_width), router.T, out_proj.T

    sent, kept, kept_stats, value_half = call(
        attend_kernel,
        "attend",
        (
            shape((half_rows, DL + 128), BF16),
            shape((half_rows, DL), F32),
            shape((half_rows, 256), F32),
            shape((half_heads,) + value_up.shape[1:], BF16),
        ),
        scalars=(lengths, blocks.reshape(-1)),
        outside=(queries[0], latent_cache[0], value_up),
        scratch=(
            pltpu.VMEM(queries.shape[1:], BF16),
            pltpu.VMEM((blocks.shape[2] * BLOCK, qk_width), BF16),
            pltpu.SemaphoreType.DMA((7,)),
        ),
    )
    arrived = swap(sent)
    w_down_other = swap(w_down)
    fanned = call(
        values_kernel,
        "values",
        shape((n_req, half_heads + 1, drafts, DV), BF16),
        kept,
        kept_stats,
        arrived,
        value_half,
        residual,
        expert_ids,
    )
    gathered = lax.all_to_all(fanned, "req", split_axis=0, concat_axis=0, tiled=True)
    gathered_other = swap(gathered)
    started = call(
        project_own_kernel,
        "project_own",
        shape((tokens, width), F32),
        gathered,
        out_proj_t,
        w_down_other,
    )
    terms, resid = call(
        project_both_kernel,
        "project_both",
        (
            shape((n_exp, tokens // n_exp, padded), BF16),
            shape((tokens // n_exp, padded), BF16),
        ),
        started,
        gathered,
        gathered_other,
        out_proj_t,
    )
    terms = lax.all_to_all(terms, "exp", split_axis=0, concat_axis=0, tiled=True)
    fanned = call(
        hidden_kernel,
        "hidden",
        shape((n_req * n_exp, tokens // n_exp, padded), BF16),
        terms,
        resid,
    )
    own = lax.all_to_all(fanned, ("req", "exp"), split_axis=0, concat_axis=0, tiled=True)
    own = own.reshape(n_req, tokens, padded)
    other = swap(own)
    started = call(
        gate_up_own_kernel,
        "gate_up_own",
        (
            shape((tokens, hidden_units), F32),
            shape((tokens, hidden_units), F32),
            shape((tokens, experts), F32),
            shape((tokens, 128), F32),
        ),
        own,
        gains,
        w_gate,
        w_up,
        router_t,
    )
    act, rows_here = call(
        gate_up_both_kernel,
        "gate_up_both",
        (
            shape((tokens, hidden_units), BF16),
            shape((n_req * 2, own_rows, padded), F32),
        ),
        *started,
        own,
        other,
        gains,
        w_gate,
        w_up,
        router_t,
    )
    pieces = call(
        down_kernel,
        "down",
        shape((tokens // 4, 4, half), BF16),
        act,
        swap(act),
        w_down,
        w_down_other,
    )
    pieces = lax.all_to_all(pieces, ("exp", "req"), split_axis=0, concat_axis=0, tiled=True)
    mine, theirs = call(
        routed_kernel,
        "routed",
        (shape((own_rows, half), F32), shape((own_rows, half), F32)),
        pieces,
    )
    return call(
        finish_kernel,
        "finish",
        shape((own_rows, model_width), BF16),
        mine,
        swap(theirs),
        rows_here,
    )


def solution(mesh):
    in_specs = (
        P(("req", "seq", "exp"), None),
        P("req", None, "exp", None),
        P("req", "seq", None),
        P("req", "seq", None),
        P("req"),
        P("exp", None, None),
        P("exp", ("req", "seq")),
        P(),
        P(),
        P(("req", "seq", "exp"), None),
        P("req", None, ("seq", "exp")),
        P("req", None, ("seq", "exp")),
        P("req", ("seq", "exp"), None),
    )
    out_specs = P(("req", "seq", "exp"), None)
    return jax.shard_map(
        per_device, mesh=mesh, in_specs=in_specs, out_specs=out_specs, check_vma=False
    )
```

```python
import jax
import jax.numpy as jnp
from jax import lax
from jax.experimental import pallas as pl
from jax.experimental.pallas import tpu as pltpu
from jax.sharding import PartitionSpec as P


DL = 512
DR = 64
DV = 128
BLOCK = 64
F32 = jnp.float32
BF16 = jnp.bfloat16
SWAP = [(0, 1), (1, 0)]


def swap(x):
    return lax.ppermute(x, "seq", SWAP)


def vmem():
    return pl.BlockSpec(memory_space=pltpu.VMEM)


def call(kernel, out_shape, *operands, scalars=(), outside=(), scratch=(), limit=24):
    many = isinstance(out_shape, (tuple, list))
    return pl.pallas_call(
        kernel,
        out_shape=out_shape,
        in_specs=[pl.BlockSpec(memory_space=pltpu.SMEM) for _ in scalars]
        + [pl.BlockSpec(memory_space=pltpu.HBM) for _ in outside]
        + [vmem() for _ in operands],
        out_specs=[vmem() for _ in out_shape] if many else vmem(),
        scratch_shapes=list(scratch),
        compiler_params=pltpu.CompilerParams(vmem_limit_bytes=limit * 2**20),
    )(*scalars, *[pltpu.with_memory_space_constraint(a, pltpu.HBM) for a in outside], *operands)


def one_hot(shape, source):
    rows = lax.broadcasted_iota(jnp.int32, shape, 0)
    columns = lax.broadcasted_iota(jnp.int32, shape, 1)
    return jnp.where(source(rows) == columns, 1.0, 0.0).astype(BF16)


def parts_of(a):
    first = a.astype(BF16)
    rest = a - first.astype(F32)
    second = rest.astype(BF16)
    return first, second, (rest - second.astype(F32)).astype(BF16)


def attend_kernel(
    lengths, blocks, queries, cache, value_up, sent, kept, kept_stats, value_half, query_rows, key_rows, sems
):
    drafts, heads, width = queries.shape
    side = lax.axis_index("seq")
    length, first, second = lengths[0], blocks[0], blocks[1]
    shard_len = cache.shape[0]
    copies = [
        pltpu.make_async_copy(
            cache.at[pl.ds(pl.multiple_of(first * BLOCK, BLOCK), BLOCK), :],
            key_rows.at[pl.ds(0, BLOCK), :],
            sems.at[0],
        ),
        pltpu.make_async_copy(
            cache.at[pl.ds(pl.multiple_of(second * BLOCK, BLOCK), BLOCK), :],
            key_rows.at[pl.ds(BLOCK, BLOCK), :],
            sems.at[1],
        ),
        pltpu.make_async_copy(queries, query_rows, sems.at[2]),
    ]
    quarter = heads // 8
    value_copies = [
        pltpu.make_async_copy(
            value_up.at[pl.ds(side * (heads // 2) + i * quarter, quarter)],
            value_half.at[pl.ds(i * quarter, quarter)],
            sems.at[3 + i],
        )
        for i in range(4)
    ]
    for place, copy in enumerate(copies):
        copy.start(priority=place // 2)
    for place, copy in enumerate(value_copies):
        copy.start(priority=place % 2)
    for copy in copies:
        copy.wait()
    keys = key_rows[...]
    rows = query_rows[...].reshape(drafts * heads, width)
    scores = lax.dot_general(
        rows, keys, (((1,), (1,)), ((), ())), preferred_element_type=F32
    ) * ((DV + DR) ** (-0.5))
    row = lax.broadcasted_iota(jnp.int32, scores.shape, 0)
    col = lax.broadcasted_iota(jnp.int32, scores.shape, 1)
    block = jnp.where(col < BLOCK, first, second - 1)
    usable = side * shard_len + block * BLOCK + col < length - (drafts - 1) + row // heads
    top = jnp.max(jnp.where(usable, scores, -1e30), -1, keepdims=True)
    probs = jnp.where(usable, jnp.exp(scores - top), 0.0).astype(BF16)
    total = jnp.sum(probs.astype(F32), -1, keepdims=True)
    out = jnp.dot(probs, keys[:, :DL], preferred_element_type=F32)
    half = heads // 2

    def split(a):
        a = a.reshape(drafts, 2, half, a.shape[-1])
        low = a[:, 0].reshape(drafts * half, a.shape[-1])
        high = a[:, 1].reshape(drafts * half, a.shape[-1])
        return jnp.where(side == 0, low, high), jnp.where(side == 0, high, low)

    mine, theirs = split(out)
    stats = jnp.concatenate(
        [jnp.broadcast_to(top, (top.shape[0], 128)), jnp.broadcast_to(total, (top.shape[0], 128))],
        -1,
    )
    my_stats, their_stats = split(stats)
    kept[...] = mine
    kept_stats[...] = my_stats
    sent[:, :DL] = theirs.astype(BF16)
    top_parts, sum_parts = parts_of(their_stats[:, :128]), parts_of(their_stats[:, 128:])
    lane = lax.broadcasted_iota(jnp.int32, (drafts * half, 128), 1)
    packed = jnp.zeros((drafts * half, 128), F32)
    for place, part in enumerate(top_parts + sum_parts):
        packed = jnp.where(lane == place, part.astype(F32), packed)
    sent[:, DL:] = packed.astype(BF16)
    for copy in value_copies:
        copy.wait()


def values_kernel(kept, kept_stats, arrived, value_up, residual, expert_ids, fanned):
    rows = kept.shape[0]
    dests, slabs, drafts, _ = fanned.shape
    half = slabs - 1
    packed = arrived[:, DL:].astype(F32)
    lane = lax.broadcasted_iota(jnp.int32, packed.shape, 1)
    other_top = jnp.sum(jnp.where(lane < 3, packed, 0.0), -1, keepdims=True)
    other_sum = jnp.sum(jnp.where((lane >= 3) & (lane < 6), packed, 0.0), -1, keepdims=True)
    my_top, my_sum = kept_stats[:, 0:1], kept_stats[:, 128:129]
    top = jnp.maximum(my_top, other_top)
    my_scale, other_scale = jnp.exp(my_top - top), jnp.exp(other_top - top)
    total = my_scale * my_sum + other_scale * other_sum
    latent = (my_scale / total) * kept[...] + (other_scale / total) * arrived[:, :DL].astype(F32)
    latent = latent.astype(BF16)
    order = one_hot((rows, rows), lambda i: i % drafts * half + i // drafts)
    latent = jnp.dot(order, latent, preferred_element_type=F32).astype(BF16)
    for head in range(half):
        out = jnp.dot(
            latent[head * drafts : (head + 1) * drafts],
            value_up[head],
            preferred_element_type=F32,
        ).astype(BF16)
        for dest in range(dests):
            fanned[dest, head] = out
    own_rows, model_width = residual.shape
    width = model_width // (2 * dests)
    lane = lax.broadcasted_iota(jnp.int32, (own_rows, 128), 1)
    named = jnp.zeros((own_rows, 128), F32)
    for k in range(expert_ids.shape[1]):
        named += jnp.where(expert_ids[:, k : k + 1] + (width - 128) == lane, 1.0, 0.0)
    values = residual[...].astype(F32)
    values = jnp.concatenate([values, jnp.zeros((own_rows, 128), F32)], -1)
    for dest in range(dests):
        pieces = []
        for row in range(own_rows):
            for core in range(2):
                start = (dest * 2 + core) * width
                pieces.append(values[row : row + 1, start : start + 128])
                tail = values[row : row + 1, start + 128 : start + 256]
                pieces.append(jnp.where(lane[:1] < width - 128, tail, named[row : row + 1]))
        pieces.append(jnp.zeros((drafts - len(pieces), 128), F32))
        fanned[dest, half] = jnp.concatenate(pieces, 0).astype(BF16)


def project_terms(gathered, out_proj_t, side):
    reqs, slabs, drafts, lanes = gathered.shape
    half = slabs - 1
    total = None
    for head in range(0, half, 2):
        pair = jnp.concatenate(
            [gathered[:, head].reshape(reqs * drafts, lanes), gathered[:, head + 1].reshape(reqs * drafts, lanes)],
            -1,
        )
        start = pl.multiple_of((side * half + head) * lanes, 256)
        term = lax.dot_general(
            pair,
            out_proj_t[:, pl.ds(start, 2 * lanes)],
            (((1,), (1,)), ((), ())),
            preferred_element_type=F32,
        )
        total = term if total is None else total + term
    return total


def residual_rows(gathered, column_side, tiles):
    reqs, slabs, drafts, lanes = gathered.shape
    beside = gathered[:, slabs - 1].reshape(reqs * drafts, lanes)
    picked = []
    for tile in range(tiles):

        def source(i):
            return i // 2 * drafts + (i % 2 * 2 + column_side) * tiles + tile

        order = one_hot((reqs * 2, reqs * drafts), source)
        picked.append(jnp.dot(order, beside, preferred_element_type=F32))
    return jnp.concatenate(picked, -1).astype(BF16)


def project_other_kernel(gathered, other_t, swapped, out):
    tokens = gathered.shape[0] * gathered.shape[2]
    side = lax.axis_index("seq")
    width, padded = other_t.shape[0], out.shape[1]
    total = project_terms(gathered, other_t, side)
    total = jnp.concatenate([total, jnp.zeros((tokens, padded - width), F32)], -1)
    out[:tokens] = total.astype(BF16)
    out[tokens:] = residual_rows(gathered, 1 - side, padded // gathered.shape[3])


def project_own_kernel(gathered, out_proj_t, out):
    out[...] = project_terms(gathered, out_proj_t, lax.axis_index("seq"))


def project_sum_kernel(started, arrived, gathered, terms, residual):
    reqs, _, drafts, lanes = gathered.shape
    exps, _, padded = terms.shape
    width = started.shape[1]
    side = lax.axis_index("seq")
    tokens = reqs * drafts
    own_rows = drafts // (2 * exps)
    total = (started[...] + arrived[:tokens, :width].astype(F32)).astype(BF16)

    def source(i):
        exp, req = i // (tokens // exps), i // (2 * own_rows) % reqs
        seq, row = i // own_rows % 2, i % own_rows
        return ((req * 2 + seq) * exps + exp) * own_rows + row

    total = jnp.dot(one_hot((tokens, tokens), source), total, preferred_element_type=F32)
    total = jnp.concatenate([total, jnp.zeros((tokens, padded - width), F32)], -1)
    terms[...] = total.astype(BF16).reshape(terms.shape)
    picked = jnp.zeros(residual.shape, F32)
    for rows, from_side in (
        (residual_rows(gathered, side, padded // lanes), side),
        (arrived[tokens:], 1 - side),
    ):

        def residual_source(i):
            req, seq, row = i // (2 * own_rows), i // own_rows % 2, i % own_rows
            return jnp.where(seq == from_side, req * own_rows + row, -1)

        order = one_hot((residual.shape[0], rows.shape[0]), residual_source)
        picked += jnp.dot(order, rows, preferred_element_type=F32)
    residual[...] = picked.astype(BF16)


def hidden_kernel(terms, residual, fanned):
    attended = jnp.sum(terms[...].astype(F32), 0).astype(BF16)
    hidden = (residual[...].astype(F32) + attended.astype(F32)).astype(BF16)
    for dest in range(fanned.shape[0]):
        fanned[dest] = hidden


def expert_terms(rows, gains, w_gate, w_up, router_t, side):
    steps, tokens, _ = rows.shape
    width = gains.shape[1] // (2 * steps)
    gate = jnp.zeros((tokens, w_gate.shape[1]), F32)
    up = jnp.zeros((tokens, w_up.shape[1]), F32)
    logits = jnp.zeros((tokens, router_t.shape[0]), F32)
    squares = jnp.zeros((tokens, width), F32)

    def columns_of(a, i):
        low = a[:, i * 2 * width : (i * 2 + 1) * width].astype(F32)
        high = a[:, (i * 2 + 1) * width : (i * 2 + 2) * width].astype(F32)
        return jnp.where(side == 0, low, high)

    for i in range(steps):
        start = pl.multiple_of((i * 2 + side) * width, 32)
        hidden = rows[i][:, :width].astype(F32)
        scaled = (hidden * columns_of(gains, i)).astype(BF16)
        gate += jnp.dot(scaled, w_gate[pl.ds(start, width), :], preferred_element_type=F32)
        up += jnp.dot(scaled, w_up[pl.ds(start, width), :], preferred_element_type=F32)
        logits += lax.dot_general(
            scaled,
            columns_of(router_t, i).astype(BF16),
            (((1,), (1,)), ((), ())),
            preferred_element_type=F32,
        )
        squares += hidden * hidden
    return gate, up, logits, jnp.sum(squares, -1, keepdims=True)


def gate_up_own_kernel(own, gains, w_gate, w_up, router_t, gate, up, logits, squares):
    a, b, c, d = expert_terms(own, gains, w_gate, w_up, router_t, lax.axis_index("seq"))
    gate[...], up[...], logits[...] = a, b, c
    squares[...] = jnp.broadcast_to(d, squares.shape)


def gate_up_both_kernel(
    gate, up, logits, squares, own, other, gains, w_gate, w_up, router_t,
    act_mine, act_theirs, rows_here,
):
    side = lax.axis_index("seq")
    own_rows = rows_here.shape[1]
    place = (lax.axis_index("exp") * own.shape[0] + lax.axis_index("req")) * 2 + side
    place = place * own_rows
    around = pl.ds(pl.multiple_of(place // 16 * 16, 16), 16)
    near = lax.broadcasted_iota(jnp.int32, (16, own.shape[2]), 0)
    for rows, from_side in ((own, side), (other, 1 - side)):
        for i in range(own.shape[0]):
            tile = rows[i, around, :].astype(F32)
            picked = [
                jnp.sum(jnp.where(near == place % 16 + row, tile, 0.0), 0, keepdims=True)
                for row in range(own_rows)
            ]
            rows_here[i * 2 + from_side] = jnp.concatenate(picked, 0)
    width = gains.shape[1] // (2 * own.shape[0])
    experts = logits.shape[1]
    columns = gains.shape[1]
    a, b, c, d = expert_terms(other, gains, w_gate, w_up, router_t, 1 - side)
    scale = lax.rsqrt((squares[:, 0:1] + d) / columns + 1e-06)
    named = own[0, :, width : width + experts].astype(F32)
    chosen = named * jax.nn.sigmoid((logits[...] + c) * scale)
    mine = lax.broadcasted_iota(jnp.int32, chosen.shape, 1) == lax.axis_index("req")
    weight = jnp.sum(jnp.where(mine, chosen, 0.0), -1, keepdims=True)
    weight = weight / jnp.sum(chosen, -1, keepdims=True) * 2.5
    act = (jax.nn.silu((gate[...] + a) * scale) * ((up[...] + b) * scale) * weight).astype(BF16)
    tokens = act.shape[0]
    reqs = own.shape[0]
    for out, seq in ((act_mine, side), (act_theirs, 1 - side)):

        def source(i):
            exp, req, row = i // (reqs * own_rows), i // own_rows % reqs, i % own_rows
            return ((exp * reqs + req) * 2 + seq) * own_rows + row

        order = one_hot((tokens // 2, tokens), source)
        out[...] = jnp.dot(order, act, preferred_element_type=F32).astype(BF16)


DOWN_STEPS = 14


def down_kernel(act, act_other, w_down, w_down_other, out):
    block = out.shape[2] // DOWN_STEPS
    for i in range(DOWN_STEPS):
        columns = slice(i * block, (i + 1) * block)
        total = jnp.dot(act[...], w_down[:, columns], preferred_element_type=F32)
        total += jnp.dot(act_other[...], w_down_other[:, columns], preferred_element_type=F32)
        out[:, :, columns] = total.reshape(out.shape[:2] + (block,)).astype(BF16)


def finish_kernel(pieces, rows_here, out):
    blocks, rows = rows_here.shape[0], out.shape[0]
    width = out.shape[1] // blocks
    total = jnp.sum(pieces[...].astype(F32), 0)
    hidden = jnp.concatenate([rows_here[block, :rows, :width] for block in range(blocks)], -1)
    out[...] = (hidden + total).astype(BF16)


def per_device(
    residual,
    queries,
    latent_cache,
    blocks,
    lengths,
    value_up,
    out_proj,
    norm_gain,
    router,
    expert_ids,
    w_gate,
    w_up,
    w_down,
):
    drafts, heads, qk_width = queries.shape[1:]
    n_req, n_exp = lax.axis_size("req"), lax.axis_size("exp")
    model_width = residual.shape[1]
    experts = router.shape[1]
    width = out_proj.shape[1]
    padded = -(-width // 128) * 128
    own_rows = residual.shape[0]
    tokens = n_req * drafts
    half_heads = heads // 2
    half_rows = drafts * half_heads
    shape = jax.ShapeDtypeStruct
    w_gate, w_up, w_down = w_gate[0], w_up[0], w_down[0]
    hidden_units = w_gate.shape[1]
    gains, router_t, out_proj_t = norm_gain.reshape(1, model_width), router.T, out_proj.T

    sent, kept, kept_stats, value_half = call(
        attend_kernel,
        (
            shape((half_rows, DL + 128), BF16),
            shape((half_rows, DL), F32),
            shape((half_rows, 256), F32),
            shape((half_heads,) + value_up.shape[1:], BF16),
        ),
        scalars=(lengths, blocks.reshape(-1)),
        outside=(queries[0], latent_cache[0], value_up),
        scratch=(
            pltpu.VMEM(queries.shape[1:], BF16),
            pltpu.VMEM((blocks.shape[2] * BLOCK, qk_width), BF16),
            pltpu.SemaphoreType.DMA((7,)),
        ),
    )
    arrived = swap(sent)
    other_t = swap(out_proj_t)
    w_down_other = swap(w_down)
    fanned = call(
        values_kernel,
        shape((n_req, half_heads + 1, drafts, DV), BF16),
        kept,
        kept_stats,
        arrived,
        value_half,
        residual,
        expert_ids,
    )
    gathered = lax.all_to_all(fanned, "req", split_axis=0, concat_axis=0, tiled=True)
    arrived = swap(
        call(
            project_other_kernel,
            shape((tokens + n_req * own_rows, padded), BF16),
            gathered,
            other_t,
            w_down_other,
        )
    )
    started = call(project_own_kernel, shape((tokens, width), F32), gathered, out_proj_t)
    terms, resid = call(
        project_sum_kernel,
        (
            shape((n_exp, tokens // n_exp, padded), BF16),
            shape((tokens // n_exp, padded), BF16),
        ),
        started,
        arrived,
        gathered,
    )
    terms = lax.all_to_all(terms, "exp", split_axis=0, concat_axis=0, tiled=True)
    fanned = call(
        hidden_kernel, shape((n_req * n_exp, tokens // n_exp, padded), BF16), terms, resid
    )
    own = lax.all_to_all(fanned, ("req", "exp"), split_axis=0, concat_axis=0, tiled=True)
    own = own.reshape(n_req, tokens, padded)
    other = swap(own)
    started = call(
        gate_up_own_kernel,
        (
            shape((tokens, hidden_units), F32),
            shape((tokens, hidden_units), F32),
            shape((tokens, experts), F32),
            shape((tokens, 128), F32),
        ),
        own,
        gains,
        w_gate,
        w_up,
        router_t,
    )
    act_mine, act_theirs, rows_here = call(
        gate_up_both_kernel,
        (
            shape((tokens // 2, hidden_units), BF16),
            shape((tokens // 2, hidden_units), BF16),
            shape((n_req * 2, own_rows, padded), F32),
        ),
        *started,
        own,
        other,
        gains,
        w_gate,
        w_up,
        router_t,
    )
    pieces = call(
        down_kernel,
        shape((n_req * n_exp, own_rows, model_width), BF16),
        act_mine,
        swap(act_theirs),
        w_down,
        w_down_other,
    )
    pieces = lax.all_to_all(pieces, ("exp", "req"), split_axis=0, concat_axis=0, tiled=True)
    return call(finish_kernel, shape((own_rows, model_width), BF16), pieces, rows_here)


def solution(mesh):
    in_specs = (
        P(("req", "seq", "exp"), None),
        P("req", None, "exp", None),
        P("req", "seq", None),
        P("req", "seq", None),
        P("req"),
        P("exp", None, None),
        P("exp", ("req", "seq")),
        P(),
        P(),
        P(("req", "seq", "exp"), None),
        P("req", None, ("seq", "exp")),
        P("req", None, ("seq", "exp")),
        P("req", ("seq", "exp"), None),
    )
    out_specs = P(("req", "seq", "exp"), None)

    return jax.shard_map(per_device, mesh=mesh, in_specs=in_specs, out_specs=out_specs, check_vma=False)
```

```python
import jax
import jax.numpy as jnp
from jax import lax
from jax.experimental import pallas as pl
from jax.experimental.pallas import tpu as pltpu
from jax.sharding import PartitionSpec as P


DL = 512
DR = 64
DV = 128
BLOCK = 64
F32 = jnp.float32
BF16 = jnp.bfloat16
SWAP = [(0, 1), (1, 0)]


def swap(x):
    return lax.ppermute(x, "seq", SWAP)


def vmem():
    return pl.BlockSpec(memory_space=pltpu.VMEM)


def call(kernel, out_shape, *operands, scalars=(), outside=(), scratch=(), limit=24):
    many = isinstance(out_shape, (tuple, list))
    return pl.pallas_call(
        kernel,
        out_shape=out_shape,
        in_specs=[pl.BlockSpec(memory_space=pltpu.SMEM) for _ in scalars]
        + [pl.BlockSpec(memory_space=pltpu.HBM) for _ in outside]
        + [vmem() for _ in operands],
        out_specs=[vmem() for _ in out_shape] if many else vmem(),
        scratch_shapes=list(scratch),
        compiler_params=pltpu.CompilerParams(vmem_limit_bytes=limit * 2**20),
    )(*scalars, *[pltpu.with_memory_space_constraint(a, pltpu.HBM) for a in outside], *operands)


def one_hot(shape, source):
    rows = lax.broadcasted_iota(jnp.int32, shape, 0)
    columns = lax.broadcasted_iota(jnp.int32, shape, 1)
    return jnp.where(source(rows) == columns, 1.0, 0.0).astype(BF16)


def parts_of(a):
    first = a.astype(BF16)
    rest = a - first.astype(F32)
    second = rest.astype(BF16)
    return first, second, (rest - second.astype(F32)).astype(BF16)


def attend_kernel(
    lengths, blocks, queries, cache, value_up, sent, kept, kept_stats, value_half, query_rows, key_rows, sems
):
    drafts, heads, width = queries.shape
    side = lax.axis_index("seq")
    length, first, second = lengths[0], blocks[0], blocks[1]
    shard_len = cache.shape[0]
    copies = [
        pltpu.make_async_copy(
            cache.at[pl.ds(pl.multiple_of(first * BLOCK, BLOCK), BLOCK), :],
            key_rows.at[pl.ds(0, BLOCK), :],
            sems.at[0],
        ),
        pltpu.make_async_copy(
            cache.at[pl.ds(pl.multiple_of(second * BLOCK, BLOCK), BLOCK), :],
            key_rows.at[pl.ds(BLOCK, BLOCK), :],
            sems.at[1],
        ),
        pltpu.make_async_copy(queries, query_rows, sems.at[2]),
    ]
    quarter = heads // 8
    value_copies = [
        pltpu.make_async_copy(
            value_up.at[pl.ds(side * (heads // 2) + i * quarter, quarter)],
            value_half.at[pl.ds(i * quarter, quarter)],
            sems.at[3 + i],
        )
        for i in range(4)
    ]
    for place, copy in enumerate(copies):
        copy.start(priority=place // 2)
    for place, copy in enumerate(value_copies):
        copy.start(priority=place % 2)
    for copy in copies:
        copy.wait()
    keys = key_rows[...]
    rows = query_rows[...].reshape(drafts * heads, width)
    scores = lax.dot_general(
        rows, keys, (((1,), (1,)), ((), ())), preferred_element_type=F32
    ) * ((DV + DR) ** (-0.5))
    row = lax.broadcasted_iota(jnp.int32, scores.shape, 0)
    col = lax.broadcasted_iota(jnp.int32, scores.shape, 1)
    block = jnp.where(col < BLOCK, first, second - 1)
    usable = side * shard_len + block * BLOCK + col < length - (drafts - 1) + row // heads
    top = jnp.max(jnp.where(usable, scores, -1e30), -1, keepdims=True)
    probs = jnp.where(usable, jnp.exp(scores - top), 0.0).astype(BF16)
    total = jnp.sum(probs.astype(F32), -1, keepdims=True)
    out = jnp.dot(probs, keys[:, :DL], preferred_element_type=F32)
    half = heads // 2

    def split(a):
        a = a.reshape(drafts, 2, half, a.shape[-1])
        low = a[:, 0].reshape(drafts * half, a.shape[-1])
        high = a[:, 1].reshape(drafts * half, a.shape[-1])
        return jnp.where(side == 0, low, high), jnp.where(side == 0, high, low)

    mine, theirs = split(out)
    stats = jnp.concatenate(
        [jnp.broadcast_to(top, (top.shape[0], 128)), jnp.broadcast_to(total, (top.shape[0], 128))],
        -1,
    )
    my_stats, their_stats = split(stats)
    kept[...] = mine
    kept_stats[...] = my_stats
    sent[:, :DL] = theirs.astype(BF16)
    top_parts, sum_parts = parts_of(their_stats[:, :128]), parts_of(their_stats[:, 128:])
    lane = lax.broadcasted_iota(jnp.int32, (drafts * half, 128), 1)
    packed = jnp.zeros((drafts * half, 128), F32)
    for place, part in enumerate(top_parts + sum_parts):
        packed = jnp.where(lane == place, part.astype(F32), packed)
    sent[:, DL:] = packed.astype(BF16)
    for copy in value_copies:
        copy.wait()


def values_kernel(kept, kept_stats, arrived, value_up, residual, expert_ids, fanned):
    rows = kept.shape[0]
    dests, slabs, drafts, _ = fanned.shape
    half = slabs - 1
    packed = arrived[:, DL:].astype(F32)
    lane = lax.broadcasted_iota(jnp.int32, packed.shape, 1)
    other_top = jnp.sum(jnp.where(lane < 3, packed, 0.0), -1, keepdims=True)
    other_sum = jnp.sum(jnp.where((lane >= 3) & (lane < 6), packed, 0.0), -1, keepdims=True)
    my_top, my_sum = kept_stats[:, 0:1], kept_stats[:, 128:129]
    top = jnp.maximum(my_top, other_top)
    my_scale, other_scale = jnp.exp(my_top - top), jnp.exp(other_top - top)
    total = my_scale * my_sum + other_scale * other_sum
    latent = (my_scale / total) * kept[...] + (other_scale / total) * arrived[:, :DL].astype(F32)
    latent = latent.astype(BF16)
    order = one_hot((rows, rows), lambda i: i % drafts * half + i // drafts)
    latent = jnp.dot(order, latent, preferred_element_type=F32).astype(BF16)
    for head in range(half):
        out = jnp.dot(
            latent[head * drafts : (head + 1) * drafts],
            value_up[head],
            preferred_element_type=F32,
        ).astype(BF16)
        for dest in range(dests):
            fanned[dest, head] = out
    own_rows, model_width = residual.shape
    width = model_width // (2 * dests)
    lane = lax.broadcasted_iota(jnp.int32, (own_rows, 128), 1)
    named = jnp.zeros((own_rows, 128), F32)
    for k in range(expert_ids.shape[1]):
        named += jnp.where(expert_ids[:, k : k + 1] + (width - 128) == lane, 1.0, 0.0)
    values = residual[...].astype(F32)
    values = jnp.concatenate([values, jnp.zeros((own_rows, 128), F32)], -1)
    for dest in range(dests):
        pieces = []
        for row in range(own_rows):
            for core in range(2):
                start = (dest * 2 + core) * width
                pieces.append(values[row : row + 1, start : start + 128])
                tail = values[row : row + 1, start + 128 : start + 256]
                pieces.append(jnp.where(lane[:1] < width - 128, tail, named[row : row + 1]))
        pieces.append(jnp.zeros((drafts - len(pieces), 128), F32))
        fanned[dest, half] = jnp.concatenate(pieces, 0).astype(BF16)


def project_terms(gathered, out_proj_t, side):
    reqs, slabs, drafts, lanes = gathered.shape
    half = slabs - 1
    total = None
    for head in range(0, half, 2):
        pair = jnp.concatenate(
            [gathered[:, head].reshape(reqs * drafts, lanes), gathered[:, head + 1].reshape(reqs * drafts, lanes)],
            -1,
        )
        start = pl.multiple_of((side * half + head) * lanes, 256)
        term = lax.dot_general(
            pair,
            out_proj_t[:, pl.ds(start, 2 * lanes)],
            (((1,), (1,)), ((), ())),
            preferred_element_type=F32,
        )
        total = term if total is None else total + term
    return total


def residual_rows(gathered, column_side, tiles):
    reqs, slabs, drafts, lanes = gathered.shape
    beside = gathered[:, slabs - 1].reshape(reqs * drafts, lanes)
    picked = []
    for tile in range(tiles):

        def source(i):
            return i // 2 * drafts + (i % 2 * 2 + column_side) * tiles + tile

        order = one_hot((reqs * 2, reqs * drafts), source)
        picked.append(jnp.dot(order, beside, preferred_element_type=F32))
    return jnp.concatenate(picked, -1).astype(BF16)


def project_other_kernel(gathered, other_t, swapped, out):
    tokens = gathered.shape[0] * gathered.shape[2]
    side = lax.axis_index("seq")
    width, padded = other_t.shape[0], out.shape[1]
    total = project_terms(gathered, other_t, side)
    total = jnp.concatenate([total, jnp.zeros((tokens, padded - width), F32)], -1)
    out[:tokens] = total.astype(BF16)
    out[tokens:] = residual_rows(gathered, 1 - side, padded // gathered.shape[3])


def project_own_kernel(gathered, out_proj_t, out):
    out[...] = project_terms(gathered, out_proj_t, lax.axis_index("seq"))


def project_sum_kernel(started, arrived, gathered, terms, residual):
    reqs, _, drafts, lanes = gathered.shape
    exps, _, padded = terms.shape
    width = started.shape[1]
    side = lax.axis_index("seq")
    tokens = reqs * drafts
    own_rows = drafts // (2 * exps)
    total = (started[...] + arrived[:tokens, :width].astype(F32)).astype(BF16)

    def source(i):
        exp, req = i // (tokens // exps), i // (2 * own_rows) % reqs
        seq, row = i // own_rows % 2, i % own_rows
        return ((req * 2 + seq) * exps + exp) * own_rows + row

    total = jnp.dot(one_hot((tokens, tokens), source), total, preferred_element_type=F32)
    total = jnp.concatenate([total, jnp.zeros((tokens, padded - width), F32)], -1)
    terms[...] = total.astype(BF16).reshape(terms.shape)
    picked = jnp.zeros(residual.shape, F32)
    for rows, from_side in (
        (residual_rows(gathered, side, padded // lanes), side),
        (arrived[tokens:], 1 - side),
    ):

        def residual_source(i):
            req, seq, row = i // (2 * own_rows), i // own_rows % 2, i % own_rows
            return jnp.where(seq == from_side, req * own_rows + row, -1)

        order = one_hot((residual.shape[0], rows.shape[0]), residual_source)
        picked += jnp.dot(order, rows, preferred_element_type=F32)
    residual[...] = picked.astype(BF16)


def hidden_kernel(terms, residual, fanned):
    attended = jnp.sum(terms[...].astype(F32), 0).astype(BF16)
    hidden = (residual[...].astype(F32) + attended.astype(F32)).astype(BF16)
    for dest in range(fanned.shape[0]):
        fanned[dest] = hidden


def expert_terms(rows, gains, w_gate, w_up, router_t, side):
    steps, tokens, _ = rows.shape
    width = gains.shape[1] // (2 * steps)
    gate = jnp.zeros((tokens, w_gate.shape[1]), F32)
    up = jnp.zeros((tokens, w_up.shape[1]), F32)
    logits = jnp.zeros((tokens, router_t.shape[0]), F32)
    squares = jnp.zeros((tokens, width), F32)

    def columns_of(a, i):
        low = a[:, i * 2 * width : (i * 2 + 1) * width].astype(F32)
        high = a[:, (i * 2 + 1) * width : (i * 2 + 2) * width].astype(F32)
        return jnp.where(side == 0, low, high)

    for i in range(steps):
        start = pl.multiple_of((i * 2 + side) * width, 32)
        hidden = rows[i][:, :width].astype(F32)
        scaled = (hidden * columns_of(gains, i)).astype(BF16)
        gate += jnp.dot(scaled, w_gate[pl.ds(start, width), :], preferred_element_type=F32)
        up += jnp.dot(scaled, w_up[pl.ds(start, width), :], preferred_element_type=F32)
        logits += lax.dot_general(
            scaled,
            columns_of(router_t, i).astype(BF16),
            (((1,), (1,)), ((), ())),
            preferred_element_type=F32,
        )
        squares += hidden * hidden
    return gate, up, logits, jnp.sum(squares, -1, keepdims=True)


def gate_up_own_kernel(own, gains, w_gate, w_up, router_t, gate, up, logits, squares):
    a, b, c, d = expert_terms(own, gains, w_gate, w_up, router_t, lax.axis_index("seq"))
    gate[...], up[...], logits[...] = a, b, c
    squares[...] = jnp.broadcast_to(d, squares.shape)


def gate_up_both_kernel(
    gate, up, logits, squares, own, other, gains, w_gate, w_up, router_t,
    act_mine, act_theirs, rows_here,
):
    side = lax.axis_index("seq")
    own_rows = rows_here.shape[1]
    place = (lax.axis_index("exp") * own.shape[0] + lax.axis_index("req")) * 2 + side
    place = place * own_rows
    around = pl.ds(pl.multiple_of(place // 16 * 16, 16), 16)
    near = lax.broadcasted_iota(jnp.int32, (16, own.shape[2]), 0)
    for rows, from_side in ((own, side), (other, 1 - side)):
        for i in range(own.shape[0]):
            tile = rows[i, around, :].astype(F32)
            picked = [
                jnp.sum(jnp.where(near == place % 16 + row, tile, 0.0), 0, keepdims=True)
                for row in range(own_rows)
            ]
            rows_here[i * 2 + from_side] = jnp.concatenate(picked, 0)
    width = gains.shape[1] // (2 * own.shape[0])
    experts = logits.shape[1]
    columns = gains.shape[1]
    a, b, c, d = expert_terms(other, gains, w_gate, w_up, router_t, 1 - side)
    scale = lax.rsqrt((squares[:, 0:1] + d) / columns + 1e-06)
    named = own[0, :, width : width + experts].astype(F32)
    chosen = named * jax.nn.sigmoid((logits[...] + c) * scale)
    mine = lax.broadcasted_iota(jnp.int32, chosen.shape, 1) == lax.axis_index("req")
    weight = jnp.sum(jnp.where(mine, chosen, 0.0), -1, keepdims=True)
    weight = weight / jnp.sum(chosen, -1, keepdims=True) * 2.5
    act = (jax.nn.silu((gate[...] + a) * scale) * ((up[...] + b) * scale) * weight).astype(BF16)
    tokens = act.shape[0]
    for out, seq in ((act_mine, side), (act_theirs, 1 - side)):

        def source(i):
            row, group = i // (tokens // (2 * own_rows)), i % (tokens // (2 * own_rows))
            return (group * 2 + seq) * own_rows + row

        order = one_hot((tokens // 2, tokens), source)
        out[...] = jnp.dot(order, act, preferred_element_type=F32).astype(BF16)


CHUNKS = 8


def down_kernel(act, act_other, w_down, w_down_other, out, rows_here):
    groups, rows, block = out.shape
    own_rows = rows // CHUNKS
    for chunk in range(CHUNKS):
        columns = slice(chunk * block, (chunk + 1) * block)
        total = jnp.dot(act[...], w_down[:, columns], preferred_element_type=F32)
        total += jnp.dot(act_other[...], w_down_other[:, columns], preferred_element_type=F32)
        for row in range(own_rows):
            for tile in range(block // 128):
                rows_here[tile, pl.ds(chunk * own_rows + row, groups, stride=rows), :] = total[
                    row * groups : (row + 1) * groups, tile * 128 : (tile + 1) * 128
                ]
    for tile in range(block // 128):
        out[:, :, tile * 128 : (tile + 1) * 128] = (
            rows_here[tile].reshape(groups, rows, 128).astype(BF16)
        )


def finish_kernel(pieces, hidden_rows, out):
    blocks, rows = hidden_rows.shape[0], out.shape[0]
    width = out.shape[1] // blocks
    total = jnp.sum(pieces[...].astype(F32), 0)
    total = jnp.concatenate([total[i * rows : (i + 1) * rows] for i in range(CHUNKS)], -1)
    hidden = jnp.concatenate([hidden_rows[block, :rows, :width] for block in range(blocks)], -1)
    out[...] = (hidden + total).astype(BF16)


def per_device(
    residual,
    queries,
    latent_cache,
    blocks,
    lengths,
    value_up,
    out_proj,
    norm_gain,
    router,
    expert_ids,
    w_gate,
    w_up,
    w_down,
):
    drafts, heads, qk_width = queries.shape[1:]
    n_req, n_exp = lax.axis_size("req"), lax.axis_size("exp")
    model_width = residual.shape[1]
    experts = router.shape[1]
    width = out_proj.shape[1]
    padded = -(-width // 128) * 128
    own_rows = residual.shape[0]
    tokens = n_req * drafts
    half_heads = heads // 2
    half_rows = drafts * half_heads
    shape = jax.ShapeDtypeStruct
    w_gate, w_up, w_down = w_gate[0], w_up[0], w_down[0]
    hidden_units = w_gate.shape[1]
    gains, router_t, out_proj_t = norm_gain.reshape(1, model_width), router.T, out_proj.T

    sent, kept, kept_stats, value_half = call(
        attend_kernel,
        (
            shape((half_rows, DL + 128), BF16),
            shape((half_rows, DL), F32),
            shape((half_rows, 256), F32),
            shape((half_heads,) + value_up.shape[1:], BF16),
        ),
        scalars=(lengths, blocks.reshape(-1)),
        outside=(queries[0], latent_cache[0], value_up),
        scratch=(
            pltpu.VMEM(queries.shape[1:], BF16),
            pltpu.VMEM((blocks.shape[2] * BLOCK, qk_width), BF16),
            pltpu.SemaphoreType.DMA((7,)),
        ),
    )
    arrived = swap(sent)
    other_t = swap(out_proj_t)
    w_down_other = swap(w_down)
    fanned = call(
        values_kernel,
        shape((n_req, half_heads + 1, drafts, DV), BF16),
        kept,
        kept_stats,
        arrived,
        value_half,
        residual,
        expert_ids,
    )
    gathered = lax.all_to_all(fanned, "req", split_axis=0, concat_axis=0, tiled=True)
    arrived = swap(
        call(
            project_other_kernel,
            shape((tokens + n_req * own_rows, padded), BF16),
            gathered,
            other_t,
            w_down_other,
        )
    )
    started = call(project_own_kernel, shape((tokens, width), F32), gathered, out_proj_t)
    terms, resid = call(
        project_sum_kernel,
        (
            shape((n_exp, tokens // n_exp, padded), BF16),
            shape((tokens // n_exp, padded), BF16),
        ),
        started,
        arrived,
        gathered,
    )
    terms = lax.all_to_all(terms, "exp", split_axis=0, concat_axis=0, tiled=True)
    fanned = call(
        hidden_kernel, shape((n_req * n_exp, tokens // n_exp, padded), BF16), terms, resid
    )
    own = lax.all_to_all(fanned, ("req", "exp"), split_axis=0, concat_axis=0, tiled=True)
    own = own.reshape(n_req, tokens, padded)
    other = swap(own)
    started = call(
        gate_up_own_kernel,
        (
            shape((tokens, hidden_units), F32),
            shape((tokens, hidden_units), F32),
            shape((tokens, experts), F32),
            shape((tokens, 128), F32),
        ),
        own,
        gains,
        w_gate,
        w_up,
        router_t,
    )
    act_mine, act_theirs, rows_here = call(
        gate_up_both_kernel,
        (
            shape((tokens // 2, hidden_units), BF16),
            shape((tokens // 2, hidden_units), BF16),
            shape((n_req * 2, own_rows, padded), F32),
        ),
        *started,
        own,
        other,
        gains,
        w_gate,
        w_up,
        router_t,
    )
    pieces = call(
        down_kernel,
        shape((n_req * n_exp, own_rows * CHUNKS, model_width // CHUNKS), BF16),
        act_mine,
        swap(act_theirs),
        w_down,
        w_down_other,
        scratch=(pltpu.VMEM((model_width // CHUNKS // 128, n_req * n_exp * own_rows * CHUNKS, 128), F32),),
    )
    pieces = lax.all_to_all(pieces, ("exp", "req"), split_axis=0, concat_axis=0, tiled=True)
    return call(finish_kernel, shape((own_rows, model_width), BF16), pieces, rows_here)


def solution(mesh):
    in_specs = (
        P(("req", "seq", "exp"), None),
        P("req", None, "exp", None),
        P("req", "seq", None),
        P("req", "seq", None),
        P("req"),
        P("exp", None, None),
        P("exp", ("req", "seq")),
        P(),
        P(),
        P(("req", "seq", "exp"), None),
        P("req", None, ("seq", "exp")),
        P("req", None, ("seq", "exp")),
        P("req", ("seq", "exp"), None),
    )
    out_specs = P(("req", "seq", "exp"), None)

    return jax.shard_map(per_device, mesh=mesh, in_specs=in_specs, out_specs=out_specs, check_vma=False)
```

```python
import jax
import jax.numpy as jnp
from jax import lax
from jax.experimental import pallas as pl
from jax.experimental.pallas import tpu as pltpu
from jax.sharding import PartitionSpec as P


DL = 512
DR = 64
DV = 128
BLOCK = 64
F32 = jnp.float32
BF16 = jnp.bfloat16
SWAP = [(0, 1), (1, 0)]


def swap(x):
    return lax.ppermute(x, "seq", SWAP)


def vmem():
    return pl.BlockSpec(memory_space=pltpu.VMEM)


def call(kernel, out_shape, *operands, scalars=(), outside=(), scratch=(), limit=24):
    many = isinstance(out_shape, (tuple, list))
    return pl.pallas_call(
        kernel,
        out_shape=out_shape,
        in_specs=[pl.BlockSpec(memory_space=pltpu.SMEM) for _ in scalars]
        + [pl.BlockSpec(memory_space=pltpu.HBM) for _ in outside]
        + [vmem() for _ in operands],
        out_specs=[vmem() for _ in out_shape] if many else vmem(),
        scratch_shapes=list(scratch),
        compiler_params=pltpu.CompilerParams(vmem_limit_bytes=limit * 2**20),
    )(*scalars, *[pltpu.with_memory_space_constraint(a, pltpu.HBM) for a in outside], *operands)


def one_hot(shape, source):
    rows = lax.broadcasted_iota(jnp.int32, shape, 0)
    columns = lax.broadcasted_iota(jnp.int32, shape, 1)
    return jnp.where(source(rows) == columns, 1.0, 0.0).astype(BF16)


def parts_of(a):
    first = a.astype(BF16)
    rest = a - first.astype(F32)
    second = rest.astype(BF16)
    return first, second, (rest - second.astype(F32)).astype(BF16)


def attend_kernel(
    lengths, blocks, queries, cache, value_up, sent, kept, kept_stats, value_half, query_rows, key_rows, sems
):
    drafts, heads, width = queries.shape
    side = lax.axis_index("seq")
    length, first, second = lengths[0], blocks[0], blocks[1]
    shard_len = cache.shape[0]
    copies = [
        pltpu.make_async_copy(
            cache.at[pl.ds(pl.multiple_of(first * BLOCK, BLOCK), BLOCK), :],
            key_rows.at[pl.ds(0, BLOCK), :],
            sems.at[0],
        ),
        pltpu.make_async_copy(
            cache.at[pl.ds(pl.multiple_of(second * BLOCK, BLOCK), BLOCK), :],
            key_rows.at[pl.ds(BLOCK, BLOCK), :],
            sems.at[1],
        ),
        pltpu.make_async_copy(queries, query_rows, sems.at[2]),
    ]
    quarter = heads // 8
    value_copies = [
        pltpu.make_async_copy(
            value_up.at[pl.ds(side * (heads // 2) + i * quarter, quarter)],
            value_half.at[pl.ds(i * quarter, quarter)],
            sems.at[3 + i],
        )
        for i in range(4)
    ]
    for place, copy in enumerate(copies):
        copy.start(priority=place // 2)
    for place, copy in enumerate(value_copies):
        copy.start(priority=place % 2)
    for copy in copies:
        copy.wait()
    keys = key_rows[...]
    rows = query_rows[...].reshape(drafts * heads, width)
    scores = lax.dot_general(
        rows, keys, (((1,), (1,)), ((), ())), preferred_element_type=F32
    ) * ((DV + DR) ** (-0.5))
    row = lax.broadcasted_iota(jnp.int32, scores.shape, 0)
    col = lax.broadcasted_iota(jnp.int32, scores.shape, 1)
    block = jnp.where(col < BLOCK, first, second - 1)
    usable = side * shard_len + block * BLOCK + col < length - (drafts - 1) + row // heads
    top = jnp.max(jnp.where(usable, scores, -1e30), -1, keepdims=True)
    probs = jnp.where(usable, jnp.exp(scores - top), 0.0).astype(BF16)
    total = jnp.sum(probs.astype(F32), -1, keepdims=True)
    out = jnp.dot(probs, keys[:, :DL], preferred_element_type=F32)
    half = heads // 2

    def split(a):
        a = a.reshape(drafts, 2, half, a.shape[-1])
        low = a[:, 0].reshape(drafts * half, a.shape[-1])
        high = a[:, 1].reshape(drafts * half, a.shape[-1])
        return jnp.where(side == 0, low, high), jnp.where(side == 0, high, low)

    mine, theirs = split(out)
    stats = jnp.concatenate(
        [jnp.broadcast_to(top, (top.shape[0], 128)), jnp.broadcast_to(total, (top.shape[0], 128))],
        -1,
    )
    my_stats, their_stats = split(stats)
    kept[...] = mine
    kept_stats[...] = my_stats
    sent[:, :DL] = theirs.astype(BF16)
    top_parts, sum_parts = parts_of(their_stats[:, :128]), parts_of(their_stats[:, 128:])
    lane = lax.broadcasted_iota(jnp.int32, (drafts * half, 128), 1)
    packed = jnp.zeros((drafts * half, 128), F32)
    for place, part in enumerate(top_parts + sum_parts):
        packed = jnp.where(lane == place, part.astype(F32), packed)
    sent[:, DL:] = packed.astype(BF16)
    for copy in value_copies:
        copy.wait()


def values_kernel(kept, kept_stats, arrived, value_up, residual, expert_ids, fanned):
    rows = kept.shape[0]
    dests, slabs, drafts, _ = fanned.shape
    half = slabs - 1
    packed = arrived[:, DL:].astype(F32)
    lane = lax.broadcasted_iota(jnp.int32, packed.shape, 1)
    other_top = jnp.sum(jnp.where(lane < 3, packed, 0.0), -1, keepdims=True)
    other_sum = jnp.sum(jnp.where((lane >= 3) & (lane < 6), packed, 0.0), -1, keepdims=True)
    my_top, my_sum = kept_stats[:, 0:1], kept_stats[:, 128:129]
    top = jnp.maximum(my_top, other_top)
    my_scale, other_scale = jnp.exp(my_top - top), jnp.exp(other_top - top)
    total = my_scale * my_sum + other_scale * other_sum
    latent = (my_scale / total) * kept[...] + (other_scale / total) * arrived[:, :DL].astype(F32)
    latent = latent.astype(BF16)
    order = one_hot((rows, rows), lambda i: i % drafts * half + i // drafts)
    latent = jnp.dot(order, latent, preferred_element_type=F32).astype(BF16)
    for head in range(half):
        out = jnp.dot(
            latent[head * drafts : (head + 1) * drafts],
            value_up[head],
            preferred_element_type=F32,
        ).astype(BF16)
        for dest in range(dests):
            fanned[dest, head] = out
    own_rows, model_width = residual.shape
    width = model_width // (2 * dests)
    lane = lax.broadcasted_iota(jnp.int32, (own_rows, 128), 1)
    named = jnp.zeros((own_rows, 128), F32)
    for k in range(expert_ids.shape[1]):
        named += jnp.where(expert_ids[:, k : k + 1] + (width - 128) == lane, 1.0, 0.0)
    values = residual[...].astype(F32)
    values = jnp.concatenate([values, jnp.zeros((own_rows, 128), F32)], -1)
    for dest in range(dests):
        pieces = []
        for row in range(own_rows):
            for core in range(2):
                start = (dest * 2 + core) * width
                pieces.append(values[row : row + 1, start : start + 128])
                tail = values[row : row + 1, start + 128 : start + 256]
                pieces.append(jnp.where(lane[:1] < width - 128, tail, named[row : row + 1]))
        pieces.append(jnp.zeros((drafts - len(pieces), 128), F32))
        fanned[dest, half] = jnp.concatenate(pieces, 0).astype(BF16)


def project_terms(gathered, out_proj_t, side):
    reqs, slabs, drafts, lanes = gathered.shape
    half = slabs - 1
    total = None
    for head in range(0, half, 2):
        pair = jnp.concatenate(
            [gathered[:, head].reshape(reqs * drafts, lanes), gathered[:, head + 1].reshape(reqs * drafts, lanes)],
            -1,
        )
        start = pl.multiple_of((side * half + head) * lanes, 256)
        term = lax.dot_general(
            pair,
            out_proj_t[:, pl.ds(start, 2 * lanes)],
            (((1,), (1,)), ((), ())),
            preferred_element_type=F32,
        )
        total = term if total is None else total + term
    return total


def residual_rows(gathered, column_side, tiles):
    reqs, slabs, drafts, lanes = gathered.shape
    beside = gathered[:, slabs - 1].reshape(reqs * drafts, lanes)
    picked = []
    for tile in range(tiles):

        def source(i):
            return i // 2 * drafts + (i % 2 * 2 + column_side) * tiles + tile

        order = one_hot((reqs * 2, reqs * drafts), source)
        picked.append(jnp.dot(order, beside, preferred_element_type=F32))
    return jnp.concatenate(picked, -1).astype(BF16)


def project_other_kernel(gathered, other_t, swapped, out):
    tokens = gathered.shape[0] * gathered.shape[2]
    side = lax.axis_index("seq")
    width, padded = other_t.shape[0], out.shape[1]
    total = project_terms(gathered, other_t, side)
    total = jnp.concatenate([total, jnp.zeros((tokens, padded - width), F32)], -1)
    out[:tokens] = total.astype(BF16)
    out[tokens:] = residual_rows(gathered, 1 - side, padded // gathered.shape[3])


def project_own_kernel(gathered, out_proj_t, out):
    out[...] = project_terms(gathered, out_proj_t, lax.axis_index("seq"))


def project_sum_kernel(started, arrived, gathered, fanned):
    reqs, _, drafts, lanes = gathered.shape
    exps, tokens, padded = fanned.shape
    width = started.shape[1]
    side, exp = lax.axis_index("seq"), lax.axis_index("exp")
    own_rows = drafts // (2 * exps)
    total = (started[...] + arrived[:tokens, :width].astype(F32)).astype(BF16)

    def parts(i):
        token_exp, req = i // (tokens // exps), i // (2 * own_rows) % reqs
        return token_exp, req, i // own_rows % 2, i % own_rows

    def source(i):
        token_exp, req, seq, row = parts(i)
        return ((req * 2 + seq) * exps + token_exp) * own_rows + row

    total = jnp.dot(one_hot((tokens, tokens), source), total, preferred_element_type=F32)
    total = jnp.concatenate([total, jnp.zeros((tokens, padded - width), F32)], -1)
    for rows, from_side in (
        (residual_rows(gathered, side, padded // lanes), side),
        (arrived[tokens:], 1 - side),
    ):

        def residual_source(i):
            token_exp, req, seq, row = parts(i)
            return jnp.where((seq == from_side) & (token_exp == exp), req * own_rows + row, -1)

        order = one_hot((tokens, rows.shape[0]), residual_source)
        total += jnp.dot(order, rows, preferred_element_type=F32)
    total = total.astype(BF16)
    for dest in range(exps):
        fanned[dest] = total


def hidden_kernel(terms, fanned):
    hidden = jnp.sum(terms[...].astype(F32), 0).astype(BF16)
    for dest in range(fanned.shape[0]):
        fanned[dest] = hidden


def expert_terms(rows, gains, w_gate, w_up, router_t, side):
    steps, tokens, _ = rows.shape
    width = gains.shape[1] // (2 * steps)
    gate = jnp.zeros((tokens, w_gate.shape[1]), F32)
    up = jnp.zeros((tokens, w_up.shape[1]), F32)
    logits = jnp.zeros((tokens, router_t.shape[0]), F32)
    squares = jnp.zeros((tokens, width), F32)

    def columns_of(a, i):
        low = a[:, i * 2 * width : (i * 2 + 1) * width].astype(F32)
        high = a[:, (i * 2 + 1) * width : (i * 2 + 2) * width].astype(F32)
        return jnp.where(side == 0, low, high)

    for i in range(steps):
        start = pl.multiple_of((i * 2 + side) * width, 32)
        hidden = rows[i][:, :width].astype(F32)
        scaled = (hidden * columns_of(gains, i)).astype(BF16)
        gate += jnp.dot(scaled, w_gate[pl.ds(start, width), :], preferred_element_type=F32)
        up += jnp.dot(scaled, w_up[pl.ds(start, width), :], preferred_element_type=F32)
        logits += lax.dot_general(
            scaled,
            columns_of(router_t, i).astype(BF16),
            (((1,), (1,)), ((), ())),
            preferred_element_type=F32,
        )
        squares += hidden * hidden
    return gate, up, logits, jnp.sum(squares, -1, keepdims=True)


def gate_up_own_kernel(own, gains, w_gate, w_up, router_t, gate, up, logits, squares):
    a, b, c, d = expert_terms(own, gains, w_gate, w_up, router_t, lax.axis_index("seq"))
    gate[...], up[...], logits[...] = a, b, c
    squares[...] = jnp.broadcast_to(d, squares.shape)


def gate_up_both_kernel(
    gate, up, logits, squares, own, other, gains, w_gate, w_up, router_t,
    act_mine, act_theirs, rows_here,
):
    side = lax.axis_index("seq")
    own_rows = rows_here.shape[1]
    place = (lax.axis_index("exp") * own.shape[0] + lax.axis_index("req")) * 2 + side
    place = place * own_rows
    around = pl.ds(pl.multiple_of(place // 16 * 16, 16), 16)
    near = lax.broadcasted_iota(jnp.int32, (16, own.shape[2]), 0)
    for rows, from_side in ((own, side), (other, 1 - side)):
        for i in range(own.shape[0]):
            tile = rows[i, around, :].astype(F32)
            picked = [
                jnp.sum(jnp.where(near == place % 16 + row, tile, 0.0), 0, keepdims=True)
                for row in range(own_rows)
            ]
            rows_here[i * 2 + from_side] = jnp.concatenate(picked, 0)
    width = gains.shape[1] // (2 * own.shape[0])
    experts = logits.shape[1]
    columns = gains.shape[1]
    a, b, c, d = expert_terms(other, gains, w_gate, w_up, router_t, 1 - side)
    scale = lax.rsqrt((squares[:, 0:1] + d) / columns + 1e-06)
    named = own[0, :, width : width + experts].astype(F32)
    chosen = named * jax.nn.sigmoid((logits[...] + c) * scale)
    mine = lax.broadcasted_iota(jnp.int32, chosen.shape, 1) == lax.axis_index("req")
    weight = jnp.sum(jnp.where(mine, chosen, 0.0), -1, keepdims=True)
    weight = weight / jnp.sum(chosen, -1, keepdims=True) * 2.5
    act = (jax.nn.silu((gate[...] + a) * scale) * ((up[...] + b) * scale) * weight).astype(BF16)
    tokens = act.shape[0]
    for out, seq in ((act_mine, side), (act_theirs, 1 - side)):

        def source(i):
            row, group = i // (tokens // (2 * own_rows)), i % (tokens // (2 * own_rows))
            return (group * 2 + seq) * own_rows + row

        order = one_hot((tokens // 2, tokens), source)
        out[...] = jnp.dot(order, act, preferred_element_type=F32).astype(BF16)


CHUNKS = 8


def down_kernel(act, act_other, w_down, w_down_other, out, rows_here):
    groups, rows, block = out.shape
    own_rows = rows // CHUNKS
    for chunk in range(CHUNKS):
        columns = slice(chunk * block, (chunk + 1) * block)
        total = jnp.dot(act[...], w_down[:, columns], preferred_element_type=F32)
        total += jnp.dot(act_other[...], w_down_other[:, columns], preferred_element_type=F32)
        for row in range(own_rows):
            for tile in range(block // 128):
                rows_here[tile, pl.ds(chunk * own_rows + row, groups, stride=rows), :] = total[
                    row * groups : (row + 1) * groups, tile * 128 : (tile + 1) * 128
                ]
    for tile in range(block // 128):
        out[:, :, tile * 128 : (tile + 1) * 128] = (
            rows_here[tile].reshape(groups, rows, 128).astype(BF16)
        )


def finish_kernel(pieces, hidden_rows, out):
    blocks, rows = hidden_rows.shape[0], out.shape[0]
    width = out.shape[1] // blocks
    total = jnp.sum(pieces[...].astype(F32), 0)
    total = jnp.concatenate([total[i * rows : (i + 1) * rows] for i in range(CHUNKS)], -1)
    hidden = jnp.concatenate([hidden_rows[block, :rows, :width] for block in range(blocks)], -1)
    out[...] = (hidden + total).astype(BF16)


def per_device(
    residual,
    queries,
    latent_cache,
    blocks,
    lengths,
    value_up,
    out_proj,
    norm_gain,
    router,
    expert_ids,
    w_gate,
    w_up,
    w_down,
):
    drafts, heads, qk_width = queries.shape[1:]
    n_req, n_exp = lax.axis_size("req"), lax.axis_size("exp")
    model_width = residual.shape[1]
    experts = router.shape[1]
    width = out_proj.shape[1]
    padded = -(-width // 128) * 128
    own_rows = residual.shape[0]
    tokens = n_req * drafts
    half_heads = heads // 2
    half_rows = drafts * half_heads
    shape = jax.ShapeDtypeStruct
    w_gate, w_up, w_down = w_gate[0], w_up[0], w_down[0]
    hidden_units = w_gate.shape[1]
    gains, router_t, out_proj_t = norm_gain.reshape(1, model_width), router.T, out_proj.T

    sent, kept, kept_stats, value_half = call(
        attend_kernel,
        (
            shape((half_rows, DL + 128), BF16),
            shape((half_rows, DL), F32),
            shape((half_rows, 256), F32),
            shape((half_heads,) + value_up.shape[1:], BF16),
        ),
        scalars=(lengths, blocks.reshape(-1)),
        outside=(queries[0], latent_cache[0], value_up),
        scratch=(
            pltpu.VMEM(queries.shape[1:], BF16),
            pltpu.VMEM((blocks.shape[2] * BLOCK, qk_width), BF16),
            pltpu.SemaphoreType.DMA((7,)),
        ),
    )
    arrived = swap(sent)
    other_t = swap(out_proj_t)
    w_down_other = swap(w_down)
    fanned = call(
        values_kernel,
        shape((n_req, half_heads + 1, drafts, DV), BF16),
        kept,
        kept_stats,
        arrived,
        value_half,
        residual,
        expert_ids,
    )
    gathered = lax.all_to_all(fanned, "req", split_axis=0, concat_axis=0, tiled=True)
    arrived = swap(
        call(
            project_other_kernel,
            shape((tokens + n_req * own_rows, padded), BF16),
            gathered,
            other_t,
            w_down_other,
        )
    )
    started = call(project_own_kernel, shape((tokens, width), F32), gathered, out_proj_t)
    terms = call(
        project_sum_kernel, shape((n_exp, tokens, padded), BF16), started, arrived, gathered
    )
    terms = lax.all_to_all(terms, "exp", split_axis=0, concat_axis=0, tiled=True)
    fanned = call(hidden_kernel, shape((n_req, tokens, padded), BF16), terms)
    own = lax.all_to_all(fanned, "req", split_axis=0, concat_axis=0, tiled=True)
    other = swap(own)
    started = call(
        gate_up_own_kernel,
        (
            shape((tokens, hidden_units), F32),
            shape((tokens, hidden_units), F32),
            shape((tokens, experts), F32),
            shape((tokens, 128), F32),
        ),
        own,
        gains,
        w_gate,
        w_up,
        router_t,
    )
    act_mine, act_theirs, rows_here = call(
        gate_up_both_kernel,
        (
            shape((tokens // 2, hidden_units), BF16),
            shape((tokens // 2, hidden_units), BF16),
            shape((n_req * 2, own_rows, padded), F32),
        ),
        *started,
        own,
        other,
        gains,
        w_gate,
        w_up,
        router_t,
    )
    pieces = call(
        down_kernel,
        shape((n_req * n_exp, own_rows * CHUNKS, model_width // CHUNKS), BF16),
        act_mine,
        swap(act_theirs),
        w_down,
        w_down_other,
        scratch=(pltpu.VMEM((model_width // CHUNKS // 128, n_req * n_exp * own_rows * CHUNKS, 128), F32),),
    )
    pieces = lax.all_to_all(pieces, ("exp", "req"), split_axis=0, concat_axis=0, tiled=True)
    return call(finish_kernel, shape((own_rows, model_width), BF16), pieces, rows_here)


def solution(mesh):
    in_specs = (
        P(("req", "seq", "exp"), None),
        P("req", None, "exp", None),
        P("req", "seq", None),
        P("req", "seq", None),
        P("req"),
        P("exp", None, None),
        P("exp", ("req", "seq")),
        P(),
        P(),
        P(("req", "seq", "exp"), None),
        P("req", None, ("seq", "exp")),
        P("req", None, ("seq", "exp")),
        P("req", ("seq", "exp"), None),
    )
    out_specs = P(("req", "seq", "exp"), None)

    return jax.shard_map(per_device, mesh=mesh, in_specs=in_specs, out_specs=out_specs, check_vma=False)
```

```python
import jax
import jax.numpy as jnp
from jax import lax
from jax.experimental import pallas as pl
from jax.experimental.pallas import tpu as pltpu
from jax.sharding import PartitionSpec as P


DL = 512
DR = 64
DV = 128
BLOCK = 64
F32 = jnp.float32
BF16 = jnp.bfloat16
SWAP = [(0, 1), (1, 0)]
PACK = 4


def swap(x):
    return lax.ppermute(x, "seq", SWAP)


def vmem():
    return pl.BlockSpec(memory_space=pltpu.VMEM)


def call(kernel, out_shape, *operands, scalars=(), outside=(), scratch=(), limit=24):
    many = isinstance(out_shape, (tuple, list))
    return pl.pallas_call(
        kernel,
        out_shape=out_shape,
        in_specs=[pl.BlockSpec(memory_space=pltpu.SMEM) for _ in scalars]
        + [pl.BlockSpec(memory_space=pltpu.HBM) for _ in outside]
        + [vmem() for _ in operands],
        out_specs=[vmem() for _ in out_shape] if many else vmem(),
        scratch_shapes=list(scratch),
        compiler_params=pltpu.CompilerParams(vmem_limit_bytes=limit * 2**20),
    )(*scalars, *[pltpu.with_memory_space_constraint(a, pltpu.HBM) for a in outside], *operands)


def one_hot(shape, source):
    rows = lax.broadcasted_iota(jnp.int32, shape, 0)
    columns = lax.broadcasted_iota(jnp.int32, shape, 1)
    return jnp.where(source(rows) == columns, 1.0, 0.0).astype(BF16)


def parts_of(a):
    first = a.astype(BF16)
    rest = a - first.astype(F32)
    second = rest.astype(BF16)
    return first, second, (rest - second.astype(F32)).astype(BF16)


def attend_kernel(
    lengths, blocks, queries, cache, value_up, sent, kept, kept_stats, value_half, query_rows, key_rows, sems
):
    drafts, heads, width = queries.shape
    side = lax.axis_index("seq")
    length, first, second = lengths[0], blocks[0], blocks[1]
    shard_len = cache.shape[0]
    copies = [
        pltpu.make_async_copy(
            cache.at[pl.ds(pl.multiple_of(first * BLOCK, BLOCK), BLOCK), :],
            key_rows.at[pl.ds(0, BLOCK), :],
            sems.at[0],
        ),
        pltpu.make_async_copy(
            cache.at[pl.ds(pl.multiple_of(second * BLOCK, BLOCK), BLOCK), :],
            key_rows.at[pl.ds(BLOCK, BLOCK), :],
            sems.at[1],
        ),
        pltpu.make_async_copy(queries, query_rows, sems.at[2]),
    ]
    quarter = heads // 8
    value_copies = [
        pltpu.make_async_copy(
            value_up.at[pl.ds(side * (heads // 2) + i * quarter, quarter)],
            value_half.at[pl.ds(i * quarter, quarter)],
            sems.at[3 + i],
        )
        for i in range(4)
    ]
    for place, copy in enumerate(copies):
        copy.start(priority=place // 2)
    for place, copy in enumerate(value_copies):
        copy.start(priority=place % 2)
    for copy in copies:
        copy.wait()
    keys = key_rows[...]
    rows = query_rows[...].reshape(drafts * heads, width)
    scores = lax.dot_general(
        rows, keys, (((1,), (1,)), ((), ())), preferred_element_type=F32
    ) * ((DV + DR) ** (-0.5))
    row = lax.broadcasted_iota(jnp.int32, scores.shape, 0)
    col = lax.broadcasted_iota(jnp.int32, scores.shape, 1)
    block = jnp.where(col < BLOCK, first, second - 1)
    usable = side * shard_len + block * BLOCK + col < length - (drafts - 1) + row // heads
    top = jnp.max(jnp.where(usable, scores, -1e30), -1, keepdims=True)
    probs = jnp.where(usable, jnp.exp(scores - top), 0.0).astype(BF16)
    total = jnp.sum(probs.astype(F32), -1, keepdims=True)
    out = jnp.dot(probs, keys[:, :DL], preferred_element_type=F32)
    half = heads // 2

    def split(a):
        a = a.reshape(drafts, 2, half, a.shape[-1])
        low = a[:, 0].reshape(drafts * half, a.shape[-1])
        high = a[:, 1].reshape(drafts * half, a.shape[-1])
        return jnp.where(side == 0, low, high), jnp.where(side == 0, high, low)

    mine, theirs = split(out)
    stats = jnp.concatenate(
        [jnp.broadcast_to(top, (top.shape[0], 128)), jnp.broadcast_to(total, (top.shape[0], 128))],
        -1,
    )
    my_stats, their_stats = split(stats)
    kept[...] = mine
    kept_stats[...] = my_stats
    sent[:, :DL] = theirs.astype(BF16)
    top_parts, sum_parts = parts_of(their_stats[:, :128]), parts_of(their_stats[:, 128:])
    lane = lax.broadcasted_iota(jnp.int32, (drafts * half, 128), 1)
    packed = jnp.zeros((drafts * half, 128), F32)
    for place, part in enumerate(top_parts + sum_parts):
        packed = jnp.where(lane == place, part.astype(F32), packed)
    sent[:, DL:] = packed.astype(BF16)
    for copy in value_copies:
        copy.wait()


def values_kernel(kept, kept_stats, arrived, value_up, residual, expert_ids, fanned):
    rows = kept.shape[0]
    dests, slabs, drafts, _ = fanned.shape
    half = slabs - 1
    packed = arrived[:, DL:].astype(F32)
    lane = lax.broadcasted_iota(jnp.int32, packed.shape, 1)
    other_top = jnp.sum(jnp.where(lane < 3, packed, 0.0), -1, keepdims=True)
    other_sum = jnp.sum(jnp.where((lane >= 3) & (lane < 6), packed, 0.0), -1, keepdims=True)
    my_top, my_sum = kept_stats[:, 0:1], kept_stats[:, 128:129]
    top = jnp.maximum(my_top, other_top)
    my_scale, other_scale = jnp.exp(my_top - top), jnp.exp(other_top - top)
    total = my_scale * my_sum + other_scale * other_sum
    latent = (my_scale / total) * kept[...] + (other_scale / total) * arrived[:, :DL].astype(F32)
    latent = latent.astype(BF16)
    order = one_hot((rows, rows), lambda i: i % drafts * half + i // drafts)
    latent = jnp.dot(order, latent, preferred_element_type=F32).astype(BF16)
    for head in range(half):
        out = jnp.dot(
            latent[head * drafts : (head + 1) * drafts],
            value_up[head],
            preferred_element_type=F32,
        ).astype(BF16)
        for dest in range(dests):
            fanned[dest, head] = out
    own_rows, model_width = residual.shape
    width = model_width // (2 * dests)
    lane = lax.broadcasted_iota(jnp.int32, (own_rows, 128), 1)
    named = jnp.zeros((own_rows, 128), F32)
    for k in range(expert_ids.shape[1]):
        named += jnp.where(expert_ids[:, k : k + 1] + (width - 128) == lane, 1.0, 0.0)
    values = residual[...].astype(F32)
    values = jnp.concatenate([values, jnp.zeros((own_rows, 128), F32)], -1)
    for dest in range(dests):
        pieces = []
        for row in range(own_rows):
            for core in range(2):
                start = (dest * 2 + core) * width
                pieces.append(values[row : row + 1, start : start + 128])
                tail = values[row : row + 1, start + 128 : start + 256]
                pieces.append(jnp.where(lane[:1] < width - 128, tail, named[row : row + 1]))
        pieces.append(jnp.zeros((drafts - len(pieces), 128), F32))
        fanned[dest, half] = jnp.concatenate(pieces, 0).astype(BF16)


def project_terms(gathered, out_proj_t, side):
    reqs, slabs, drafts, lanes = gathered.shape
    half = slabs - 1
    total = None
    for head in range(0, half, 2):
        pair = jnp.concatenate(
            [gathered[:, head].reshape(reqs * drafts, lanes), gathered[:, head + 1].reshape(reqs * drafts, lanes)],
            -1,
        )
        start = pl.multiple_of((side * half + head) * lanes, 256)
        term = lax.dot_general(
            pair,
            out_proj_t[:, pl.ds(start, 2 * lanes)],
            (((1,), (1,)), ((), ())),
            preferred_element_type=F32,
        )
        total = term if total is None else total + term
    return total


def residual_rows(gathered, column_side, tiles):
    reqs, slabs, drafts, lanes = gathered.shape
    beside = gathered[:, slabs - 1].reshape(reqs * drafts, lanes)
    picked = []
    for tile in range(tiles):

        def source(i):
            return i // 2 * drafts + (i % 2 * 2 + column_side) * tiles + tile

        order = one_hot((reqs * 2, reqs * drafts), source)
        picked.append(jnp.dot(order, beside, preferred_element_type=F32))
    return jnp.concatenate(picked, -1).astype(BF16)


def project_other_kernel(gathered, other_t, swapped, out):
    tokens = gathered.shape[0] * gathered.shape[2]
    side = lax.axis_index("seq")
    width, padded = other_t.shape[0], out.shape[1]
    total = project_terms(gathered, other_t, side)
    total = jnp.concatenate([total, jnp.zeros((tokens, padded - width), F32)], -1)
    out[:tokens] = total.astype(BF16)
    out[tokens:] = residual_rows(gathered, 1 - side, padded // gathered.shape[3])


def project_own_kernel(gathered, out_proj_t, out):
    out[...] = project_terms(gathered, out_proj_t, lax.axis_index("seq"))


def project_sum_kernel(started, arrived, gathered, terms, residual):
    reqs, _, drafts, lanes = gathered.shape
    exps, _, padded = terms.shape
    width = started.shape[1]
    side = lax.axis_index("seq")
    tokens = reqs * drafts
    own_rows = drafts // (2 * exps)
    total = (started[...] + arrived[:tokens, :width].astype(F32)).astype(BF16)

    def source(i):
        exp, req = i // (tokens // exps), i // (2 * own_rows) % reqs
        seq, row = i // own_rows % 2, i % own_rows
        return ((req * 2 + seq) * exps + exp) * own_rows + row

    total = jnp.dot(one_hot((tokens, tokens), source), total, preferred_element_type=F32)
    total = jnp.concatenate([total, jnp.zeros((tokens, padded - width), F32)], -1)
    picked = jnp.zeros(residual.shape, F32)
    for rows, from_side in (
        (residual_rows(gathered, side, padded // lanes), side),
        (arrived[tokens:], 1 - side),
    ):

        def residual_source(i):
            req, seq, row = i // (2 * own_rows), i // own_rows % 2, i % own_rows
            return jnp.where(seq == from_side, req * own_rows + row, -1)

        order = one_hot((residual.shape[0], rows.shape[0]), residual_source)
        picked += jnp.dot(order, rows, preferred_element_type=F32)
    residual[...] = picked.astype(BF16)
    lane = lax.broadcasted_iota(jnp.int32, residual.shape, 1)
    named = jnp.where(lane < width, 0.0, picked)
    for dest in range(exps):
        rows = total[dest * residual.shape[0] : (dest + 1) * residual.shape[0]]
        terms[dest] = (rows + named).astype(BF16)


def hidden_kernel(terms, residual, fanned):
    attended = jnp.sum(terms[...].astype(F32), 0).astype(BF16)
    hidden = residual[...].astype(F32) + attended.astype(F32)
    rows, width = fanned.shape[1], fanned.shape[2] // PACK
    packed = jnp.concatenate(
        [hidden[i * rows : (i + 1) * rows, :width] for i in range(PACK)], -1
    ).astype(BF16)
    for dest in range(fanned.shape[0]):
        fanned[dest] = packed


def unpacked(rows, i, width):
    exps = rows.shape[1]
    pieces = []
    for exp in range(exps):
        tile = rows[i, exp].astype(F32)
        pieces += [tile[:, j * width : (j + 1) * width] for j in range(PACK)]
    return jnp.concatenate(pieces, 0)


def expert_terms(rows, gains, w_gate, w_up, router_t, side):
    steps, exps, packed_rows, _ = rows.shape
    tokens = exps * packed_rows * PACK
    width = gains.shape[1] // (2 * steps)
    gate = jnp.zeros((tokens, w_gate.shape[1]), F32)
    up = jnp.zeros((tokens, w_up.shape[1]), F32)
    logits = jnp.zeros((tokens, router_t.shape[0]), F32)
    squares = jnp.zeros((tokens, width), F32)

    def columns_of(a, i):
        low = a[:, i * 2 * width : (i * 2 + 1) * width].astype(F32)
        high = a[:, (i * 2 + 1) * width : (i * 2 + 2) * width].astype(F32)
        return jnp.where(side == 0, low, high)

    for i in range(steps):
        start = pl.multiple_of((i * 2 + side) * width, 32)
        hidden = unpacked(rows, i, width)
        scaled = (hidden * columns_of(gains, i)).astype(BF16)
        gate += jnp.dot(scaled, w_gate[pl.ds(start, width), :], preferred_element_type=F32)
        up += jnp.dot(scaled, w_up[pl.ds(start, width), :], preferred_element_type=F32)
        logits += lax.dot_general(
            scaled,
            columns_of(router_t, i).astype(BF16),
            (((1,), (1,)), ((), ())),
            preferred_element_type=F32,
        )
        squares += hidden * hidden
    return gate, up, logits, jnp.sum(squares, -1, keepdims=True)


def gate_up_own_kernel(own, gains, w_gate, w_up, router_t, gate, up, logits, squares):
    a, b, c, d = expert_terms(own, gains, w_gate, w_up, router_t, lax.axis_index("seq"))
    gate[...], up[...], logits[...] = a, b, c
    squares[...] = jnp.broadcast_to(d, squares.shape)


def gate_up_both_kernel(
    gate, up, logits, squares, own, other, terms, gains, w_gate, w_up, router_t,
    act_mine, act_theirs, rows_here,
):
    side = lax.axis_index("seq")
    own_rows = rows_here.shape[1]
    exp, req = lax.axis_index("exp"), lax.axis_index("req")
    packed_rows = own.shape[2]
    place = (req * 2 + side) * own_rows
    group, first = place // packed_rows, place % packed_rows
    part = rows_here.shape[2]
    near = lax.broadcasted_iota(jnp.int32, own.shape[2:], 0)
    for rows, from_side in ((own, side), (other, 1 - side)):
        for i in range(own.shape[0]):
            tile = rows[i, exp].astype(F32)
            for row in range(own_rows):
                line = jnp.sum(jnp.where(near == first + row, tile, 0.0), 0, keepdims=True)
                picked = line[:, :part]
                for j in range(1, PACK):
                    picked = jnp.where(group == j, line[:, j * part : (j + 1) * part], picked)
                rows_here[i * 2 + from_side, row : row + 1, :] = picked
    width = gains.shape[1] // (2 * own.shape[0])
    experts = logits.shape[1]
    columns = gains.shape[1]
    a, b, c, d = expert_terms(other, gains, w_gate, w_up, router_t, 1 - side)
    scale = lax.rsqrt((squares[:, 0:1] + d) / columns + 1e-06)
    tokens = gate.shape[0]
    named = terms[...].reshape(tokens, terms.shape[2])[:, width : width + experts].astype(F32)
    chosen = named * jax.nn.sigmoid((logits[...] + c) * scale)
    mine = lax.broadcasted_iota(jnp.int32, chosen.shape, 1) == lax.axis_index("req")
    weight = jnp.sum(jnp.where(mine, chosen, 0.0), -1, keepdims=True)
    weight = weight / jnp.sum(chosen, -1, keepdims=True) * 2.5
    act = (jax.nn.silu((gate[...] + a) * scale) * ((up[...] + b) * scale) * weight).astype(BF16)
    tokens = act.shape[0]
    for out, seq in ((act_mine, side), (act_theirs, 1 - side)):

        def source(i):
            row, group = i // (tokens // (2 * own_rows)), i % (tokens // (2 * own_rows))
            return (group * 2 + seq) * own_rows + row

        order = one_hot((tokens // 2, tokens), source)
        out[...] = jnp.dot(order, act, preferred_element_type=F32).astype(BF16)


CHUNKS = 8


def down_kernel(act, act_other, w_down, w_down_other, out, rows_here):
    groups, rows, block = out.shape
    own_rows = rows // CHUNKS
    for chunk in range(CHUNKS):
        columns = slice(chunk * block, (chunk + 1) * block)
        total = jnp.dot(act[...], w_down[:, columns], preferred_element_type=F32)
        total += jnp.dot(act_other[...], w_down_other[:, columns], preferred_element_type=F32)
        for row in range(own_rows):
            for tile in range(block // 128):
                rows_here[tile, pl.ds(chunk * own_rows + row, groups, stride=rows), :] = total[
                    row * groups : (row + 1) * groups, tile * 128 : (tile + 1) * 128
                ]
    for tile in range(block // 128):
        out[:, :, tile * 128 : (tile + 1) * 128] = (
            rows_here[tile].reshape(groups, rows, 128).astype(BF16)
        )


def finish_kernel(pieces, hidden_rows, out):
    blocks, rows = hidden_rows.shape[0], out.shape[0]
    width = out.shape[1] // blocks
    total = jnp.sum(pieces[...].astype(F32), 0)
    total = jnp.concatenate([total[i * rows : (i + 1) * rows] for i in range(CHUNKS)], -1)
    hidden = jnp.concatenate([hidden_rows[block, :rows, :width] for block in range(blocks)], -1)
    out[...] = (hidden + total).astype(BF16)


def per_device(
    residual,
    queries,
    latent_cache,
    blocks,
    lengths,
    value_up,
    out_proj,
    norm_gain,
    router,
    expert_ids,
    w_gate,
    w_up,
    w_down,
):
    drafts, heads, qk_width = queries.shape[1:]
    n_req, n_exp = lax.axis_size("req"), lax.axis_size("exp")
    model_width = residual.shape[1]
    experts = router.shape[1]
    width = out_proj.shape[1]
    padded = -(-width // 128) * 128
    own_rows = residual.shape[0]
    tokens = n_req * drafts
    half_heads = heads // 2
    half_rows = drafts * half_heads
    shape = jax.ShapeDtypeStruct
    w_gate, w_up, w_down = w_gate[0], w_up[0], w_down[0]
    hidden_units = w_gate.shape[1]
    gains, router_t, out_proj_t = norm_gain.reshape(1, model_width), router.T, out_proj.T

    sent, kept, kept_stats, value_half = call(
        attend_kernel,
        (
            shape((half_rows, DL + 128), BF16),
            shape((half_rows, DL), F32),
            shape((half_rows, 256), F32),
            shape((half_heads,) + value_up.shape[1:], BF16),
        ),
        scalars=(lengths, blocks.reshape(-1)),
        outside=(queries[0], latent_cache[0], value_up),
        scratch=(
            pltpu.VMEM(queries.shape[1:], BF16),
            pltpu.VMEM((blocks.shape[2] * BLOCK, qk_width), BF16),
            pltpu.SemaphoreType.DMA((7,)),
        ),
    )
    arrived = swap(sent)
    other_t = swap(out_proj_t)
    w_down_other = swap(w_down)
    fanned = call(
        values_kernel,
        shape((n_req, half_heads + 1, drafts, DV), BF16),
        kept,
        kept_stats,
        arrived,
        value_half,
        residual,
        expert_ids,
    )
    gathered = lax.all_to_all(fanned, "req", split_axis=0, concat_axis=0, tiled=True)
    arrived = swap(
        call(
            project_other_kernel,
            shape((tokens + n_req * own_rows, padded), BF16),
            gathered,
            other_t,
            w_down_other,
        )
    )
    started = call(project_own_kernel, shape((tokens, width), F32), gathered, out_proj_t)
    terms, resid = call(
        project_sum_kernel,
        (
            shape((n_exp, tokens // n_exp, padded), BF16),
            shape((tokens // n_exp, padded), BF16),
        ),
        started,
        arrived,
        gathered,
    )
    terms = lax.all_to_all(terms, "exp", split_axis=0, concat_axis=0, tiled=True)
    fanned = call(
        hidden_kernel,
        shape((n_req * n_exp, tokens // n_exp // PACK, width * PACK), BF16),
        terms,
        resid,
    )
    own = lax.all_to_all(fanned, ("req", "exp"), split_axis=0, concat_axis=0, tiled=True)
    own = own.reshape(n_req, n_exp, tokens // n_exp // PACK, width * PACK)
    other = swap(own)
    started = call(
        gate_up_own_kernel,
        (
            shape((tokens, hidden_units), F32),
            shape((tokens, hidden_units), F32),
            shape((tokens, experts), F32),
            shape((tokens, 128), F32),
        ),
        own,
        gains,
        w_gate,
        w_up,
        router_t,
    )
    act_mine, act_theirs, rows_here = call(
        gate_up_both_kernel,
        (
            shape((tokens // 2, hidden_units), BF16),
            shape((tokens // 2, hidden_units), BF16),
            shape((n_req * 2, own_rows, width), F32),
        ),
        *started,
        own,
        other,
        terms,
        gains,
        w_gate,
        w_up,
        router_t,
    )
    pieces = call(
        down_kernel,
        shape((n_req * n_exp, own_rows * CHUNKS, model_width // CHUNKS), BF16),
        act_mine,
        swap(act_theirs),
        w_down,
        w_down_other,
        scratch=(pltpu.VMEM((model_width // CHUNKS // 128, n_req * n_exp * own_rows * CHUNKS, 128), F32),),
    )
    pieces = lax.all_to_all(pieces, ("exp", "req"), split_axis=0, concat_axis=0, tiled=True)
    return call(finish_kernel, shape((own_rows, model_width), BF16), pieces, rows_here)


def solution(mesh):
    in_specs = (
        P(("req", "seq", "exp"), None),
        P("req", None, "exp", None),
        P("req", "seq", None),
        P("req", "seq", None),
        P("req"),
        P("exp", None, None),
        P("exp", ("req", "seq")),
        P(),
        P(),
        P(("req", "seq", "exp"), None),
        P("req", None, ("seq", "exp")),
        P("req", None, ("seq", "exp")),
        P("req", ("seq", "exp"), None),
    )
    out_specs = P(("req", "seq", "exp"), None)

    return jax.shard_map(per_device, mesh=mesh, in_specs=in_specs, out_specs=out_specs, check_vma=False)
```

```python
import jax
import jax.numpy as jnp
from jax import lax
from jax.experimental import pallas as pl
from jax.experimental.pallas import tpu as pltpu
from jax.sharding import PartitionSpec as P


DL = 512
DR = 64
DV = 128
BLOCK = 64
F32 = jnp.float32
BF16 = jnp.bfloat16
SWAP = [(0, 1), (1, 0)]
PACK = 4


def swap(x):
    return lax.ppermute(x, "seq", SWAP)


def vmem():
    return pl.BlockSpec(memory_space=pltpu.VMEM)


def call(kernel, out_shape, *operands, scalars=(), outside=(), scratch=(), limit=24):
    many = isinstance(out_shape, (tuple, list))
    return pl.pallas_call(
        kernel,
        out_shape=out_shape,
        in_specs=[pl.BlockSpec(memory_space=pltpu.SMEM) for _ in scalars]
        + [pl.BlockSpec(memory_space=pltpu.HBM) for _ in outside]
        + [vmem() for _ in operands],
        out_specs=[vmem() for _ in out_shape] if many else vmem(),
        scratch_shapes=list(scratch),
        compiler_params=pltpu.CompilerParams(vmem_limit_bytes=limit * 2**20),
    )(*scalars, *[pltpu.with_memory_space_constraint(a, pltpu.HBM) for a in outside], *operands)


def one_hot(shape, source):
    rows = lax.broadcasted_iota(jnp.int32, shape, 0)
    columns = lax.broadcasted_iota(jnp.int32, shape, 1)
    return jnp.where(source(rows) == columns, 1.0, 0.0).astype(BF16)


def parts_of(a):
    first = a.astype(BF16)
    rest = a - first.astype(F32)
    second = rest.astype(BF16)
    return first, second, (rest - second.astype(F32)).astype(BF16)


def attend_kernel(
    lengths, blocks, queries, cache, value_up, sent, kept, kept_stats, value_half, query_rows, key_rows, sems
):
    drafts, heads, width = queries.shape
    side = lax.axis_index("seq")
    length, first, second = lengths[0], blocks[0], blocks[1]
    shard_len = cache.shape[0]
    copies = [
        pltpu.make_async_copy(
            cache.at[pl.ds(pl.multiple_of(first * BLOCK, BLOCK), BLOCK), :],
            key_rows.at[pl.ds(0, BLOCK), :],
            sems.at[0],
        ),
        pltpu.make_async_copy(
            cache.at[pl.ds(pl.multiple_of(second * BLOCK, BLOCK), BLOCK), :],
            key_rows.at[pl.ds(BLOCK, BLOCK), :],
            sems.at[1],
        ),
        pltpu.make_async_copy(queries, query_rows, sems.at[2]),
    ]
    quarter = heads // 8
    value_copies = [
        pltpu.make_async_copy(
            value_up.at[pl.ds(side * (heads // 2) + i * quarter, quarter)],
            value_half.at[pl.ds(i * quarter, quarter)],
            sems.at[3 + i],
        )
        for i in range(4)
    ]
    for place, copy in enumerate(copies):
        copy.start(priority=place // 2)
    for place, copy in enumerate(value_copies):
        copy.start(priority=place % 2)
    for copy in copies:
        copy.wait()
    keys = key_rows[...]
    rows = query_rows[...].reshape(drafts * heads, width)
    scores = lax.dot_general(
        rows, keys, (((1,), (1,)), ((), ())), preferred_element_type=F32
    ) * ((DV + DR) ** (-0.5))
    row = lax.broadcasted_iota(jnp.int32, scores.shape, 0)
    col = lax.broadcasted_iota(jnp.int32, scores.shape, 1)
    block = jnp.where(col < BLOCK, first, second - 1)
    usable = side * shard_len + block * BLOCK + col < length - (drafts - 1) + row // heads
    top = jnp.max(jnp.where(usable, scores, -1e30), -1, keepdims=True)
    probs = jnp.where(usable, jnp.exp(scores - top), 0.0).astype(BF16)
    total = jnp.sum(probs.astype(F32), -1, keepdims=True)
    out = jnp.dot(probs, keys[:, :DL], preferred_element_type=F32)
    half = heads // 2

    def split(a):
        a = a.reshape(drafts, 2, half, a.shape[-1])
        low = a[:, 0].reshape(drafts * half, a.shape[-1])
        high = a[:, 1].reshape(drafts * half, a.shape[-1])
        return jnp.where(side == 0, low, high), jnp.where(side == 0, high, low)

    mine, theirs = split(out)
    stats = jnp.concatenate(
        [jnp.broadcast_to(top, (top.shape[0], 128)), jnp.broadcast_to(total, (top.shape[0], 128))],
        -1,
    )
    my_stats, their_stats = split(stats)
    kept[...] = mine
    kept_stats[...] = my_stats
    sent[:, :DL] = theirs.astype(BF16)
    top_parts, sum_parts = parts_of(their_stats[:, :128]), parts_of(their_stats[:, 128:])
    lane = lax.broadcasted_iota(jnp.int32, (drafts * half, 128), 1)
    packed = jnp.zeros((drafts * half, 128), F32)
    for place, part in enumerate(top_parts + sum_parts):
        packed = jnp.where(lane == place, part.astype(F32), packed)
    sent[:, DL:] = packed.astype(BF16)
    for copy in value_copies:
        copy.wait()


def values_kernel(kept, kept_stats, arrived, value_up, residual, expert_ids, fanned):
    rows = kept.shape[0]
    dests, slabs, drafts, _ = fanned.shape
    half = slabs - 1
    packed = arrived[:, DL:].astype(F32)
    lane = lax.broadcasted_iota(jnp.int32, packed.shape, 1)
    other_top = jnp.sum(jnp.where(lane < 3, packed, 0.0), -1, keepdims=True)
    other_sum = jnp.sum(jnp.where((lane >= 3) & (lane < 6), packed, 0.0), -1, keepdims=True)
    my_top, my_sum = kept_stats[:, 0:1], kept_stats[:, 128:129]
    top = jnp.maximum(my_top, other_top)
    my_scale, other_scale = jnp.exp(my_top - top), jnp.exp(other_top - top)
    total = my_scale * my_sum + other_scale * other_sum
    latent = (my_scale / total) * kept[...] + (other_scale / total) * arrived[:, :DL].astype(F32)
    latent = latent.astype(BF16)
    order = one_hot((rows, rows), lambda i: i % drafts * half + i // drafts)
    latent = jnp.dot(order, latent, preferred_element_type=F32).astype(BF16)
    for head in range(half):
        out = jnp.dot(
            latent[head * drafts : (head + 1) * drafts],
            value_up[head],
            preferred_element_type=F32,
        ).astype(BF16)
        for dest in range(dests):
            fanned[dest, head] = out
    own_rows, model_width = residual.shape
    width = model_width // (2 * dests)
    lane = lax.broadcasted_iota(jnp.int32, (own_rows, 128), 1)
    named = jnp.zeros((own_rows, 128), F32)
    for k in range(expert_ids.shape[1]):
        named += jnp.where(expert_ids[:, k : k + 1] + (width - 128) == lane, 1.0, 0.0)
    values = residual[...].astype(F32)
    values = jnp.concatenate([values, jnp.zeros((own_rows, 128), F32)], -1)
    for dest in range(dests):
        pieces = []
        for row in range(own_rows):
            for core in range(2):
                start = (dest * 2 + core) * width
                pieces.append(values[row : row + 1, start : start + 128])
                tail = values[row : row + 1, start + 128 : start + 256]
                pieces.append(jnp.where(lane[:1] < width - 128, tail, named[row : row + 1]))
        pieces.append(jnp.zeros((drafts - len(pieces), 128), F32))
        fanned[dest, half] = jnp.concatenate(pieces, 0).astype(BF16)


def project_terms(gathered, out_proj_t, side):
    reqs, slabs, drafts, lanes = gathered.shape
    half = slabs - 1
    total = None
    for head in range(0, half, 2):
        pair = jnp.concatenate(
            [gathered[:, head].reshape(reqs * drafts, lanes), gathered[:, head + 1].reshape(reqs * drafts, lanes)],
            -1,
        )
        start = pl.multiple_of((side * half + head) * lanes, 256)
        term = lax.dot_general(
            pair,
            out_proj_t[:, pl.ds(start, 2 * lanes)],
            (((1,), (1,)), ((), ())),
            preferred_element_type=F32,
        )
        total = term if total is None else total + term
    return total


def residual_rows(gathered, column_side, tiles):
    reqs, slabs, drafts, lanes = gathered.shape
    beside = gathered[:, slabs - 1].reshape(reqs * drafts, lanes)
    picked = []
    for tile in range(tiles):

        def source(i):
            return i // 2 * drafts + (i % 2 * 2 + column_side) * tiles + tile

        order = one_hot((reqs * 2, reqs * drafts), source)
        picked.append(jnp.dot(order, beside, preferred_element_type=F32))
    return jnp.concatenate(picked, -1).astype(BF16)


def project_other_kernel(gathered, other_t, swapped, out):
    tokens = gathered.shape[0] * gathered.shape[2]
    side = lax.axis_index("seq")
    width, padded = other_t.shape[0], out.shape[1]
    total = project_terms(gathered, other_t, side)
    total = jnp.concatenate([total, jnp.zeros((tokens, padded - width), F32)], -1)
    out[:tokens] = total.astype(BF16)
    out[tokens:] = residual_rows(gathered, 1 - side, padded // gathered.shape[3])


def project_own_kernel(gathered, out_proj_t, out):
    out[...] = project_terms(gathered, out_proj_t, lax.axis_index("seq"))


def project_sum_kernel(started, arrived, gathered, terms, residual):
    reqs, _, drafts, lanes = gathered.shape
    exps, _, padded = terms.shape
    width = started.shape[1]
    side = lax.axis_index("seq")
    tokens = reqs * drafts
    own_rows = drafts // (2 * exps)
    total = (started[...] + arrived[:tokens, :width].astype(F32)).astype(BF16)

    def source(i):
        exp, req = i // (tokens // exps), i // (2 * own_rows) % reqs
        seq, row = i // own_rows % 2, i % own_rows
        return ((req * 2 + seq) * exps + exp) * own_rows + row

    total = jnp.dot(one_hot((tokens, tokens), source), total, preferred_element_type=F32)
    total = jnp.concatenate([total, jnp.zeros((tokens, padded - width), F32)], -1)
    picked = jnp.zeros(residual.shape, F32)
    for rows, from_side in (
        (residual_rows(gathered, side, padded // lanes), side),
        (arrived[tokens:], 1 - side),
    ):

        def residual_source(i):
            req, seq, row = i // (2 * own_rows), i // own_rows % 2, i % own_rows
            return jnp.where(seq == from_side, req * own_rows + row, -1)

        order = one_hot((residual.shape[0], rows.shape[0]), residual_source)
        picked += jnp.dot(order, rows, preferred_element_type=F32)
    residual[...] = picked.astype(BF16)
    lane = lax.broadcasted_iota(jnp.int32, residual.shape, 1)
    named = jnp.where(lane < width, 0.0, picked)
    for dest in range(exps):
        rows = total[dest * residual.shape[0] : (dest + 1) * residual.shape[0]]
        terms[dest] = (rows + named).astype(BF16)


def hidden_kernel(terms, residual, fanned):
    attended = jnp.sum(terms[...].astype(F32), 0).astype(BF16)
    hidden = residual[...].astype(F32) + attended.astype(F32)
    rows, width = fanned.shape[1], fanned.shape[2] // PACK
    packed = jnp.concatenate(
        [hidden[i * rows : (i + 1) * rows, :width] for i in range(PACK)], -1
    ).astype(BF16)
    for dest in range(fanned.shape[0]):
        fanned[dest] = packed


def unpacked(rows, i, width):
    exps = rows.shape[1]
    pieces = []
    for exp in range(exps):
        tile = rows[i, exp].astype(F32)
        pieces += [tile[:, j * width : (j + 1) * width] for j in range(PACK)]
    return jnp.concatenate(pieces, 0)


def expert_terms(rows, gains, w_gate, w_up, router_t, side):
    steps, exps, packed_rows, _ = rows.shape
    tokens = exps * packed_rows * PACK
    width = gains.shape[1] // (2 * steps)
    gate = jnp.zeros((tokens, w_gate.shape[1]), F32)
    up = jnp.zeros((tokens, w_up.shape[1]), F32)
    logits = jnp.zeros((tokens, router_t.shape[0]), F32)
    squares = jnp.zeros((tokens, width), F32)

    def columns_of(a, i):
        low = a[:, i * 2 * width : (i * 2 + 1) * width].astype(F32)
        high = a[:, (i * 2 + 1) * width : (i * 2 + 2) * width].astype(F32)
        return jnp.where(side == 0, low, high)

    for i in range(steps):
        start = pl.multiple_of((i * 2 + side) * width, 32)
        hidden = unpacked(rows, i, width)
        scaled = (hidden * columns_of(gains, i)).astype(BF16)
        gate += jnp.dot(scaled, w_gate[pl.ds(start, width), :], preferred_element_type=F32)
        up += jnp.dot(scaled, w_up[pl.ds(start, width), :], preferred_element_type=F32)
        logits += lax.dot_general(
            scaled,
            columns_of(router_t, i).astype(BF16),
            (((1,), (1,)), ((), ())),
            preferred_element_type=F32,
        )
        squares += hidden * hidden
    return gate, up, logits, jnp.sum(squares, -1, keepdims=True)


def gate_up_own_kernel(own, gains, w_gate, w_up, router_t, gate, up, logits, squares):
    a, b, c, d = expert_terms(own, gains, w_gate, w_up, router_t, lax.axis_index("seq"))
    gate[...], up[...], logits[...] = a, b, c
    squares[...] = jnp.broadcast_to(d, squares.shape)


def gate_up_both_kernel(
    gate, up, logits, squares, own, other, terms, gains, w_gate, w_up, router_t,
    act_mine, act_theirs, rows_here, lines,
):
    side = lax.axis_index("seq")
    own_rows = rows_here.shape[0] // (2 * own.shape[0])
    exp, req = lax.axis_index("exp"), lax.axis_index("req")
    packed_rows = own.shape[2]
    place = (req * 2 + side) * own_rows
    group, first = place // packed_rows, place % packed_rows
    part = rows_here.shape[1]
    near = lax.broadcasted_iota(jnp.int32, own.shape[2:], 0)
    for rows, from_side in ((own, side), (other, 1 - side)):
        for i in range(own.shape[0]):
            tile = rows[i, exp].astype(F32)
            for row in range(own_rows):
                line = jnp.sum(jnp.where(near == first + row, tile, 0.0), 0, keepdims=True)
                lines[pl.ds((i * 2 + from_side) * own_rows + row, 1), :] = line
    picked = lines[:, :part]
    for j in range(1, PACK):
        picked = jnp.where(group == j, lines[:, j * part : (j + 1) * part], picked)
    rows_here[...] = picked
    width = gains.shape[1] // (2 * own.shape[0])
    experts = logits.shape[1]
    columns = gains.shape[1]
    a, b, c, d = expert_terms(other, gains, w_gate, w_up, router_t, 1 - side)
    scale = lax.rsqrt((squares[:, 0:1] + d) / columns + 1e-06)
    tokens = gate.shape[0]
    named = terms[...].reshape(tokens, terms.shape[2])[:, width : width + experts].astype(F32)
    chosen = named * jax.nn.sigmoid((logits[...] + c) * scale)
    mine = lax.broadcasted_iota(jnp.int32, chosen.shape, 1) == lax.axis_index("req")
    weight = jnp.sum(jnp.where(mine, chosen, 0.0), -1, keepdims=True)
    weight = weight / jnp.sum(chosen, -1, keepdims=True) * 2.5
    act = (jax.nn.silu((gate[...] + a) * scale) * ((up[...] + b) * scale) * weight).astype(BF16)
    tokens = act.shape[0]
    for out, seq in ((act_mine, side), (act_theirs, 1 - side)):

        def source(i):
            row, group = i // (tokens // (2 * own_rows)), i % (tokens // (2 * own_rows))
            return (group * 2 + seq) * own_rows + row

        order = one_hot((tokens // 2, tokens), source)
        out[...] = jnp.dot(order, act, preferred_element_type=F32).astype(BF16)


CHUNKS = 8


def down_kernel(act, act_other, w_down, w_down_other, out, rows_here):
    groups, rows, block = out.shape
    own_rows = rows // CHUNKS
    for chunk in range(CHUNKS):
        columns = slice(chunk * block, (chunk + 1) * block)
        total = jnp.dot(act[...], w_down[:, columns], preferred_element_type=F32)
        total += jnp.dot(act_other[...], w_down_other[:, columns], preferred_element_type=F32)
        for row in range(own_rows):
            for tile in range(block // 128):
                rows_here[tile, pl.ds(chunk * own_rows + row, groups, stride=rows), :] = total[
                    row * groups : (row + 1) * groups, tile * 128 : (tile + 1) * 128
                ]
    for tile in range(block // 128):
        out[:, :, tile * 128 : (tile + 1) * 128] = (
            rows_here[tile].reshape(groups, rows, 128).astype(BF16)
        )


def finish_kernel(pieces, hidden_rows, out):
    rows = out.shape[0]
    blocks = hidden_rows.shape[0] // rows
    total = jnp.sum(pieces[...].astype(F32), 0)
    total = jnp.concatenate([total[i * rows : (i + 1) * rows] for i in range(CHUNKS)], -1)
    hidden = jnp.concatenate([hidden_rows[block * rows : (block + 1) * rows] for block in range(blocks)], -1)
    out[...] = (hidden + total).astype(BF16)


def per_device(
    residual,
    queries,
    latent_cache,
    blocks,
    lengths,
    value_up,
    out_proj,
    norm_gain,
    router,
    expert_ids,
    w_gate,
    w_up,
    w_down,
):
    drafts, heads, qk_width = queries.shape[1:]
    n_req, n_exp = lax.axis_size("req"), lax.axis_size("exp")
    model_width = residual.shape[1]
    experts = router.shape[1]
    width = out_proj.shape[1]
    padded = -(-width // 128) * 128
    own_rows = residual.shape[0]
    tokens = n_req * drafts
    half_heads = heads // 2
    half_rows = drafts * half_heads
    shape = jax.ShapeDtypeStruct
    w_gate, w_up, w_down = w_gate[0], w_up[0], w_down[0]
    hidden_units = w_gate.shape[1]
    gains, router_t, out_proj_t = norm_gain.reshape(1, model_width), router.T, out_proj.T

    sent, kept, kept_stats, value_half = call(
        attend_kernel,
        (
            shape((half_rows, DL + 128), BF16),
            shape((half_rows, DL), F32),
            shape((half_rows, 256), F32),
            shape((half_heads,) + value_up.shape[1:], BF16),
        ),
        scalars=(lengths, blocks.reshape(-1)),
        outside=(queries[0], latent_cache[0], value_up),
        scratch=(
            pltpu.VMEM(queries.shape[1:], BF16),
            pltpu.VMEM((blocks.shape[2] * BLOCK, qk_width), BF16),
            pltpu.SemaphoreType.DMA((7,)),
        ),
    )
    arrived = swap(sent)
    other_t = swap(out_proj_t)
    w_down_other = swap(w_down)
    fanned = call(
        values_kernel,
        shape((n_req, half_heads + 1, drafts, DV), BF16),
        kept,
        kept_stats,
        arrived,
        value_half,
        residual,
        expert_ids,
    )
    gathered = lax.all_to_all(fanned, "req", split_axis=0, concat_axis=0, tiled=True)
    arrived = swap(
        call(
            project_other_kernel,
            shape((tokens + n_req * own_rows, padded), BF16),
            gathered,
            other_t,
            w_down_other,
        )
    )
    started = call(project_own_kernel, shape((tokens, width), F32), gathered, out_proj_t)
    terms, resid = call(
        project_sum_kernel,
        (
            shape((n_exp, tokens // n_exp, padded), BF16),
            shape((tokens // n_exp, padded), BF16),
        ),
        started,
        arrived,
        gathered,
    )
    terms = lax.all_to_all(terms, "exp", split_axis=0, concat_axis=0, tiled=True)
    fanned = call(
        hidden_kernel,
        shape((n_req * n_exp, tokens // n_exp // PACK, width * PACK), BF16),
        terms,
        resid,
    )
    own = lax.all_to_all(fanned, ("req", "exp"), split_axis=0, concat_axis=0, tiled=True)
    own = own.reshape(n_req, n_exp, tokens // n_exp // PACK, width * PACK)
    other = swap(own)
    started = call(
        gate_up_own_kernel,
        (
            shape((tokens, hidden_units), F32),
            shape((tokens, hidden_units), F32),
            shape((tokens, experts), F32),
            shape((tokens, 128), F32),
        ),
        own,
        gains,
        w_gate,
        w_up,
        router_t,
    )
    act_mine, act_theirs, rows_here = call(
        gate_up_both_kernel,
        (
            shape((tokens // 2, hidden_units), BF16),
            shape((tokens // 2, hidden_units), BF16),
            shape((n_req * 2 * own_rows, width), F32),
        ),
        *started,
        own,
        other,
        terms,
        gains,
        w_gate,
        w_up,
        router_t,
        scratch=(pltpu.VMEM((n_req * 2 * own_rows, width * PACK), F32),),
    )
    pieces = call(
        down_kernel,
        shape((n_req * n_exp, own_rows * CHUNKS, model_width // CHUNKS), BF16),
        act_mine,
        swap(act_theirs),
        w_down,
        w_down_other,
        scratch=(pltpu.VMEM((model_width // CHUNKS // 128, n_req * n_exp * own_rows * CHUNKS, 128), F32),),
    )
    pieces = lax.all_to_all(pieces, ("exp", "req"), split_axis=0, concat_axis=0, tiled=True)
    return call(finish_kernel, shape((own_rows, model_width), BF16), pieces, rows_here)


def solution(mesh):
    in_specs = (
        P(("req", "seq", "exp"), None),
        P("req", None, "exp", None),
        P("req", "seq", None),
        P("req", "seq", None),
        P("req"),
        P("exp", None, None),
        P("exp", ("req", "seq")),
        P(),
        P(),
        P(("req", "seq", "exp"), None),
        P("req", None, ("seq", "exp")),
        P("req", None, ("seq", "exp")),
        P("req", ("seq", "exp"), None),
    )
    out_specs = P(("req", "seq", "exp"), None)

    return jax.shard_map(per_device, mesh=mesh, in_specs=in_specs, out_specs=out_specs, check_vma=False)
```
